32 devices in a mesh: fluid: 8 (over z, core), struct: 4 (over y, x).
Axes of the slice: x: 2, y: 2, z: 4, core: 2. Of those that a mesh axis runs over, the one named last changes fastest.
Arguments:
- fluid_adjoint: float32 [5, 16384], P(None, ('fluid', 'struct')), may hold values from -6 to 6
- fluid_rhs: float32 [5, 16384], P(None, ('fluid', 'struct')), may hold values from -6 to 6
- diag_inverse: float32 [5, 5, 16384], P(None, None, ('fluid', 'struct'))
- face_blocks: float32 [6, 5, 5, 16384], P(None, None, None, ('fluid', 'struct')), may hold values from -0.625 to 0.625
- face_index: int32 [6, 16384], P(None, ('fluid', 'struct')), may hold values from 0 to 1023, as said below
- surface_cell: int32 [8192], P(('fluid', 'struct')), may hold values from 0 to 511, as said below
- surface_count: int32 [32], P(('fluid', 'struct')), may hold values from 32 to 256, as said below
- transfer_node: int32 [3, 8192], P(None, ('fluid', 'struct')), may hold values from 0 to 2047
- transfer_weight: float32 [3, 8192], P(None, ('fluid', 'struct')), may hold values from 0.2 to 1
- load_sens: float32 [3, 5, 8192], P(None, None, ('fluid', 'struct')), may hold values from -4 to 4
- disp_sens: float32 [5, 3, 8192], P(None, None, ('fluid', 'struct')), may hold values from -2.4 to 2.4
- struct_adjoint: float32 [12288], P('struct'), may hold values from -6 to 6
- struct_rhs: float32 [12288], P('struct'), may hold values from -6 to 6
- shell_blocks: float32 [4, 128, 9216], P(None, 'struct'), may hold values from -0.15625 to 0.15625
- shell_inverse: float32 [128, 9216], P('struct')
- shell_columns: int32 [4, 128], P(None, 'struct'), may hold values from 0 to 127
Outputs:
- fluid_out: float32 [5, 16384], P(None, ('fluid', 'struct'))
- struct_out: float32 [12288], P('struct')
The draws below stay inside these ranges and needn't reach their ends.
Inputs may be any that keep to these rules, and one draw needn't show every extreme that they name: `face_index`: neighbour positions lie within 256 cells of the cell's own position in the extended block; the two ends of the range are taken. `surface_cell`: distinct within each block of 256 slots; every block holds the first and the last cell of the block. `surface_count`: some block has all its slots live and some has 32.
All inputs are finite; a program needn't handle non-finite values.
Results may differ from the reference program's by a relative error of at most 0.00021.
Values sent between devices are 32-bit elements; how exact they have to be, the bound alone decides.
A program may use at most 64 MiB of HBM per device.

```python
import math
import jax
import jax.numpy as jnp
from jax import lax

NVAR = 5
FACES = 6
CELL_DEV = 512
HALO = 256
BLOCKS = 32
CELLS = 16384
SURF_DEV = 256
SURFS = 8192
TMAP = 3
DOF = 6
BLK = 96
NSB = 128
NODES = 2048
NB = 4
SWEEPS = 6
ITERS = 2


def draw_diag_inverse(key, part):
    first, second = jax.random.split(key)
    rows = jnp.arange(NVAR, dtype=jnp.int32)
    identity = (rows[:, None] == rows[None, :]).astype(jnp.float32)[:, :, None]
    scale = jnp.exp(jax.random.uniform(first, (1, 1, CELLS), jnp.float32, math.log(0.5), math.log(2.0)))
    spread = 0.25 * jax.random.normal(second, (NVAR, NVAR, CELLS), jnp.float32)
    return identity * scale + (1.0 - identity) * spread * scale


def draw_shell_inverse(key, part):
    first, second = jax.random.split(key)
    flat = jnp.arange(BLK * BLK, dtype=jnp.int32)
    identity = (flat // BLK == flat % BLK).astype(jnp.float32)[None, :]
    scale = jnp.exp(jax.random.uniform(first, (NSB, BLK * BLK), jnp.float32, math.log(0.5), math.log(2.0)))
    spread = 0.3 * BLK ** (-0.5) * jax.random.normal(second, (NSB, BLK * BLK), jnp.float32)
    return identity * scale + (1.0 - identity) * spread


def draw_face_index(key, part):
    position = jnp.arange(CELLS, dtype=jnp.int32) % CELL_DEV
    offsets = jax.random.randint(key, (FACES, CELLS), -HALO, HALO + 1, jnp.int32)
    faces = jnp.arange(FACES, dtype=jnp.int32)[:, None]
    offsets = jnp.where(faces == 0, -1, offsets)
    offsets = jnp.where(faces == 1, 1, offsets)
    offsets = jnp.where((faces == 2) & (position[None, :] == 0), -HALO, offsets)
    offsets = jnp.where((faces == FACES - 1) & (position[None, :] == CELL_DEV - 1), HALO, offsets)
    return (position[None, :] + HALO + offsets).astype(jnp.int32)


def pick_cells(single):
    first, second = jax.random.split(single)
    inner = jax.random.permutation(first, CELL_DEV - 2)[:SURF_DEV - 2].astype(jnp.int32) + 1
    ends = jnp.array([0, CELL_DEV - 1], jnp.int32)
    gathered = jnp.concatenate([ends, inner]).astype(jnp.int32)
    order = jax.random.permutation(second, SURF_DEV)
    return gathered[order]


def draw_surface_cell(key, part):
    keys = jax.random.split(key, BLOCKS)
    picked = jax.vmap(pick_cells)(keys)
    return picked.reshape(-1).astype(jnp.int32)


def draw_surface_count(key, part):
    first, second = jax.random.split(key)
    levels = SURF_DEV // jnp.array([1, 2, 4, 8], jnp.int32)
    counts = levels[jax.random.randint(first, (BLOCKS,), 0, 4, jnp.int32)]
    fullest = jax.random.randint(second, (), 0, BLOCKS, jnp.int32)
    blocks = jnp.arange(BLOCKS, dtype=jnp.int32)
    counts = jnp.where(blocks == fullest, SURF_DEV, counts)
    counts = jnp.where(blocks == (fullest + 1) % BLOCKS, SURF_DEV // 8, counts)
    return counts.astype(jnp.int32)


def set_ends(entries, stream_key, low, high):
    place = [jax.random.randint(jax.random.fold_in(stream_key, axis), (), 0, length) for axis, length in enumerate(entries.shape)]
    main_axis = entries.shape.index(max(entries.shape))
    beside = place[:main_axis] + [(place[main_axis] + 1) % entries.shape[main_axis]] + place[main_axis + 1:]
    return entries.at[tuple(place)].set(low).at[tuple(beside)].set(high)


def block_levels(key, shape, shards, smallest, high):
    gain = 1.0
    for dim, shards_of in shards:
        draws = jax.random.uniform(jax.random.fold_in(jax.random.fold_in(key, 6), dim), (shards_of,), jnp.float32, smallest / len(shards), high / len(shards))
        gain = gain * jnp.repeat(jnp.exp(draws), shape[dim] // shards_of).reshape((-1,) + (1,) * (len(shape) - 1 - dim))
    return gain


def noise(rng, shape, scale, reach, cuts=(), held_as=jnp.bfloat16):
    level = block_levels(rng, shape, cuts, -0.22, 0.18) if cuts else 1.0
    values = jax.random.normal(rng, shape, jnp.float32) * scale * level
    return jnp.minimum(jnp.maximum(values, -reach), reach).astype(held_as)


def setup_inputs(seed: int = 0) -> dict:
    key_of = jax.random.split(jax.random.key(seed), 17)
    return {
        "fluid_adjoint": noise(key_of[0], (NVAR, CELLS), 1.0, 6.0, ((1, 32),), jnp.float32),
        "fluid_rhs": noise(key_of[1], (NVAR, CELLS), 1.0, 6.0, ((1, 32),), jnp.float32),
        "diag_inverse": draw_diag_inverse(jax.random.fold_in(key_of[16], 71), 0),
        "face_blocks": noise(key_of[3], (FACES, NVAR, NVAR, CELLS), 100 ** -0.5, 0.625, ((3, 32),), jnp.float32),
        "face_index": draw_face_index(jax.random.fold_in(key_of[16], 71), 0),
        "surface_cell": draw_surface_cell(jax.random.fold_in(key_of[16], 71), 0),
        "surface_count": draw_surface_count(jax.random.fold_in(key_of[16], 71), 0),
        "transfer_node": set_ends(jax.random.randint(key_of[7], (TMAP, SURFS), 0, NODES), jax.random.fold_in(key_of[7], 1), 0, NODES - 1).astype(jnp.int32),
        "transfer_weight": jnp.clip(0.2 + 0.8 * jax.random.uniform(key_of[8], (TMAP, SURFS), jnp.float32) ** block_levels(key_of[8], (TMAP, SURFS), ((1, 32),), -0.2, 0.2), 0.2, 1.0),
        "load_sens": noise(key_of[9], (3, NVAR, SURFS), 0.5, 4.0, ((2, 32),), jnp.float32),
        "disp_sens": noise(key_of[10], (NVAR, 3, SURFS), 0.3, 2.4, ((2, 32),), jnp.float32),
        "struct_adjoint": noise(key_of[11], (NSB * BLK,), 1.0, 6.0, ((0, 4),), jnp.float32),
        "struct_rhs": noise(key_of[12], (NSB * BLK,), 1.0, 6.0, ((0, 4),), jnp.float32),
        "shell_blocks": noise(key_of[13], (NB, NSB, BLK * BLK), (4 * NB * BLK) ** -0.5, 0.15625, ((1, 4),), jnp.float32),
        "shell_inverse": draw_shell_inverse(jax.random.fold_in(key_of[16], 71), 0),
        "shell_columns": set_ends(jax.random.randint(key_of[15], (NB, NSB), 0, NSB), jax.random.fold_in(key_of[15], 1), 0, NSB - 1).astype(jnp.int32),
    }


def reference(fluid_adjoint, fluid_rhs, diag_inverse, face_blocks, face_index, surface_cell, surface_count, transfer_node, transfer_weight, load_sens, disp_sens, struct_adjoint, struct_rhs, shell_blocks, shell_inverse, shell_columns):
    highest = lax.Precision.HIGHEST
    cell_total = fluid_adjoint.shape[1]
    block_of_cell = (jnp.arange(cell_total, dtype=jnp.int32) // CELL_DEV).astype(jnp.int32)
    padded_index = (face_index + (block_of_cell * CELL_DEV)[None, :]).astype(jnp.int32)
    surf_total = surface_cell.shape[0]
    slot_ids = jnp.arange(surf_total, dtype=jnp.int32)
    surf_block = (slot_ids // SURF_DEV).astype(jnp.int32)
    global_cell = (surface_cell + surf_block * CELL_DEV).astype(jnp.int32)
    live_slot = (slot_ids % SURF_DEV < surface_count[surf_block]).astype(jnp.float32)
    component = jnp.arange(3, dtype=jnp.int32)
    dof_index = (transfer_node[:, None, :] * DOF + component[None, :, None]).astype(jnp.int32)
    fluid_state = fluid_adjoint
    struct_state = struct_adjoint
    for iteration in range(ITERS):
        displaced = jnp.sum(transfer_weight[:, None, :] * struct_state[dof_index], axis=0)
        load_adj = live_slot[None, :] * jnp.einsum("jvs,js->vs", load_sens, displaced, precision=highest)
        coupling = jnp.zeros_like(fluid_state).at[:, global_cell].add(load_adj)
        shell_rows = struct_state.reshape(NSB, BLK)[shell_columns]
        shell_terms = jnp.einsum("mbqp,mbq->bp", shell_blocks.reshape(NB, NSB, BLK, BLK), shell_rows, precision=highest)
        for sweep_step in range(SWEEPS):
            padded = jnp.pad(fluid_state, ((0, 0), (HALO, HALO)))
            beside = padded[:, padded_index]
            face_terms = jnp.einsum("kuvc,ukc->vc", face_blocks, beside, precision=highest)
            fluid_state = jnp.einsum("vuc,uc->vc", diag_inverse, fluid_rhs + coupling - face_terms, precision=highest)
        surface_sens = live_slot[None, :] * jnp.einsum("vjs,vs->js", disp_sens, fluid_state[:, global_cell], precision=highest)
        forces = jnp.zeros_like(struct_state).at[dof_index].add(transfer_weight[:, None, :] * surface_sens[None, :, :])
        struct_total = struct_rhs.reshape(NSB, BLK) + forces.reshape(NSB, BLK) - shell_terms
        struct_state = jnp.einsum("bpq,bq->bp", shell_inverse.reshape(NSB, BLK, BLK), struct_total, precision=highest).reshape(-1)
    return fluid_state, struct_state
```

```python
import functools

import jax
import jax.numpy as jnp
from jax import lax
from jax.experimental import pallas as pl
from jax.experimental.pallas import tpu as pltpu
from jax.sharding import PartitionSpec as P

NVAR = 5
FACES = 6
TMAP = 3
DOF = 6
BLK = 96
NB = 4
SWEEPS = 6
ITERS = 2
NPB = BLK // DOF
WIDE = (2, 4)
LANE = 128
ROWS = 8
FOLD = 384
CHUNK = 768
MESH = pl.DeviceIdType.MESH
NN = (((1,), (0,)), ((), ()))
NT = (((1,), (1,)), ((), ()))


def split(value):
    high = value.astype(jnp.bfloat16)
    return high, (value - high.astype(jnp.float32)).astype(jnp.bfloat16)


def dot(left, right, dims):
    return lax.dot_general(left, right, dims, preferred_element_type=jnp.float32)


def dot_left(value, table, dims):
    rows = value.shape[0]
    stacked = jnp.concatenate([p.astype(jnp.float32) for p in split(value)], axis=0)
    out = dot(stacked.astype(jnp.bfloat16), table, dims)
    return out[0:rows] + out[rows : 2 * rows]


def dot_right(table, value, dims):
    high, low = split(value)
    return dot(table, high, dims) + dot(table, low, dims)


def iota(shape, axis):
    return lax.broadcasted_iota(jnp.int32, shape, axis)


def pad_rows(value, rows=ROWS):
    return jnp.concatenate(
        [value, jnp.zeros((rows - value.shape[0], value.shape[1]), value.dtype)], axis=0
    )


def by_block(flat, out):
    groups = flat.shape[0] * LANE // FOLD
    wide = jnp.concatenate(
        [flat[pl.ds(a, groups, stride=FOLD // LANE)] for a in range(FOLD // LANE)], axis=1
    )
    for q in range(FOLD // BLK):
        part = wide[:, q * BLK : (q + 1) * BLK]
        full = jnp.concatenate([part, jnp.zeros((groups, LANE - BLK), jnp.float32)], axis=1)
        out[pl.ds(q, groups, stride=FOLD // BLK)] = full


def kernel(
    fluid_n,
    struct_n,
    piece,
    adj_ref,
    rhs_ref,
    diag_ref,
    face_ref,
    index_ref,
    cell_ref,
    count_ref,
    node_ref,
    weight_ref,
    load_ref,
    disp_ref,
    sadj_ref,
    srhs_ref,
    blocks_ref,
    inverse_ref,
    columns_ref,
    fluid_ref,
    struct_ref,
    state,
    low_halo,
    high_halo,
    folded,
    fold_low,
    fold_high,
    bias,
    bias_low,
    bias_high,
    index_all,
    index_low,
    index_high,
    diag_t,
    cell_table,
    block_table,
    node_mask,
    blocks,
    inverse,
    expand,
    start_struct,
    right_struct,
    struct_land,
    struct_all,
    rows_x,
    terms,
    forces_out,
    forces_land,
    result,
    final_land,
    halo_send,
    halo_recv,
    once_send,
    once_recv,
    start_send,
    start_recv,
    force_send,
    force_recv,
    gather_send,
    gather_recv,
    final_send,
    final_recv,
    local_sem,
):
    me_f = lax.axis_index("fluid")
    me_s = lax.axis_index("struct")
    me = me_f * struct_n + me_s
    total = fluid_n * struct_n
    cells = adj_ref.shape[1]
    half = cells // 2
    tiles = cells // LANE
    half_tiles = half // LANE
    slots = cell_ref.shape[1]
    shell_total = block_table.shape[0]
    shard_rows = start_struct.shape[0]
    my_row = me_f * piece
    base = (my_row // ROWS) * ROWS

    def dev(index):
        return (index // struct_n, index % struct_n)

    fold_low[...] = jnp.zeros_like(fold_low)
    fold_high[...] = jnp.zeros_like(fold_high)
    barrier = pltpu.get_barrier_semaphore()

    def greet(r, carry):
        pl.semaphore_signal(
            barrier, inc=1, device_id=dev((me + r) % total), device_id_type=MESH
        )
        return carry

    lax.fori_loop(1, total, greet, 0)

    local = []
    for m in range(NB):
        local.append(
            pltpu.make_async_copy(
                blocks_ref.at[m, pl.ds(pl.multiple_of(base, ROWS), ROWS)],
                blocks.at[m],
                local_sem.at[m],
            )
        )
    local.append(
        pltpu.make_async_copy(
            inverse_ref.at[pl.ds(pl.multiple_of(base, ROWS), ROWS)], inverse, local_sem.at[NB]
        )
    )
    for copy in local:
        copy.start()

    @pl.when(me == 0)
    def _():
        for ref in (low_halo, bias_low, index_low):
            ref[...] = jnp.zeros_like(ref)

    @pl.when(me == total - 1)
    def _():
        for ref in (high_halo, bias_high, index_high):
            ref[...] = jnp.zeros_like(ref)

    state[0] = pad_rows(adj_ref[...])
    index_all[...] = pad_rows(index_ref[...])
    forces_out[...] = jnp.zeros_like(forces_out)
    by_block(sadj_ref, start_struct)
    by_block(srhs_ref, right_struct)

    pl.semaphore_wait(barrier, total - 1)

    def start_copy(r):
        peer = (me_s + r) % struct_n
        return pltpu.make_async_remote_copy(
            src_ref=start_struct,
            dst_ref=struct_land.at[me_s],
            send_sem=start_send.at[r],
            recv_sem=start_recv.at[me_s],
            device_id=(me_f, peer),
            device_id_type=MESH,
        )

    for r in range(1, struct_n):
        start_copy(r).start()

    def to_low(source, landing, send, recv):
        return pltpu.make_async_remote_copy(
            src_ref=source,
            dst_ref=landing,
            send_sem=send,
            recv_sem=recv,
            device_id=dev(me - 1),
            device_id_type=MESH,
        )

    def to_high(source, landing, send, recv):
        return pltpu.make_async_remote_copy(
            src_ref=source,
            dst_ref=landing,
            send_sem=send,
            recv_sem=recv,
            device_id=dev(me + 1),
            device_id_type=MESH,
        )

    def swap_start(down, up):
        @pl.when(me > 0)
        def _():
            to_low(*down).start()

        @pl.when(me < total - 1)
        def _():
            to_high(*up).start()

    def swap_wait(down, up):
        @pl.when(me > 0)
        def _():
            to_low(*down).wait_send()
            to_high(*up).wait_recv()

        @pl.when(me < total - 1)
        def _():
            to_high(*up).wait_send()
            to_low(*down).wait_recv()

    def halo(t):
        return (
            (state.at[t], high_halo.at[t], halo_send.at[t, 0], halo_recv.at[t, 0]),
            (state.at[t], low_halo.at[t], halo_send.at[t, 1], halo_recv.at[t, 1]),
        )

    low_span, high_span = slice(0, half), slice(half, cells)

    def fold_swap():
        return (
            (folded.at[:, :, 0:NVAR, low_span], fold_high.at[:, :, 0:NVAR], once_send.at[0, 0], once_recv.at[0, 0]),
            (folded.at[:, :, 0:NVAR, high_span], fold_low.at[:, :, 0:NVAR], once_send.at[0, 1], once_recv.at[0, 1]),
        )

    def index_swap():
        return (
            (index_all.at[:, low_span], index_high, once_send.at[1, 0], once_recv.at[1, 0]),
            (index_all.at[:, high_span], index_low, once_send.at[1, 1], once_recv.at[1, 1]),
        )

    def bias_swap(i):
        n = 2 + i
        return (
            (bias.at[i, :, low_span], bias_high.at[i], once_send.at[n, 0], once_recv.at[n, 0]),
            (bias.at[i, :, high_span], bias_low.at[i], once_send.at[n, 1], once_recv.at[n, 1]),
        )

    swap_start(*halo(0))
    swap_start(*index_swap())

    for w in range(NVAR):
        for v in range(NVAR):
            diag_t[w, v : v + 1] = diag_ref[v, w : w + 1]
    for k in range(FACES):
        for u in range(NVAR):
            out = jnp.zeros((NVAR, cells), jnp.float32)
            for w in range(NVAR):
                out = out + diag_t[w, 0:NVAR] * face_ref[u, w, k : k + 1]
            folded[k, u] = pad_rows(out)
    swap_start(*fold_swap())

    live = (iota((1, slots), 1) < count_ref[...]).astype(jnp.float32)
    cell_table[...] = jnp.where(iota((cells, slots), 0) == cell_ref[...], 1.0, 0.0).astype(
        jnp.bfloat16
    )
    for t in range(TMAP):
        node = node_ref[t : t + 1]
        block_of = lax.shift_right_logical(node, NPB.bit_length() - 1)
        inside = node & (NPB - 1)
        block_table[:, t * slots : (t + 1) * slots] = jnp.where(
            iota((shell_total, slots), 0) == block_of, 1.0, 0.0
        ).astype(jnp.bfloat16)
        node_mask[:, t * slots : (t + 1) * slots] = jnp.where(
            iota((NPB, slots), 0) == inside, weight_ref[t : t + 1], 0.0
        )
    for c in range(0, BLK * BLK, CHUNK):
        offset = iota((LANE, CHUNK), 1) + c - BLK * iota((LANE, CHUNK), 0)
        expand[:, c : c + CHUNK] = jnp.where((offset >= 0) & (offset < BLK), 1.0, 0.0).astype(
            jnp.bfloat16
        )
    out_row = iota((3 * NPB, LANE), 0)
    perm = jnp.where(
        iota((3 * NPB, LANE), 1)
        == (out_row & (NPB - 1)) * DOF + lax.shift_right_logical(out_row, NPB.bit_length() - 1),
        1.0,
        0.0,
    ).astype(jnp.bfloat16)
    behind = iota((FOLD, LANE), 0) - iota((FOLD, LANE), 1)
    near = (behind == 0) | (behind == BLK) | (behind == 2 * BLK) | (behind == 3 * BLK)
    fold = jnp.where(near & (iota((FOLD, LANE), 1) < BLK), 1.0, 0.0).astype(jnp.bfloat16)

    struct_all[pl.ds(pl.multiple_of(me_s * shard_rows, shard_rows), shard_rows)] = start_struct[...]
    for r in range(1, struct_n):
        source = (me_s + r) % struct_n
        copy = pltpu.make_async_remote_copy(
            src_ref=start_struct,
            dst_ref=struct_land.at[source],
            send_sem=start_send.at[r],
            recv_sem=start_recv.at[source],
            device_id=(me_f, source),
            device_id_type=MESH,
        )
        copy.wait()
        struct_all[pl.ds(pl.multiple_of(source * shard_rows, shard_rows), shard_rows)] = (
            struct_land[source]
        )

    peers_f = [(me_f + r) % fluid_n for r in range(fluid_n)]
    peers_s = [(me_s + r) % struct_n for r in range(struct_n)]

    def all_copies(iteration, sources, dest, send, recv, mode):
        if mode == "start":
            for rf in reversed(range(fluid_n)):
                for rs in reversed(range(struct_n)):
                    if rf + rs == 0:
                        continue
                    peer_f, peer_s = peers_f[rf], peers_s[rs]
                    pltpu.make_async_remote_copy(
                        src_ref=sources(peer_s * fluid_n + peer_f),
                        dst_ref=dest(me),
                        send_sem=send.at[iteration],
                        recv_sem=recv.at[iteration],
                        device_id=(peer_f, peer_s),
                        device_id_type=MESH,
                    ).start()
        else:
            every = dest(slice(0, total - 1))
            done = pltpu.make_async_remote_copy(
                src_ref=every,
                dst_ref=every,
                send_sem=send.at[iteration],
                recv_sem=recv.at[iteration],
                device_id=(peers_f[1], me_s),
                device_id_type=MESH,
            )
            done.wait_recv()
            done.wait_send()

    def shell_terms():
        for m in range(NB):
            for i in range(ROWS):
                column = columns_ref[m, base + i]
                rows_x[m * ROWS + i : m * ROWS + i + 1] = struct_all[pl.ds(column, 1)]
        if iteration == 0:
            for copy in local:
                copy.wait()
        entries = rows_x[...]
        parts = jnp.concatenate([p.astype(jnp.float32) for p in split(entries)], axis=0).astype(
            jnp.bfloat16
        )
        count = NB * ROWS
        acc = jnp.zeros((ROWS, FOLD), jnp.float32)
        for c in range(0, BLK * BLK, CHUNK):
            wide = dot(parts, expand[:, c : c + CHUNK], NN)
            wide = wide[0:count] + wide[count:]
            for m in range(NB):
                product = wide[m * ROWS : (m + 1) * ROWS] * blocks[m, :, c : c + CHUNK]
                for g in range(0, CHUNK, FOLD):
                    acc = acc + product[:, g : g + FOLD]
        terms[...] = dot_left(acc, fold, NN)

    width = 3 * NPB
    for iteration in range(ITERS):
        first = iteration * SWEEPS
        by_node = dot_right(perm, struct_all[...], NT)
        picked = dot_left(by_node, block_table[...], NN)
        moved = []
        for j in range(3):
            masked = picked[j * NPB : (j + 1) * NPB] * node_mask[...]
            shifted = masked[:, 0:slots]
            for t in range(1, TMAP):
                shifted = shifted + masked[:, t * slots : (t + 1) * slots]
            moved.append(jnp.sum(shifted, axis=0, keepdims=True))
        displaced = jnp.concatenate(moved, axis=0)
        coupled = jnp.concatenate(
            [jnp.sum(load_ref[v] * displaced, axis=0, keepdims=True) for v in range(NVAR)], axis=0
        )
        coupling = dot_left(pad_rows(coupled * live), cell_table[...], NT)
        right = coupling[0:NVAR] + rhs_ref[...]
        out = jnp.zeros((NVAR, cells), jnp.float32)
        for w in range(NVAR):
            out = out + diag_t[w, 0:NVAR] * right[w : w + 1]
        bias[iteration] = pad_rows(out)
        swap_start(*bias_swap(iteration))

        for sweep in range(SWEEPS):
            t = first + sweep
            if sweep == 1:
                shell_terms()
            wide = sweep in WIDE
            if sweep - 1 not in WIDE:
                swap_wait(*halo(t))
                whole = []
                for ref in (low_halo, state, high_halo):
                    for a in range(tiles):
                        whole.append(ref[t, :, a * LANE : (a + 1) * LANE])
            if iteration == 0 and sweep == WIDE[0]:
                swap_wait(*index_swap())
                swap_wait(*fold_swap())
            if sweep == WIDE[0]:
                swap_wait(*bias_swap(iteration))
            targets = [(folded, bias, index_all, a, tiles + a, tiles - half_tiles) for a in range(tiles)]
            if wide:
                for a in range(half_tiles):
                    targets.append(
                        (fold_low, bias_low, index_low, a, tiles - half_tiles + a, -half_tiles)
                    )
                    targets.append(
                        (fold_high, bias_high, index_high, a, 2 * tiles + a, 2 * tiles - half_tiles)
                    )
            after = [None] * (3 * tiles)
            for fold_ref, bias_ref, place_ref, a, at, shift in targets:
                span = slice(a * LANE, (a + 1) * LANE)
                acc = bias_ref[iteration, :, span]
                for k in range(FACES):
                    index = jnp.broadcast_to(place_ref[k : k + 1, span], (ROWS, LANE))
                    lane = index & (LANE - 1)
                    tile = lax.shift_right_logical(index, 7) + shift
                    beside = None
                    for b in range(at - half_tiles, at + half_tiles + 1):
                        found = jnp.take_along_axis(
                            whole[b], lane, axis=1, mode="promise_in_bounds"
                        )
                        beside = found if beside is None else jnp.where(tile == b, found, beside)
                    for u in range(NVAR):
                        acc = acc - fold_ref[k, u, :, span] * beside[u : u + 1]
                after[at] = acc
                if at == tiles + a:
                    state[t + 1, :, span] = acc
            whole = after
            if t + 1 < ITERS * SWEEPS and not wide:
                swap_start(*halo(t + 1))

        last = state[first + SWEEPS]
        at_surface = dot_left(last, cell_table[...], (((1,), (0,)), ((), ())))
        sens = jnp.zeros((3, slots), jnp.float32)
        for v in range(NVAR):
            sens = sens + disp_ref[v] * at_surface[v : v + 1]
        sens = sens * live
        scaled = []
        for j in range(3):
            row = sens[j : j + 1]
            scaled.append(node_mask[...] * jnp.concatenate([row] * TMAP, axis=1))
        values = jnp.concatenate(scaled, axis=0)
        forces = dot_right(block_table[...], values, NT)
        for p in range(total):
            forces_out[iteration, p, :, 0:width] = forces[p * piece : (p + 1) * piece]
        all_copies(
            iteration,
            lambda p: forces_out.at[iteration, p],
            lambda q: forces_land.at[iteration, q],
            force_send,
            force_recv,
            "start",
        )
        forces_land[iteration, me] = forces_out[iteration, me_s * fluid_n + me_f]
        all_copies(
            iteration,
            lambda p: forces_out.at[iteration, p],
            lambda q: forces_land.at[iteration, q],
            force_send,
            force_recv,
            "wait",
        )
        mine = forces_land[iteration, 0]
        for q in range(1, total):
            mine = mine + forces_land[iteration, q]
        mine = jnp.concatenate([mine] * (ROWS // piece), axis=0)
        spread = dot_left(mine[:, 0:width], perm, NN)
        load = right_struct[pl.ds(pl.multiple_of(base, ROWS), ROWS)] + spread - terms[...]
        tiled = dot_left(load, fold, NT)
        solved = jnp.zeros((2 * ROWS, LANE), jnp.float32)
        for c in range(0, BLK * BLK, CHUNK):
            product = inverse[:, c : c + CHUNK] * jnp.concatenate([tiled] * (CHUNK // FOLD), axis=1)
            parts = jnp.concatenate(
                [p.astype(jnp.float32) for p in split(product)], axis=0
            ).astype(jnp.bfloat16)
            solved = solved + dot(parts, expand[:, c : c + CHUNK], NT)
        solved = solved[0:ROWS] + solved[ROWS:]
        for g in range(ROWS // piece):
            @pl.when(my_row - base == g * piece)
            def _():
                result[iteration] = solved[g * piece : (g + 1) * piece]

        if iteration + 1 < ITERS:
            all_copies(
                iteration,
                lambda p: result.at[iteration],
                lambda q: final_land.at[iteration, q],
                gather_send,
                gather_recv,
                "start",
            )
            final_land[iteration, me] = result[iteration]
            all_copies(
                iteration,
                lambda p: result.at[iteration],
                lambda q: final_land.at[iteration, q],
                gather_send,
                gather_recv,
                "wait",
            )
            for q in range(total):
                f, s = q // struct_n, q % struct_n
                row = (s * fluid_n + f) * piece
                struct_all[row : row + piece] = final_land[iteration, q]
        else:
            def one(r, landing_f, action):
                copy = pltpu.make_async_remote_copy(
                    src_ref=result.at[iteration],
                    dst_ref=final_land.at[iteration, landing_f],
                    send_sem=final_send.at[r],
                    recv_sem=final_recv.at[landing_f],
                    device_id=((me_f + r) % fluid_n, me_s),
                    device_id_type=MESH,
                )
                getattr(copy, action)()

            for r in range(1, fluid_n):
                one(r, me_f, "start")
            fluid_ref[...] = last[0:NVAR]
            final_land[iteration, me_f] = result[iteration]
            for r in range(1, fluid_n):
                one(r, (me_f + r) % fluid_n, "wait")
            for f in range(fluid_n):
                struct_ref[f * piece : (f + 1) * piece] = final_land[iteration, f]


def finish(fluid_in, struct_in, fluid_ref, struct_ref):
    fluid_ref[...] = fluid_in[...]
    per = FOLD // BLK
    groups = struct_in.shape[0] // per
    wide = jnp.concatenate(
        [struct_in[pl.ds(q, groups, stride=per)][:, 0:BLK] for q in range(per)], axis=1
    )
    for q in range(FOLD // LANE):
        struct_ref[pl.ds(q, groups, stride=FOLD // LANE)] = wide[:, q * LANE : (q + 1) * LANE]


def body(
    fluid_n,
    struct_n,
    fluid_adjoint,
    fluid_rhs,
    diag_inverse,
    face_blocks,
    face_index,
    surface_cell,
    surface_count,
    transfer_node,
    transfer_weight,
    load_sens,
    disp_sens,
    struct_adjoint,
    struct_rhs,
    shell_blocks,
    shell_inverse,
    shell_columns,
):
    cells = fluid_adjoint.shape[1]
    slots = surface_cell.shape[0]
    block_rows = struct_adjoint.shape[0] // BLK
    shell_total = block_rows * struct_n
    piece = block_rows // fluid_n
    total = fluid_n * struct_n
    half = cells // 2
    sweeps = ITERS * SWEEPS
    vmem = pl.BlockSpec(memory_space=pltpu.VMEM)
    far = pl.BlockSpec(memory_space=pl.ANY)
    smem = pl.BlockSpec(memory_space=pltpu.SMEM)
    f32, bf16 = jnp.float32, jnp.bfloat16
    dma = pltpu.SemaphoreType.DMA

    fluid_out, struct_out = pl.pallas_call(
        functools.partial(kernel, fluid_n, struct_n, piece),
        out_shape=(
            jax.ShapeDtypeStruct((NVAR, cells), f32),
            jax.ShapeDtypeStruct((block_rows, LANE), f32),
        ),
        in_specs=[vmem] * 13 + [far, far, smem],
        out_specs=(vmem, vmem),
        scratch_shapes=[
            pltpu.VMEM((sweeps + 1, ROWS, cells), f32),
            pltpu.VMEM((sweeps, ROWS, cells), f32),
            pltpu.VMEM((sweeps, ROWS, cells), f32),
            pltpu.VMEM((FACES, NVAR, ROWS, cells), f32),
            pltpu.VMEM((FACES, NVAR, ROWS, half), f32),
            pltpu.VMEM((FACES, NVAR, ROWS, half), f32),
            pltpu.VMEM((ITERS, ROWS, cells), f32),
            pltpu.VMEM((ITERS, ROWS, half), f32),
            pltpu.VMEM((ITERS, ROWS, half), f32),
            pltpu.VMEM((ROWS, cells), jnp.int32),
            pltpu.VMEM((ROWS, half), jnp.int32),
            pltpu.VMEM((ROWS, half), jnp.int32),
            pltpu.VMEM((NVAR, ROWS, cells), f32),
            pltpu.VMEM((cells, slots), bf16),
            pltpu.VMEM((shell_total, TMAP * slots), bf16),
            pltpu.VMEM((NPB, TMAP * slots), f32),
            pltpu.VMEM((NB, ROWS, BLK * BLK), f32),
            pltpu.VMEM((ROWS, BLK * BLK), f32),
            pltpu.VMEM((LANE, BLK * BLK), bf16),
            pltpu.VMEM((block_rows, LANE), f32),
            pltpu.VMEM((block_rows, LANE), f32),
            pltpu.VMEM((struct_n, block_rows, LANE), f32),
            pltpu.VMEM((shell_total, LANE), f32),
            pltpu.VMEM((NB * ROWS, LANE), f32),
            pltpu.VMEM((ROWS, LANE), f32),
            pltpu.VMEM((ITERS, total, piece, LANE), f32),
            pltpu.VMEM((ITERS, total, piece, LANE), f32),
            pltpu.VMEM((ITERS, piece, LANE), f32),
            pltpu.VMEM((ITERS, total, piece, LANE), f32),
            dma((sweeps, 2)),
            dma((sweeps, 2)),
            dma((2 + ITERS, 2)),
            dma((2 + ITERS, 2)),
            dma((struct_n,)),
            dma((struct_n,)),
            dma((ITERS,)),
            dma((ITERS,)),
            dma((ITERS,)),
            dma((ITERS,)),
            dma((fluid_n,)),
            dma((fluid_n,)),
            dma((NB + 1,)),
        ],
        compiler_params=pltpu.CompilerParams(collective_id=0, has_side_effects=True),
    )(
        fluid_adjoint,
        fluid_rhs,
        diag_inverse,
        jnp.transpose(face_blocks, (1, 2, 0, 3)),
        face_index,
        surface_cell.reshape(1, slots),
        surface_count.reshape(1, 1),
        transfer_node,
        transfer_weight,
        jnp.transpose(load_sens, (1, 0, 2)),
        disp_sens,
        struct_adjoint.reshape(-1, LANE),
        struct_rhs.reshape(-1, LANE),
        shell_blocks,
        shell_inverse,
        shell_columns,
    )
    fluid_out, struct_out = pl.pallas_call(
        finish,
        out_shape=(
            jax.ShapeDtypeStruct((NVAR, cells), f32),
            jax.ShapeDtypeStruct((block_rows * BLK // LANE, LANE), f32),
        ),
        in_specs=[vmem, vmem],
        out_specs=(vmem, vmem),
    )(fluid_out, struct_out)
    return fluid_out, struct_out.reshape(-1)


def solution(mesh):
    placed = (
        P(None, ("fluid", "struct")),
        P(None, ("fluid", "struct")),
        P(None, None, ("fluid", "struct")),
        P(None, None, None, ("fluid", "struct")),
        P(None, ("fluid", "struct")),
        P(("fluid", "struct")),
        P(("fluid", "struct")),
        P(None, ("fluid", "struct")),
        P(None, ("fluid", "struct")),
        P(None, None, ("fluid", "struct")),
        P(None, None, ("fluid", "struct")),
        P("struct"),
        P("struct"),
        P(None, "struct", None),
        P("struct", None),
        P(None, "struct"),
    )
    return jax.shard_map(
        functools.partial(body, mesh.shape["fluid"], mesh.shape["struct"]),
        mesh=mesh,
        in_specs=placed,
        out_specs=(P(None, ("fluid", "struct")), P("struct")),
        check_vma=False,
    )
```

```python
import functools

import jax
import jax.numpy as jnp
from jax import lax
from jax.experimental import pallas as pl
from jax.experimental.pallas import tpu as pltpu
from jax.sharding import PartitionSpec as P

NVAR = 5
FACES = 6
TMAP = 3
DOF = 6
BLK = 96
NB = 4
SWEEPS = 6
ITERS = 2
NPB = BLK // DOF
LANE = 128
ROWS = 8
FOLD = 384
CHUNK = 768
NEAR = (2, 5)
FAR = 3
MESH = pl.DeviceIdType.MESH
NN = (((1,), (0,)), ((), ()))
NT = (((1,), (1,)), ((), ()))


def split(value):
    high = value.astype(jnp.bfloat16)
    return high, (value - high.astype(jnp.float32)).astype(jnp.bfloat16)


def dot(left, right, dims):
    return lax.dot_general(left, right, dims, preferred_element_type=jnp.float32)


def dot_left(value, table, dims):
    rows = value.shape[0]
    stacked = jnp.concatenate([p.astype(jnp.float32) for p in split(value)], axis=0)
    out = dot(stacked.astype(jnp.bfloat16), table, dims)
    return out[0:rows] + out[rows : 2 * rows]


def dot_right(table, value, dims):
    high, low = split(value)
    return dot(table, high, dims) + dot(table, low, dims)


def iota(shape, axis):
    return lax.broadcasted_iota(jnp.int32, shape, axis)


def pad_rows(value, rows=ROWS):
    return jnp.concatenate(
        [value, jnp.zeros((rows - value.shape[0], value.shape[1]), value.dtype)], axis=0
    )


def by_block(flat, out):
    groups = flat.shape[0] * LANE // FOLD
    wide = jnp.concatenate(
        [flat[pl.ds(a, groups, stride=FOLD // LANE)] for a in range(FOLD // LANE)], axis=1
    )
    for q in range(FOLD // BLK):
        part = wide[:, q * BLK : (q + 1) * BLK]
        full = jnp.concatenate([part, jnp.zeros((groups, LANE - BLK), jnp.float32)], axis=1)
        out[pl.ds(q, groups, stride=FOLD // BLK)] = full


def kernel(
    fluid_n,
    struct_n,
    piece,
    adj_far,
    rhs_far,
    diag_far,
    face_far,
    index_far,
    cell_far,
    count_ref,
    node_far,
    weight_far,
    load_far,
    disp_far,
    sadj_far,
    srhs_far,
    blocks_ref,
    inverse_ref,
    columns_far,
    fluid_ref,
    struct_ref,
    state,
    work,
    folded,
    code,
    pair_fold,
    pair_code,
    base_bias,
    bias,
    partial,
    mix,
    mix_int,
    fold_mix,
    diag_mix,
    pack,
    pack_near,
    cell_table,
    block_table,
    node_mask,
    blocks,
    inverse,
    expand,
    start_struct,
    right_struct,
    struct_all,
    rows_x,
    terms,
    forces_out,
    forces_land,
    result,
    final_land,
    state_send,
    state_recv,
    once_send,
    once_recv,
    start_send,
    start_recv,
    force_send,
    force_recv,
    gather_send,
    gather_recv,
    final_send,
    final_recv,
    local_sem,
    input_sem,
    adj_ref,
    rhs_ref,
    diag_ref,
    face_ref,
    index_ref,
    cell_ref,
    node_ref,
    weight_ref,
    load_ref,
    disp_ref,
    sadj_ref,
    srhs_ref,
    columns_ref,
):
    me_f = lax.axis_index("fluid")
    me_s = lax.axis_index("struct")
    me = me_f * struct_n + me_s
    total = fluid_n * struct_n
    cells = adj_ref.shape[1]
    tiles = cells // LANE
    half = tiles // 2
    slots = cell_ref.shape[1]
    shell_total = struct_all.shape[1]
    shard_rows = start_struct.shape[0]
    my_row = me_f * piece
    base = (my_row // ROWS) * ROWS
    own_row = me_s * shard_rows + my_row
    own_x = 3 * half
    own = tiles

    def dev(index):
        return (index // struct_n, index % struct_n)

    peers_f = [(me_f + r) % fluid_n for r in range(fluid_n)]
    peers_s = [(me_s + r) % struct_n for r in range(struct_n)]
    barrier = pltpu.get_barrier_semaphore()
    for rf in reversed(range(fluid_n)):
        for rs in reversed(range(struct_n)):
            if rf + rs:
                pl.semaphore_signal(
                    barrier, inc=1, device_id=(peers_f[rf], peers_s[rs]), device_id_type=MESH
                )

    inputs = []
    for n, (source, landing) in enumerate(
        (
            (sadj_far, sadj_ref),
            (adj_far, adj_ref),
            (srhs_far, srhs_ref),
            (diag_far, diag_ref),
            (face_far, face_ref),
            (index_far, index_ref),
            (cell_far, cell_ref),
            (node_far, node_ref),
            (weight_far, weight_ref),
            (load_far, load_ref),
            (rhs_far, rhs_ref),
            (disp_far, disp_ref),
            (columns_far, columns_ref),
        )
    ):
        inputs.append(pltpu.make_async_copy(source, landing, input_sem.at[n]))
        inputs[n].start()
    local = []
    for m in range(NB):
        local.append(
            pltpu.make_async_copy(
                blocks_ref.at[m, pl.ds(pl.multiple_of(base, ROWS), ROWS)],
                blocks.at[m],
                local_sem.at[m],
            )
        )
    local.append(
        pltpu.make_async_copy(
            inverse_ref.at[pl.ds(pl.multiple_of(base, ROWS), ROWS)], inverse, local_sem.at[NB]
        )
    )
    for copy in local:
        copy.start()

    shifts = (-1, 1, -2, 2)
    sends = (me > 0, me < total - 1, me > 1, me < total - 2)
    takes = (me < total - 1, me > 0, me < total - 2, me > 1)

    def swap_start(copies, send, recv):
        for d, (source, landing) in enumerate(copies):
            @pl.when(sends[d])
            def _():
                pltpu.make_async_remote_copy(
                    src_ref=source,
                    dst_ref=landing,
                    send_sem=send.at[d],
                    recv_sem=recv.at[d],
                    device_id=dev(me + shifts[d]),
                    device_id_type=MESH,
                ).start()

    def swap_wait(copies, send, recv):
        for d, (source, landing) in enumerate(copies):
            copy = pltpu.make_async_remote_copy(
                src_ref=source,
                dst_ref=landing,
                send_sem=send.at[d],
                recv_sem=recv.at[d],
                device_id=dev(me + shifts[d]),
                device_id_type=MESH,
            )

            @pl.when(takes[d])
            def _():
                copy.wait_recv()

            @pl.when(sends[d])
            def _():
                copy.wait_send()

    def rows(ref, first, count):
        return ref.at[:, first : first + count]

    def state_swap(e, wide):
        now = state.at[e]
        copies = [
            (rows(now, own_x, tiles), rows(now, own_x + tiles, tiles)),
            (rows(now, own_x, tiles), rows(now, own_x - tiles, tiles)),
        ]
        if wide:
            copies += [
                (rows(now, own_x, half), rows(now, own_x + 2 * tiles, half)),
                (rows(now, own_x + half, half), rows(now, 0, half)),
            ]
        return copies, state_send.at[e], state_recv.at[e]

    def row_swap(ref, n):
        copies = [
            (rows(ref, own, tiles), rows(ref, own + tiles, tiles)),
            (rows(ref, own, tiles), rows(ref, 0, tiles)),
        ]
        return copies, once_send.at[n], once_recv.at[n]

    def fold_swap(n, first_face, faces, far):
        some = folded.at[first_face * NVAR * NVAR : (first_face + faces) * NVAR * NVAR]
        low, high = rows(some, own, half), rows(some, own + half, half)
        if far:
            copies = [(high, rows(some, own + tiles + half, half)), (low, rows(some, 0, half))]
        else:
            copies = [(low, rows(some, own + tiles, half)), (high, rows(some, half, half))]
        return copies, once_send.at[n], once_recv.at[n]

    near_first = (0, 0, NEAR[0], False)
    near_next = (3, NEAR[0], NEAR[1] - NEAR[0], False)
    near_rest = (8, NEAR[1], FACES - NEAR[1], False)
    far_first = (6, 0, FAR, True)
    far_rest = (7, FAR, FACES - FAR, True)

    def pack_swap(n):
        copies = [(pack, pack_near.at[1]), (pack, pack_near.at[0])]
        return copies, once_send.at[n], once_recv.at[n]

    def span(a):
        return slice(a * LANE, (a + 1) * LANE)

    def to_rows(value, scratch, count):
        for a in range(tiles):
            scratch[a * ROWS : a * ROWS + count] = value[:, span(a)]
        return [scratch[pl.ds(v, tiles, stride=ROWS)] for v in range(count)]

    def clear(ref, first, count):
        ref[:, first : first + count] = jnp.zeros((ref.shape[0], count, LANE), ref.dtype)

    spare = state.shape[2]
    for e in range(state.shape[0]):
        clear(state.at[e], own_x + 2 * tiles + half, spare - own_x - 2 * tiles - half)

        @pl.when(me == 0)
        def _():
            clear(state.at[e], 0, own_x)

        @pl.when(me == 1)
        def _():
            clear(state.at[e], 0, half)

        @pl.when(me == total - 2)
        def _():
            clear(state.at[e], own_x + 2 * tiles, half)

        @pl.when(me == total - 1)
        def _():
            clear(state.at[e], own_x + tiles, tiles + half)

    @pl.when(me == 0)
    def _():
        for ref in (folded, code, base_bias, bias.at[0]):
            clear(ref, 0, tiles)
        pack_near[0] = jnp.zeros_like(pack)

    @pl.when(me == total - 1)
    def _():
        for ref in (folded, code, base_bias, bias.at[0]):
            clear(ref, own + tiles, tiles)
        pack_near[1] = jnp.zeros_like(pack)

    for copy in inputs[0:3]:
        copy.wait()
    for v, value in enumerate(to_rows(adj_ref[...], mix, NVAR)):
        state[0, v, own_x : own_x + tiles] = value
    by_block(sadj_ref, start_struct)
    by_block(srhs_ref, right_struct)
    forces_out[...] = jnp.zeros_like(forces_out)

    pl.semaphore_wait(barrier, total - 1)

    def start_copy(r, landing):
        return pltpu.make_async_remote_copy(
            src_ref=start_struct,
            dst_ref=struct_all.at[0, pl.ds(pl.multiple_of(landing * shard_rows, shard_rows), shard_rows)],
            send_sem=start_send.at[r],
            recv_sem=start_recv.at[landing],
            device_id=(me_f, peers_s[r]),
            device_id_type=MESH,
        )

    for r in range(1, struct_n):
        start_copy(r, me_s).start()
    swap_start(*state_swap(0, False))

    for copy in inputs[3:]:
        copy.wait()

    def pair(k):
        return slice((k % 2) * tiles, (k % 2 + 1) * tiles)

    for a in range(tiles):
        for v in range(NVAR):
            scale = [
                jnp.broadcast_to(diag_ref[v, w : w + 1, span(a)], (FACES, LANE)) for w in range(NVAR)
            ]
            for u in range(NVAR):
                out = scale[0] * face_ref[u, 0, :, span(a)]
                for w in range(1, NVAR):
                    out = out + scale[w] * face_ref[u, w, :, span(a)]
                at = ((u * NVAR + v) * tiles + a) * ROWS
                fold_mix[at : at + FACES] = out
    for k in range(FACES):
        for u in range(NVAR):
            for v in range(NVAR):
                at = (u * NVAR + v) * tiles * ROWS + k
                value = fold_mix[pl.ds(at, tiles, stride=ROWS)]
                folded[(k * NVAR + u) * NVAR + v, own : own + tiles] = value
                pair_fold[((k // 2) * NVAR + u) * NVAR + v, pair(k)] = value
        if k + 1 == NEAR[0]:
            swap_start(*fold_swap(*near_first))
    for k, value in enumerate(to_rows(index_ref[...], mix_int, FACES)):
        value = value - LANE * iota((tiles, LANE), 0)
        code[k, own : own + tiles] = value
        pair_code[k // 2, pair(k)] = value
    swap_start(*row_swap(code, 1))

    def tables(b, node_of, weight_of, cell_of):
        cell_table[b] = jnp.where(iota((cells, slots), 0) == cell_of, 1.0, 0.0).astype(jnp.bfloat16)
        for t in range(TMAP):
            node = node_of(t)
            block_of = lax.shift_right_logical(node, NPB.bit_length() - 1)
            inside = node & (NPB - 1)
            block_table[b, :, t * slots : (t + 1) * slots] = jnp.where(
                iota((shell_total, slots), 0) == block_of, 1.0, 0.0
            ).astype(jnp.bfloat16)
            node_mask[b, :, t * slots : (t + 1) * slots] = jnp.where(
                iota((NPB, slots), 0) == inside, weight_of(t), 0.0
            )

    live = (iota((1, slots), 1) < count_ref[...]).astype(jnp.float32)
    tables(0, lambda t: node_ref[t : t + 1], lambda t: weight_ref[t : t + 1], cell_ref[...])

    for u in range(NVAR):
        for v in range(NVAR):
            diag_mix[u * ROWS + v : u * ROWS + v + 1] = diag_ref[v, u : u + 1]
    at_slots = dot_left(diag_mix[...], cell_table[0], NN)
    for j in range(3):
        out = at_slots[0:NVAR] * load_ref[0, j : j + 1]
        for u in range(1, NVAR):
            out = out + at_slots[u * ROWS : u * ROWS + NVAR] * load_ref[u, j : j + 1]
        pack[j * ROWS : j * ROWS + NVAR] = out * live
    pack[NVAR : NVAR + TMAP] = weight_ref[...]
    pack[ROWS + NVAR : ROWS + NVAR + TMAP] = node_ref[...].astype(jnp.float32)
    pack[2 * ROWS + NVAR : 3 * ROWS] = jnp.concatenate(
        [cell_ref[...].astype(jnp.float32)] * (ROWS - NVAR), axis=0
    )

    for v in range(NVAR):
        mixed = jnp.sum(diag_ref[v] * rhs_ref[...], axis=0, keepdims=True)
        for a in range(tiles):
            base_bias[v, own + a : own + a + 1] = mixed[:, span(a)]

    for c in range(0, BLK * BLK, CHUNK):
        offset = iota((LANE, CHUNK), 1) + c - BLK * iota((LANE, CHUNK), 0)
        expand[:, c : c + CHUNK] = jnp.where((offset >= 0) & (offset < BLK), 1.0, 0.0).astype(
            jnp.bfloat16
        )
    width = 3 * NPB
    out_row = iota((width, LANE), 0)
    perm = jnp.where(
        iota((width, LANE), 1)
        == (out_row & (NPB - 1)) * DOF + lax.shift_right_logical(out_row, NPB.bit_length() - 1),
        1.0,
        0.0,
    ).astype(jnp.bfloat16)
    perm_twice = jnp.concatenate([perm, perm], axis=0)
    behind = iota((FOLD, LANE), 0) - iota((FOLD, LANE), 1)
    near = (behind == 0) | (behind == BLK) | (behind == 2 * BLK) | (behind == 3 * BLK)
    fold = jnp.where(near & (iota((FOLD, LANE), 1) < BLK), 1.0, 0.0).astype(jnp.bfloat16)

    def sweep(source, first, start):
        acc = list(start)
        for k in range(FACES):
            place = code[k, first : first + ROWS]
            lane = place & (LANE - 1)
            tile = lax.shift_right_logical(place, LANE.bit_length() - 1)
            picks = [tile == o for o in range(tiles + 1)]
            for u in range(NVAR):
                beside = None
                for o in range(tiles + 1):
                    found = jnp.take_along_axis(
                        source[u, first + o : first + o + ROWS], lane, axis=1, mode="promise_in_bounds"
                    )
                    beside = found if beside is None else jnp.where(picks[o], found, beside)
                for v in range(NVAR):
                    at = (k * NVAR + u) * NVAR + v
                    acc[v] = acc[v] - folded[at, first : first + ROWS] * beside
        return acc

    def own_sweep(source):
        acc = [None] * NVAR
        beside_rows = {}
        for u in range(NVAR):
            for o in range(tiles + 1):
                first = own_x - half + o
                once = source[u, first : first + tiles]
                beside_rows[u, o] = jnp.concatenate([once, once], axis=0)
        for k in range(FACES // 2):
            place = pair_code[k]
            lane = place & (LANE - 1)
            tile = lax.shift_right_logical(place, LANE.bit_length() - 1)
            picks = [tile == o for o in range(tiles + 1)]
            for u in range(NVAR):
                beside = None
                for o in range(tiles + 1):
                    found = jnp.take_along_axis(
                        beside_rows[u, o], lane, axis=1, mode="promise_in_bounds"
                    )
                    beside = found if beside is None else jnp.where(picks[o], found, beside)
                for v in range(NVAR):
                    term = pair_fold[(k * NVAR + u) * NVAR + v] * beside
                    acc[v] = term if acc[v] is None else acc[v] + term
        return [a[0:tiles] + a[tiles : 2 * tiles] for a in acc]

    def own_step(i, e, source):
        for v, taken in enumerate(own_sweep(source)):
            state[e, v, own_x : own_x + tiles] = bias[i, v, own : own + tiles] - taken

    def bias_rows(i, first):
        return [bias[i, v, first : first + ROWS] for v in range(NVAR)]

    def into_work(first, values):
        for v in range(NVAR):
            work[v, first + half : first + half + ROWS] = values[v]

    def last_steps(i, e):
        into_work(half, sweep(work, half, bias_rows(i, half)))
        own_step(i, e, work)

    def two_steps(i, e):
        into_work(half, sweep(state.at[e], half, bias_rows(i, half)))
        own_step(i, e + 1, work)

    def three_steps(i, e):
        outer = [sweep(state.at[e], f, bias_rows(i, f)) for f in (0, ROWS)]
        into_work(0, outer[0])
        into_work(ROWS, outer[1])
        last_steps(i, e + 1)

    def couple(i, which):
        by_node = dot_right(perm, struct_all[i], NT)
        parts = jnp.concatenate([p.astype(jnp.float32) for p in split(by_node)], axis=0).astype(
            jnp.bfloat16
        )
        for b in which:
            picked = dot(parts, block_table[b], NN)
            picked = picked[0:width] + picked[width : 2 * width]
            moved = []
            for j in range(3):
                masked = picked[j * NPB : (j + 1) * NPB] * node_mask[b]
                shifted = masked[:, 0:slots]
                for t in range(1, TMAP):
                    shifted = shifted + masked[:, t * slots : (t + 1) * slots]
                moved.append(jnp.sum(shifted, axis=0, keepdims=True))
            displaced = jnp.concatenate(moved, axis=0)
            rates = pack if b == 0 else pack_near.at[b - 1]
            coupled = rates[0:ROWS] * displaced[0:1]
            for j in range(1, 3):
                coupled = coupled + rates[j * ROWS : (j + 1) * ROWS] * displaced[j : j + 1]
            spread = dot_left(coupled, cell_table[b], NT)
            first = (own, 0, own + tiles)[b]
            for v, value in enumerate(to_rows(spread[0:NVAR], mix, NVAR)):
                bias[i, v, first : first + tiles] = base_bias[v, first : first + tiles] + value

    def all_start(source, landing, send, recv):
        for rf in reversed(range(fluid_n)):
            for rs in reversed(range(struct_n)):
                if rf + rs == 0:
                    continue
                peer_f, peer_s = peers_f[rf], peers_s[rs]
                pltpu.make_async_remote_copy(
                    src_ref=source(peer_s * fluid_n + peer_f),
                    dst_ref=landing,
                    send_sem=send,
                    recv_sem=recv,
                    device_id=(peer_f, peer_s),
                    device_id_type=MESH,
                ).start()

    def all_wait(every, send, recv):
        done = pltpu.make_async_remote_copy(
            src_ref=every,
            dst_ref=every,
            send_sem=send,
            recv_sem=recv,
            device_id=(peers_f[1], me_s),
            device_id_type=MESH,
        )
        done.wait_recv()
        done.wait_send()

    def shell_terms(i):
        for m in range(NB):
            for r in range(ROWS):
                column = columns_ref[m, base + r]
                rows_x[m * ROWS + r : m * ROWS + r + 1] = struct_all[i, pl.ds(column, 1)]
        if i == 0:
            for copy in local:
                copy.wait()
        entries = rows_x[...]
        parts = jnp.concatenate([p.astype(jnp.float32) for p in split(entries)], axis=0).astype(
            jnp.bfloat16
        )
        count = NB * ROWS
        acc = jnp.zeros((ROWS, FOLD), jnp.float32)
        for c in range(0, BLK * BLK, CHUNK):
            wide = dot(parts, expand[:, c : c + CHUNK], NN)
            wide = wide[0:count] + wide[count:]
            for m in range(NB):
                product = wide[m * ROWS : (m + 1) * ROWS] * blocks[m, :, c : c + CHUNK]
                for g in range(0, CHUNK, FOLD):
                    acc = acc + product[:, g : g + FOLD]
        terms[...] = dot_left(acc, fold, NN)

    def send_forces(i, e):
        for v in range(NVAR):
            mix[v * tiles : (v + 1) * tiles] = state[e, v, own_x : own_x + tiles]
        last = jnp.concatenate(
            [mix[pl.ds(a, NVAR, stride=tiles)] for a in range(tiles)], axis=1
        )
        at_surface = dot_left(pad_rows(last), cell_table[0], NN)
        sens = jnp.zeros((3, slots), jnp.float32)
        for v in range(NVAR):
            sens = sens + disp_ref[v] * at_surface[v : v + 1]
        sens = sens * live
        scaled = []
        for j in range(3):
            row = sens[j : j + 1]
            scaled.append(node_mask[0] * jnp.concatenate([row] * TMAP, axis=1))
        values = jnp.concatenate(scaled, axis=0)
        both = jnp.concatenate([p.astype(jnp.float32) for p in split(values)], axis=0)
        forces_out[i, :, 0 : 2 * width] = dot(block_table[0], both.astype(jnp.bfloat16), NT)
        all_start(
            lambda p: forces_out.at[i, pl.ds(pl.multiple_of(p * piece, piece), piece)],
            forces_land.at[i, me],
            force_send.at[i],
            force_recv.at[i],
        )
        forces_land[i, me] = forces_out[i, pl.ds(pl.multiple_of(own_row, piece), piece)]
        return last

    def solve(i):
        all_wait(forces_land.at[i, 0 : total - 1], force_send.at[i], force_recv.at[i])
        mine = forces_land[i, 0]
        for q in range(1, total):
            mine = mine + forces_land[i, q]
        mine = jnp.concatenate([mine] * (ROWS // piece), axis=0)
        spread = dot_left(mine[:, 0 : 2 * width], perm_twice, NN)
        load = right_struct[pl.ds(pl.multiple_of(base, ROWS), ROWS)] + spread - terms[...]
        tiled = dot_left(load, fold, NT)
        solved = jnp.zeros((2 * ROWS, LANE), jnp.float32)
        for c in range(0, BLK * BLK, CHUNK):
            product = inverse[:, c : c + CHUNK] * jnp.concatenate([tiled] * (CHUNK // FOLD), axis=1)
            parts = jnp.concatenate(
                [p.astype(jnp.float32) for p in split(product)], axis=0
            ).astype(jnp.bfloat16)
            solved = solved + dot(parts, expand[:, c : c + CHUNK], NT)
        solved = solved[0:ROWS] + solved[ROWS:]
        for g in range(ROWS // piece):
            @pl.when(my_row - base == g * piece)
            def _():
                result[i] = solved[g * piece : (g + 1) * piece]

    swap_wait(*state_swap(0, False))
    early = own_sweep(state.at[0])
    struct_all[0, pl.ds(pl.multiple_of(me_s * shard_rows, shard_rows), shard_rows)] = start_struct[...]
    for r in range(1, struct_n):
        start_copy(r, peers_s[r]).wait()
    couple(0, (0,))
    for v in range(NVAR):
        state[1, v, own_x : own_x + tiles] = bias[0, v, own : own + tiles] - early[v]
    swap_start(*state_swap(1, False))
    swap_start(*row_swap(bias.at[0], 2))
    swap_start(*fold_swap(*near_next))
    shell_terms(0)
    swap_wait(*state_swap(1, False))
    own_step(0, 2, state.at[1])
    swap_start(*state_swap(2, False))
    swap_start(*fold_swap(*near_rest))
    swap_start(*pack_swap(4))
    swap_start(*row_swap(base_bias, 5))
    swap_wait(*fold_swap(*near_first))
    swap_wait(*fold_swap(*near_next))
    swap_wait(*fold_swap(*near_rest))
    swap_wait(*row_swap(code, 1))
    swap_wait(*row_swap(bias.at[0], 2))
    swap_wait(*state_swap(2, False))
    two_steps(0, 2)
    swap_start(*state_swap(3, False))
    swap_start(*fold_swap(*far_first))
    swap_wait(*state_swap(3, False))
    two_steps(0, 3)
    swap_start(*state_swap(4, True))
    send_forces(0, 4)
    swap_start(*fold_swap(*far_rest))

    swap_wait(*pack_swap(4))
    swap_wait(*row_swap(base_bias, 5))
    for b in (1, 2):
        near_pack = pack_near.at[b - 1]
        tables(
            b,
            lambda t: near_pack[ROWS + NVAR + t : ROWS + NVAR + t + 1].astype(jnp.int32),
            lambda t: near_pack[NVAR + t : NVAR + t + 1],
            near_pack[2 * ROWS + NVAR : 2 * ROWS + NVAR + 1].astype(jnp.int32),
        )
    swap_wait(*fold_swap(*far_first))
    swap_wait(*fold_swap(*far_rest))
    swap_wait(*state_swap(4, True))
    for f in (0, ROWS):
        outer = sweep(state.at[4], f, [jnp.zeros((ROWS, LANE), jnp.float32)] * NVAR)
        for v in range(NVAR):
            partial[v, f : f + ROWS] = outer[v]
    solve(0)
    landing = struct_all.at[1, pl.ds(pl.multiple_of(own_row, piece), piece)]
    all_start(lambda p: result.at[0], landing, gather_send, gather_recv)
    struct_all[1, pl.ds(pl.multiple_of(own_row, piece), piece)] = result[0]
    all_wait(struct_all.at[1, 0 : shell_total - piece], gather_send, gather_recv)

    couple(1, (0, 1, 2))
    for f in (0, ROWS):
        into_work(f, [partial[v, f : f + ROWS] + bias[1, v, f : f + ROWS] for v in range(NVAR)])
    last_steps(1, 5)
    swap_start(*state_swap(5, True))
    shell_terms(1)
    swap_wait(*state_swap(5, True))
    three_steps(1, 5)
    last = send_forces(1, 6)
    fluid_ref[...] = last
    solve(1)

    def final_copy(r, landing):
        return pltpu.make_async_remote_copy(
            src_ref=result.at[1],
            dst_ref=final_land.at[landing],
            send_sem=final_send.at[r],
            recv_sem=final_recv.at[landing],
            device_id=(peers_f[r], me_s),
            device_id_type=MESH,
        )

    for r in range(1, fluid_n):
        final_copy(r, me_f).start()
    final_land[me_f] = result[1]
    for r in range(1, fluid_n):
        final_copy(r, peers_f[r]).wait()
    for f in range(fluid_n):
        struct_ref[f * piece : (f + 1) * piece] = final_land[f]


def finish(fluid_in, struct_in, fluid_ref, struct_ref):
    fluid_ref[...] = fluid_in[...]
    per = FOLD // BLK
    groups = struct_in.shape[0] // per
    wide = jnp.concatenate(
        [struct_in[pl.ds(q, groups, stride=per)][:, 0:BLK] for q in range(per)], axis=1
    )
    for q in range(FOLD // LANE):
        struct_ref[pl.ds(q, groups, stride=FOLD // LANE)] = wide[:, q * LANE : (q + 1) * LANE]


def body(
    fluid_n,
    struct_n,
    fluid_adjoint,
    fluid_rhs,
    diag_inverse,
    face_blocks,
    face_index,
    surface_cell,
    surface_count,
    transfer_node,
    transfer_weight,
    load_sens,
    disp_sens,
    struct_adjoint,
    struct_rhs,
    shell_blocks,
    shell_inverse,
    shell_columns,
):
    cells = fluid_adjoint.shape[1]
    slots = surface_cell.shape[0]
    block_rows = struct_adjoint.shape[0] // BLK
    shell_total = block_rows * struct_n
    piece = block_rows // fluid_n
    total = fluid_n * struct_n
    tiles = cells // LANE
    vmem = pl.BlockSpec(memory_space=pltpu.VMEM)
    far = pl.BlockSpec(memory_space=pl.ANY)
    f32, bf16 = jnp.float32, jnp.bfloat16
    dma = pltpu.SemaphoreType.DMA

    fluid_out, struct_out = pl.pallas_call(
        functools.partial(kernel, fluid_n, struct_n, piece),
        out_shape=(
            jax.ShapeDtypeStruct((NVAR, cells), f32),
            jax.ShapeDtypeStruct((block_rows, LANE), f32),
        ),
        in_specs=[far] * 6 + [vmem] + [far] * 9,
        out_specs=(vmem, vmem),
        scratch_shapes=[
            pltpu.VMEM((7, NVAR, 3 * ROWS, LANE), f32),
            pltpu.VMEM((NVAR, 3 * ROWS, LANE), f32),
            pltpu.VMEM((FACES * NVAR * NVAR, 2 * ROWS, LANE), f32),
            pltpu.VMEM((FACES, 2 * ROWS, LANE), jnp.int32),
            pltpu.VMEM((FACES // 2 * NVAR * NVAR, ROWS, LANE), f32),
            pltpu.VMEM((FACES // 2, ROWS, LANE), jnp.int32),
            pltpu.VMEM((NVAR, 2 * ROWS, LANE), f32),
            pltpu.VMEM((ITERS, NVAR, 2 * ROWS, LANE), f32),
            pltpu.VMEM((NVAR, 2 * ROWS, LANE), f32),
            pltpu.VMEM((tiles * ROWS, LANE), f32),
            pltpu.VMEM((tiles * ROWS, LANE), jnp.int32),
            pltpu.VMEM((NVAR * NVAR * tiles * ROWS, LANE), f32),
            pltpu.VMEM((NVAR * ROWS, cells), f32),
            pltpu.VMEM((3 * ROWS, slots), f32),
            pltpu.VMEM((2, 3 * ROWS, slots), f32),
            pltpu.VMEM((3, cells, slots), bf16),
            pltpu.VMEM((3, shell_total, TMAP * slots), bf16),
            pltpu.VMEM((3, NPB, TMAP * slots), f32),
            pltpu.VMEM((NB, ROWS, BLK * BLK), f32),
            pltpu.VMEM((ROWS, BLK * BLK), f32),
            pltpu.VMEM((LANE, BLK * BLK), bf16),
            pltpu.VMEM((block_rows, LANE), f32),
            pltpu.VMEM((block_rows, LANE), f32),
            pltpu.VMEM((ITERS, shell_total, LANE), f32),
            pltpu.VMEM((NB * ROWS, LANE), f32),
            pltpu.VMEM((ROWS, LANE), f32),
            pltpu.VMEM((ITERS, shell_total, LANE), f32),
            pltpu.VMEM((ITERS, total, piece, LANE), f32),
            pltpu.VMEM((ITERS, piece, LANE), f32),
            pltpu.VMEM((fluid_n, piece, LANE), f32),
            dma((6, 4)),
            dma((6, 4)),
            dma((9, 2)),
            dma((9, 2)),
            dma((struct_n,)),
            dma((struct_n,)),
            dma((ITERS,)),
            dma((ITERS,)),
            dma,
            dma,
            dma((fluid_n,)),
            dma((fluid_n,)),
            dma((NB + 1,)),
            dma((13,)),
            pltpu.VMEM((NVAR, cells), f32),
            pltpu.VMEM((NVAR, cells), f32),
            pltpu.VMEM((NVAR, NVAR, cells), f32),
            pltpu.VMEM((NVAR, NVAR, FACES, cells), f32),
            pltpu.VMEM((FACES, cells), jnp.int32),
            pltpu.VMEM((1, slots), jnp.int32),
            pltpu.VMEM((TMAP, slots), jnp.int32),
            pltpu.VMEM((TMAP, slots), f32),
            pltpu.VMEM((NVAR, 3, slots), f32),
            pltpu.VMEM((NVAR, 3, slots), f32),
            pltpu.VMEM((block_rows * BLK // LANE, LANE), f32),
            pltpu.VMEM((block_rows * BLK // LANE, LANE), f32),
            pltpu.SMEM((NB, block_rows), jnp.int32),
        ],
        compiler_params=pltpu.CompilerParams(collective_id=0, has_side_effects=True),
    )(
        fluid_adjoint,
        fluid_rhs,
        diag_inverse,
        jnp.transpose(face_blocks, (1, 2, 0, 3)),
        face_index,
        surface_cell.reshape(1, slots),
        surface_count.reshape(1, 1),
        transfer_node,
        transfer_weight,
        jnp.transpose(load_sens, (1, 0, 2)),
        disp_sens,
        struct_adjoint.reshape(-1, LANE),
        struct_rhs.reshape(-1, LANE),
        shell_blocks,
        shell_inverse,
        shell_columns,
    )
    fluid_out, struct_out = pl.pallas_call(
        finish,
        out_shape=(
            jax.ShapeDtypeStruct((NVAR, cells), f32),
            jax.ShapeDtypeStruct((block_rows * BLK // LANE, LANE), f32),
        ),
        in_specs=[vmem, vmem],
        out_specs=(vmem, vmem),
    )(fluid_out, struct_out)
    return fluid_out, struct_out.reshape(-1)


def solution(mesh):
    placed = (
        P(None, ("fluid", "struct")),
        P(None, ("fluid", "struct")),
        P(None, None, ("fluid", "struct")),
        P(None, None, None, ("fluid", "struct")),
        P(None, ("fluid", "struct")),
        P(("fluid", "struct")),
        P(("fluid", "struct")),
        P(None, ("fluid", "struct")),
        P(None, ("fluid", "struct")),
        P(None, None, ("fluid", "struct")),
        P(None, None, ("fluid", "struct")),
        P("struct"),
        P("struct"),
        P(None, "struct", None),
        P("struct", None),
        P(None, "struct"),
    )
    return jax.shard_map(
        functools.partial(body, mesh.shape["fluid"], mesh.shape["struct"]),
        mesh=mesh,
        in_specs=placed,
        out_specs=(P(None, ("fluid", "struct")), P("struct")),
        check_vma=False,
    )
```

```python
import functools

import jax
import jax.numpy as jnp
from jax import lax
from jax.experimental import pallas as pl
from jax.experimental.pallas import tpu as pltpu
from jax.sharding import PartitionSpec as P

NVAR = 5
FACES = 6
TMAP = 3
DOF = 6
BLK = 96
NB = 4
SWEEPS = 6
ITERS = 2
NPB = BLK // DOF
LANE = 128
ROWS = 8
FOLD = 384
CHUNK = 768
NEAR = (2, 5)
FAR = 3
MESH = pl.DeviceIdType.MESH
NN = (((1,), (0,)), ((), ()))
NT = (((1,), (1,)), ((), ()))


def split(value):
    high = value.astype(jnp.bfloat16)
    return high, (value - high.astype(jnp.float32)).astype(jnp.bfloat16)


def dot(left, right, dims):
    return lax.dot_general(left, right, dims, preferred_element_type=jnp.float32)


def dot_left(value, table, dims):
    rows = value.shape[0]
    stacked = jnp.concatenate([p.astype(jnp.float32) for p in split(value)], axis=0)
    out = dot(stacked.astype(jnp.bfloat16), table, dims)
    return out[0:rows] + out[rows : 2 * rows]


def dot_right(table, value, dims):
    high, low = split(value)
    return dot(table, high, dims) + dot(table, low, dims)


def iota(shape, axis):
    return lax.broadcasted_iota(jnp.int32, shape, axis)


def pad_rows(value, rows=ROWS):
    return jnp.concatenate(
        [value, jnp.zeros((rows - value.shape[0], value.shape[1]), value.dtype)], axis=0
    )


def by_block(flat, out):
    groups = flat.shape[0] * LANE // FOLD
    wide = jnp.concatenate(
        [flat[pl.ds(a, groups, stride=FOLD // LANE)] for a in range(FOLD // LANE)], axis=1
    )
    for q in range(FOLD // BLK):
        part = wide[:, q * BLK : (q + 1) * BLK]
        full = jnp.concatenate([part, jnp.zeros((groups, LANE - BLK), jnp.float32)], axis=1)
        out[pl.ds(q, groups, stride=FOLD // BLK)] = full


def kernel(
    fluid_n,
    struct_n,
    piece,
    adj_far,
    rhs_far,
    diag_far,
    face_far,
    index_far,
    cell_far,
    count_ref,
    node_far,
    weight_far,
    load_far,
    disp_far,
    sadj_far,
    srhs_far,
    blocks_ref,
    inverse_ref,
    columns_far,
    fluid_ref,
    struct_ref,
    state,
    work,
    folded,
    code,
    pair_fold,
    pair_code,
    base_bias,
    bias,
    partial,
    mix,
    mix_int,
    fold_mix,
    diag_mix,
    pack,
    pack_near,
    cell_table,
    block_table,
    node_mask,
    blocks,
    inverse,
    expand,
    start_struct,
    right_struct,
    struct_all,
    rows_x,
    known,
    flat,
    mats,
    forces_out,
    forces_land,
    result,
    final_land,
    state_send,
    state_recv,
    once_send,
    once_recv,
    start_send,
    start_recv,
    force_send,
    force_recv,
    gather_send,
    gather_recv,
    final_send,
    final_recv,
    local_sem,
    input_sem,
    adj_ref,
    rhs_ref,
    diag_ref,
    face_ref,
    index_ref,
    cell_ref,
    node_ref,
    weight_ref,
    load_ref,
    disp_ref,
    sadj_ref,
    srhs_ref,
    columns_ref,
):
    me_f = lax.axis_index("fluid")
    me_s = lax.axis_index("struct")
    me = me_f * struct_n + me_s
    total = fluid_n * struct_n
    cells = adj_ref.shape[1]
    tiles = cells // LANE
    half = tiles // 2
    slots = cell_ref.shape[1]
    shell_total = struct_all.shape[1]
    shard_rows = start_struct.shape[0]
    my_row = me_f * piece
    base = (my_row // ROWS) * ROWS
    own_row = me_s * shard_rows + my_row
    own_x = 3 * half
    own = tiles

    def dev(index):
        return (index // struct_n, index % struct_n)

    peers_f = [(me_f + r) % fluid_n for r in range(fluid_n)]
    peers_s = [(me_s + r) % struct_n for r in range(struct_n)]
    barrier = pltpu.get_barrier_semaphore()
    for rf in reversed(range(fluid_n)):
        for rs in reversed(range(struct_n)):
            if rf + rs:
                pl.semaphore_signal(
                    barrier, inc=1, device_id=(peers_f[rf], peers_s[rs]), device_id_type=MESH
                )

    inputs = []
    for n, (source, landing) in enumerate(
        (
            (sadj_far, sadj_ref),
            (adj_far, adj_ref),
            (srhs_far, srhs_ref),
            (diag_far, diag_ref),
            (face_far, face_ref),
            (index_far, index_ref),
            (cell_far, cell_ref),
            (node_far, node_ref),
            (weight_far, weight_ref),
            (load_far, load_ref),
            (rhs_far, rhs_ref),
            (disp_far, disp_ref),
            (columns_far, columns_ref),
        )
    ):
        inputs.append(pltpu.make_async_copy(source, landing, input_sem.at[n]))
        inputs[n].start()
    local = []
    for m in range(NB):
        local.append(
            pltpu.make_async_copy(
                blocks_ref.at[m, pl.ds(pl.multiple_of(base, ROWS), ROWS)],
                blocks.at[m],
                local_sem.at[m],
            )
        )
    local.append(
        pltpu.make_async_copy(
            inverse_ref.at[pl.ds(pl.multiple_of(base, ROWS), ROWS)], inverse, local_sem.at[NB]
        )
    )
    for copy in local:
        copy.start()

    shifts = (-1, 1, -2, 2)
    sends = (me > 0, me < total - 1, me > 1, me < total - 2)
    takes = (me < total - 1, me > 0, me < total - 2, me > 1)

    def swap_start(copies, send, recv):
        for d, (source, landing) in enumerate(copies):
            @pl.when(sends[d])
            def _():
                pltpu.make_async_remote_copy(
                    src_ref=source,
                    dst_ref=landing,
                    send_sem=send.at[d],
                    recv_sem=recv.at[d],
                    device_id=dev(me + shifts[d]),
                    device_id_type=MESH,
                ).start()

    def swap_wait(copies, send, recv):
        for d, (source, landing) in enumerate(copies):
            copy = pltpu.make_async_remote_copy(
                src_ref=source,
                dst_ref=landing,
                send_sem=send.at[d],
                recv_sem=recv.at[d],
                device_id=dev(me + shifts[d]),
                device_id_type=MESH,
            )

            @pl.when(takes[d])
            def _():
                copy.wait_recv()

            @pl.when(sends[d])
            def _():
                copy.wait_send()

    def rows(ref, first, count):
        return ref.at[:, first : first + count]

    def state_swap(e, wide):
        now = state.at[e]
        copies = [
            (rows(now, own_x, tiles), rows(now, own_x + tiles, tiles)),
            (rows(now, own_x, tiles), rows(now, own_x - tiles, tiles)),
        ]
        if wide:
            copies += [
                (rows(now, own_x, half), rows(now, own_x + 2 * tiles, half)),
                (rows(now, own_x + half, half), rows(now, 0, half)),
            ]
        return copies, state_send.at[e], state_recv.at[e]

    def row_swap(ref, n):
        copies = [
            (rows(ref, own, tiles), rows(ref, own + tiles, tiles)),
            (rows(ref, own, tiles), rows(ref, 0, tiles)),
        ]
        return copies, once_send.at[n], once_recv.at[n]

    def fold_swap(n, first_face, faces, far):
        some = folded.at[first_face * NVAR * NVAR : (first_face + faces) * NVAR * NVAR]
        low, high = rows(some, own, half), rows(some, own + half, half)
        if far:
            copies = [(high, rows(some, own + tiles + half, half)), (low, rows(some, 0, half))]
        else:
            copies = [(low, rows(some, own + tiles, half)), (high, rows(some, half, half))]
        return copies, once_send.at[n], once_recv.at[n]

    near_first = (0, 0, NEAR[0], False)
    near_next = (3, NEAR[0], NEAR[1] - NEAR[0], False)
    near_rest = (8, NEAR[1], FACES - NEAR[1], False)
    far_first = (6, 0, FAR, True)
    far_rest = (7, FAR, FACES - FAR, True)

    def pack_swap(n):
        copies = [(pack, pack_near.at[1]), (pack, pack_near.at[0])]
        return copies, once_send.at[n], once_recv.at[n]

    def span(a):
        return slice(a * LANE, (a + 1) * LANE)

    def to_rows(value, scratch, count):
        for a in range(tiles):
            scratch[a * ROWS : a * ROWS + count] = value[:, span(a)]
        return [scratch[pl.ds(v, tiles, stride=ROWS)] for v in range(count)]

    def clear(ref, first, count):
        ref[:, first : first + count] = jnp.zeros((ref.shape[0], count, LANE), ref.dtype)

    spare = state.shape[2]
    for e in range(state.shape[0]):
        clear(state.at[e], own_x + 2 * tiles + half, spare - own_x - 2 * tiles - half)

        @pl.when(me == 0)
        def _():
            clear(state.at[e], 0, own_x)

        @pl.when(me == 1)
        def _():
            clear(state.at[e], 0, half)

        @pl.when(me == total - 2)
        def _():
            clear(state.at[e], own_x + 2 * tiles, half)

        @pl.when(me == total - 1)
        def _():
            clear(state.at[e], own_x + tiles, tiles + half)

    @pl.when(me == 0)
    def _():
        for ref in (folded, code, base_bias, bias.at[0]):
            clear(ref, 0, tiles)
        pack_near[0] = jnp.zeros_like(pack)

    @pl.when(me == total - 1)
    def _():
        for ref in (folded, code, base_bias, bias.at[0]):
            clear(ref, own + tiles, tiles)
        pack_near[1] = jnp.zeros_like(pack)

    for copy in inputs[0:3]:
        copy.wait()
    for v, value in enumerate(to_rows(adj_ref[...], mix, NVAR)):
        state[0, v, own_x : own_x + tiles] = value
    by_block(sadj_ref, start_struct)
    by_block(srhs_ref, right_struct)
    forces_out[...] = jnp.zeros_like(forces_out)
    result[...] = jnp.zeros_like(result)

    pl.semaphore_wait(barrier, total - 1)

    def start_copy(r, landing):
        return pltpu.make_async_remote_copy(
            src_ref=start_struct,
            dst_ref=struct_all.at[0, pl.ds(pl.multiple_of(landing * shard_rows, shard_rows), shard_rows)],
            send_sem=start_send.at[r],
            recv_sem=start_recv.at[landing],
            device_id=(me_f, peers_s[r]),
            device_id_type=MESH,
        )

    for r in range(1, struct_n):
        start_copy(r, me_s).start()
    swap_start(*state_swap(0, False))

    for copy in inputs[3:]:
        copy.wait()

    def pair(k):
        return slice((k % 2) * tiles, (k % 2 + 1) * tiles)

    for a in range(tiles):
        for v in range(NVAR):
            scale = [
                jnp.broadcast_to(diag_ref[v, w : w + 1, span(a)], (FACES, LANE)) for w in range(NVAR)
            ]
            for u in range(NVAR):
                out = scale[0] * face_ref[u, 0, :, span(a)]
                for w in range(1, NVAR):
                    out = out + scale[w] * face_ref[u, w, :, span(a)]
                at = ((u * NVAR + v) * tiles + a) * ROWS
                fold_mix[at : at + FACES] = out
    for k in range(FACES):
        for u in range(NVAR):
            for v in range(NVAR):
                at = (u * NVAR + v) * tiles * ROWS + k
                value = fold_mix[pl.ds(at, tiles, stride=ROWS)]
                folded[(k * NVAR + u) * NVAR + v, own : own + tiles] = value
                pair_fold[((k // 2) * NVAR + u) * NVAR + v, pair(k)] = value
        if k + 1 == NEAR[0]:
            swap_start(*fold_swap(*near_first))
    for k, value in enumerate(to_rows(index_ref[...], mix_int, FACES)):
        value = value - LANE * iota((tiles, LANE), 0)
        code[k, own : own + tiles] = value
        pair_code[k // 2, pair(k)] = value
    swap_start(*row_swap(code, 1))

    def tables(b, node_of, weight_of, cell_of):
        cell_table[b] = jnp.where(iota((cells, slots), 0) == cell_of, 1.0, 0.0).astype(jnp.bfloat16)
        for t in range(TMAP):
            node = node_of(t)
            block_of = lax.shift_right_logical(node, NPB.bit_length() - 1)
            inside = node & (NPB - 1)
            block_table[b, :, t * slots : (t + 1) * slots] = jnp.where(
                iota((shell_total, slots), 0) == block_of, 1.0, 0.0
            ).astype(jnp.bfloat16)
            node_mask[b, :, t * slots : (t + 1) * slots] = jnp.where(
                iota((NPB, slots), 0) == inside, weight_of(t), 0.0
            )

    live = (iota((1, slots), 1) < count_ref[...]).astype(jnp.float32)
    tables(0, lambda t: node_ref[t : t + 1], lambda t: weight_ref[t : t + 1], cell_ref[...])

    for u in range(NVAR):
        for v in range(NVAR):
            diag_mix[u * ROWS + v : u * ROWS + v + 1] = diag_ref[v, u : u + 1]
    at_slots = dot_left(diag_mix[...], cell_table[0], NN)
    for j in range(3):
        out = at_slots[0:NVAR] * load_ref[0, j : j + 1]
        for u in range(1, NVAR):
            out = out + at_slots[u * ROWS : u * ROWS + NVAR] * load_ref[u, j : j + 1]
        pack[j * ROWS : j * ROWS + NVAR] = out * live
    pack[NVAR : NVAR + TMAP] = weight_ref[...]
    pack[ROWS + NVAR : ROWS + NVAR + TMAP] = node_ref[...].astype(jnp.float32)
    pack[2 * ROWS + NVAR : 3 * ROWS] = jnp.concatenate(
        [cell_ref[...].astype(jnp.float32)] * (ROWS - NVAR), axis=0
    )

    for v in range(NVAR):
        mixed = jnp.sum(diag_ref[v] * rhs_ref[...], axis=0, keepdims=True)
        for a in range(tiles):
            base_bias[v, own + a : own + a + 1] = mixed[:, span(a)]

    for c in range(0, BLK * BLK, CHUNK):
        offset = iota((LANE, CHUNK), 1) + c - BLK * iota((LANE, CHUNK), 0)
        expand[:, c : c + CHUNK] = jnp.where((offset >= 0) & (offset < BLK), 1.0, 0.0).astype(
            jnp.bfloat16
        )
    width = 3 * NPB
    out_row = iota((width, LANE), 0)
    perm = jnp.where(
        iota((width, LANE), 1)
        == (out_row & (NPB - 1)) * DOF + lax.shift_right_logical(out_row, NPB.bit_length() - 1),
        1.0,
        0.0,
    ).astype(jnp.bfloat16)
    perm_twice = jnp.concatenate([perm, perm], axis=0)
    behind = iota((FOLD, LANE), 0) - iota((FOLD, LANE), 1)
    near = (behind == 0) | (behind == BLK) | (behind == 2 * BLK) | (behind == 3 * BLK)
    fold = jnp.where(near & (iota((FOLD, LANE), 1) < BLK), 1.0, 0.0).astype(jnp.bfloat16)

    def sweep(source, first, start):
        acc = list(start)
        for k in range(FACES):
            place = code[k, first : first + ROWS]
            lane = place & (LANE - 1)
            tile = lax.shift_right_logical(place, LANE.bit_length() - 1)
            picks = [tile == o for o in range(tiles + 1)]
            for u in range(NVAR):
                beside = None
                for o in range(tiles + 1):
                    found = jnp.take_along_axis(
                        source[u, first + o : first + o + ROWS], lane, axis=1, mode="promise_in_bounds"
                    )
                    beside = found if beside is None else jnp.where(picks[o], found, beside)
                for v in range(NVAR):
                    at = (k * NVAR + u) * NVAR + v
                    acc[v] = acc[v] - folded[at, first : first + ROWS] * beside
        return acc

    def own_sweep(source):
        acc = [None] * NVAR
        beside_rows = {}
        for u in range(NVAR):
            for o in range(tiles + 1):
                first = own_x - half + o
                once = source[u, first : first + tiles]
                beside_rows[u, o] = jnp.concatenate([once, once], axis=0)
        for k in range(FACES // 2):
            place = pair_code[k]
            lane = place & (LANE - 1)
            tile = lax.shift_right_logical(place, LANE.bit_length() - 1)
            picks = [tile == o for o in range(tiles + 1)]
            for u in range(NVAR):
                beside = None
                for o in range(tiles + 1):
                    found = jnp.take_along_axis(
                        beside_rows[u, o], lane, axis=1, mode="promise_in_bounds"
                    )
                    beside = found if beside is None else jnp.where(picks[o], found, beside)
                for v in range(NVAR):
                    term = pair_fold[(k * NVAR + u) * NVAR + v] * beside
                    acc[v] = term if acc[v] is None else acc[v] + term
        return [a[0:tiles] + a[tiles : 2 * tiles] for a in acc]

    def own_step(i, e, source):
        for v, taken in enumerate(own_sweep(source)):
            state[e, v, own_x : own_x + tiles] = bias[i, v, own : own + tiles] - taken

    def bias_rows(i, first):
        return [bias[i, v, first : first + ROWS] for v in range(NVAR)]

    def into_work(first, values):
        for v in range(NVAR):
            work[v, first + half : first + half + ROWS] = values[v]

    def last_steps(i, e):
        into_work(half, sweep(work, half, bias_rows(i, half)))
        own_step(i, e, work)

    def two_steps(i, e):
        into_work(half, sweep(state.at[e], half, bias_rows(i, half)))
        own_step(i, e + 1, work)

    def three_steps(i, e):
        outer = [sweep(state.at[e], f, bias_rows(i, f)) for f in (0, ROWS)]
        into_work(0, outer[0])
        into_work(ROWS, outer[1])
        last_steps(i, e + 1)

    def couple(i, which):
        by_node = dot_right(perm, struct_all[i], NT)
        parts = jnp.concatenate([p.astype(jnp.float32) for p in split(by_node)], axis=0).astype(
            jnp.bfloat16
        )
        for b in which:
            picked = dot(parts, block_table[b], NN)
            picked = picked[0:width] + picked[width : 2 * width]
            moved = []
            for j in range(3):
                masked = picked[j * NPB : (j + 1) * NPB] * node_mask[b]
                shifted = masked[:, 0:slots]
                for t in range(1, TMAP):
                    shifted = shifted + masked[:, t * slots : (t + 1) * slots]
                moved.append(jnp.sum(shifted, axis=0, keepdims=True))
            displaced = jnp.concatenate(moved, axis=0)
            rates = pack if b == 0 else pack_near.at[b - 1]
            coupled = rates[0:ROWS] * displaced[0:1]
            for j in range(1, 3):
                coupled = coupled + rates[j * ROWS : (j + 1) * ROWS] * displaced[j : j + 1]
            spread = dot_left(coupled, cell_table[b], NT)
            first = (own, 0, own + tiles)[b]
            for v, value in enumerate(to_rows(spread[0:NVAR], mix, NVAR)):
                bias[i, v, first : first + tiles] = base_bias[v, first : first + tiles] + value

    def all_start(source, landing, send, recv):
        for rf in reversed(range(fluid_n)):
            for rs in reversed(range(struct_n)):
                if rf + rs == 0:
                    continue
                peer_f, peer_s = peers_f[rf], peers_s[rs]
                pltpu.make_async_remote_copy(
                    src_ref=source(peer_s * fluid_n + peer_f),
                    dst_ref=landing,
                    send_sem=send,
                    recv_sem=recv,
                    device_id=(peer_f, peer_s),
                    device_id_type=MESH,
                ).start()

    def all_wait(every, send, recv):
        done = pltpu.make_async_remote_copy(
            src_ref=every,
            dst_ref=every,
            send_sem=send,
            recv_sem=recv,
            device_id=(peers_f[1], me_s),
            device_id_type=MESH,
        )
        done.wait_recv()
        done.wait_send()

    def shell_terms(i):
        for m in range(NB):
            for r in range(ROWS):
                column = columns_ref[m, base + r]
                rows_x[m * ROWS + r : m * ROWS + r + 1] = struct_all[i, pl.ds(column, 1)]
        if i == 0:
            for copy in local:
                copy.wait()
        entries = rows_x[...]
        parts = jnp.concatenate([p.astype(jnp.float32) for p in split(entries)], axis=0).astype(
            jnp.bfloat16
        )
        count = NB * ROWS
        acc = jnp.zeros((ROWS, FOLD), jnp.float32)
        for c in range(0, BLK * BLK, CHUNK):
            wide = dot(parts, expand[:, c : c + CHUNK], NN)
            wide = wide[0:count] + wide[count:]
            for m in range(NB):
                product = wide[m * ROWS : (m + 1) * ROWS] * blocks[m, :, c : c + CHUNK]
                for g in range(0, CHUNK, FOLD):
                    acc = acc + product[:, g : g + FOLD]
        known[...] = right_struct[pl.ds(pl.multiple_of(base, ROWS), ROWS)] - dot_left(acc, fold, NN)

    def send_forces(i, e):
        for v in range(NVAR):
            mix[v * tiles : (v + 1) * tiles] = state[e, v, own_x : own_x + tiles]
        last = jnp.concatenate(
            [mix[pl.ds(a, NVAR, stride=tiles)] for a in range(tiles)], axis=1
        )
        at_surface = dot_left(pad_rows(last), cell_table[0], NN)
        sens = jnp.zeros((3, slots), jnp.float32)
        for v in range(NVAR):
            sens = sens + disp_ref[v] * at_surface[v : v + 1]
        sens = sens * live
        scaled = []
        for j in range(3):
            row = sens[j : j + 1]
            scaled.append(node_mask[0] * jnp.concatenate([row] * TMAP, axis=1))
        values = jnp.concatenate(scaled, axis=0)
        both = jnp.concatenate([p.astype(jnp.float32) for p in split(values)], axis=0)
        forces_out[i, :, 0 : 2 * width] = dot(block_table[0], both.astype(jnp.bfloat16), NT)
        all_start(
            lambda p: forces_out.at[i, pl.ds(pl.multiple_of(p * piece, piece), piece)],
            forces_land.at[i, me],
            force_send.at[i],
            force_recv.at[i],
        )
        forces_land[i, me] = forces_out[i, pl.ds(pl.multiple_of(own_row, piece), piece)]
        return last

    def solve(i):
        all_wait(forces_land.at[i, 0 : total - 1], force_send.at[i], force_recv.at[i])
        pieces = [forces_land[i, q] for q in range(total)]
        while len(pieces) > 1:
            pieces = [sum(pieces[q : q + 2][1:], pieces[q]) for q in range(0, len(pieces), 2)]
        mine = jnp.concatenate(pieces * (ROWS // piece), axis=0)
        spread = dot_left(mine[:, 0 : 2 * width], perm_twice, NN)
        load = known[pl.ds(pl.multiple_of(my_row - base, piece), piece)] + spread[0:piece]
        high, low = [p.astype(jnp.float32) for p in split(load)]
        parts = jnp.concatenate(
            [
                jnp.concatenate([high, high], axis=1),
                jnp.concatenate([low, jnp.zeros_like(low)], axis=1),
            ],
            axis=0,
        ).astype(jnp.bfloat16)
        for r in range(piece):
            out = dot(parts, mats[r], NT)
            result[i, r : r + 1, 0:BLK] = out[r : r + 1] + out[piece + r : piece + r + 1]

    def matrices():
        for p in range(BLK):
            flat[p * ROWS : (p + 1) * ROWS] = jnp.concatenate(
                [inverse[:, p * BLK : (p + 1) * BLK], jnp.zeros((ROWS, LANE - BLK), jnp.float32)],
                axis=1,
            )
        for g in range(ROWS // piece):
            @pl.when(my_row - base == g * piece)
            def _():
                for r in range(piece):
                    high, low = split(flat[pl.ds(g * piece + r, BLK, stride=ROWS)])
                    mats[r, :, 0:LANE] = high
                    mats[r, :, LANE : 2 * LANE] = low

    swap_wait(*state_swap(0, False))
    early = own_sweep(state.at[0])
    struct_all[0, pl.ds(pl.multiple_of(me_s * shard_rows, shard_rows), shard_rows)] = start_struct[...]
    for r in range(1, struct_n):
        start_copy(r, peers_s[r]).wait()
    couple(0, (0,))
    for v in range(NVAR):
        state[1, v, own_x : own_x + tiles] = bias[0, v, own : own + tiles] - early[v]
    swap_start(*state_swap(1, False))
    swap_start(*row_swap(bias.at[0], 2))
    swap_start(*fold_swap(*near_next))
    shell_terms(0)
    matrices()
    swap_wait(*state_swap(1, False))
    own_step(0, 2, state.at[1])
    swap_start(*state_swap(2, False))
    swap_start(*fold_swap(*near_rest))
    swap_start(*pack_swap(4))
    swap_start(*row_swap(base_bias, 5))
    swap_wait(*fold_swap(*near_first))
    swap_wait(*fold_swap(*near_next))
    swap_wait(*fold_swap(*near_rest))
    swap_wait(*row_swap(code, 1))
    swap_wait(*row_swap(bias.at[0], 2))
    swap_wait(*state_swap(2, False))
    two_steps(0, 2)
    swap_start(*state_swap(3, False))
    swap_start(*fold_swap(*far_first))
    swap_wait(*state_swap(3, False))
    two_steps(0, 3)
    swap_start(*state_swap(4, True))
    send_forces(0, 4)
    swap_start(*fold_swap(*far_rest))

    swap_wait(*pack_swap(4))
    swap_wait(*row_swap(base_bias, 5))
    for b in (1, 2):
        near_pack = pack_near.at[b - 1]
        tables(
            b,
            lambda t: near_pack[ROWS + NVAR + t : ROWS + NVAR + t + 1].astype(jnp.int32),
            lambda t: near_pack[NVAR + t : NVAR + t + 1],
            near_pack[2 * ROWS + NVAR : 2 * ROWS + NVAR + 1].astype(jnp.int32),
        )
    solve(0)
    landing = struct_all.at[1, pl.ds(pl.multiple_of(own_row, piece), piece)]
    all_start(lambda p: result.at[0], landing, gather_send, gather_recv)
    struct_all[1, pl.ds(pl.multiple_of(own_row, piece), piece)] = result[0]
    swap_wait(*fold_swap(*far_first))
    swap_wait(*fold_swap(*far_rest))
    swap_wait(*state_swap(4, True))
    for f in (0, ROWS):
        outer = sweep(state.at[4], f, [jnp.zeros((ROWS, LANE), jnp.float32)] * NVAR)
        for v in range(NVAR):
            partial[v, f : f + ROWS] = outer[v]
    all_wait(struct_all.at[1, 0 : shell_total - piece], gather_send, gather_recv)

    couple(1, (0, 1, 2))
    for f in (0, ROWS):
        into_work(f, [partial[v, f : f + ROWS] + bias[1, v, f : f + ROWS] for v in range(NVAR)])
    last_steps(1, 5)
    swap_start(*state_swap(5, True))
    shell_terms(1)
    swap_wait(*state_swap(5, True))
    three_steps(1, 5)
    last = send_forces(1, 6)
    fluid_ref[...] = last
    solve(1)

    def final_copy(r, landing):
        return pltpu.make_async_remote_copy(
            src_ref=result.at[1],
            dst_ref=final_land.at[landing],
            send_sem=final_send.at[r],
            recv_sem=final_recv.at[landing],
            device_id=(peers_f[r], me_s),
            device_id_type=MESH,
        )

    for r in range(1, fluid_n):
        final_copy(r, me_f).start()
    final_land[me_f] = result[1]
    for r in range(1, fluid_n):
        final_copy(r, peers_f[r]).wait()
    for f in range(fluid_n):
        struct_ref[f * piece : (f + 1) * piece] = final_land[f]


def finish(fluid_in, struct_in, fluid_ref, struct_ref):
    fluid_ref[...] = fluid_in[...]
    per = FOLD // BLK
    groups = struct_in.shape[0] // per
    wide = jnp.concatenate(
        [struct_in[pl.ds(q, groups, stride=per)][:, 0:BLK] for q in range(per)], axis=1
    )
    for q in range(FOLD // LANE):
        struct_ref[pl.ds(q, groups, stride=FOLD // LANE)] = wide[:, q * LANE : (q + 1) * LANE]


def body(
    fluid_n,
    struct_n,
    fluid_adjoint,
    fluid_rhs,
    diag_inverse,
    face_blocks,
    face_index,
    surface_cell,
    surface_count,
    transfer_node,
    transfer_weight,
    load_sens,
    disp_sens,
    struct_adjoint,
    struct_rhs,
    shell_blocks,
    shell_inverse,
    shell_columns,
):
    cells = fluid_adjoint.shape[1]
    slots = surface_cell.shape[0]
    block_rows = struct_adjoint.shape[0] // BLK
    shell_total = block_rows * struct_n
    piece = block_rows // fluid_n
    total = fluid_n * struct_n
    tiles = cells // LANE
    vmem = pl.BlockSpec(memory_space=pltpu.VMEM)
    far = pl.BlockSpec(memory_space=pl.ANY)
    f32, bf16 = jnp.float32, jnp.bfloat16
    dma = pltpu.SemaphoreType.DMA

    fluid_out, struct_out = pl.pallas_call(
        functools.partial(kernel, fluid_n, struct_n, piece),
        out_shape=(
            jax.ShapeDtypeStruct((NVAR, cells), f32),
            jax.ShapeDtypeStruct((block_rows, LANE), f32),
        ),
        in_specs=[far] * 6 + [vmem] + [far] * 9,
        out_specs=(vmem, vmem),
        scratch_shapes=[
            pltpu.VMEM((7, NVAR, 3 * ROWS, LANE), f32),
            pltpu.VMEM((NVAR, 3 * ROWS, LANE), f32),
            pltpu.VMEM((FACES * NVAR * NVAR, 2 * ROWS, LANE), f32),
            pltpu.VMEM((FACES, 2 * ROWS, LANE), jnp.int32),
            pltpu.VMEM((FACES // 2 * NVAR * NVAR, ROWS, LANE), f32),
            pltpu.VMEM((FACES // 2, ROWS, LANE), jnp.int32),
            pltpu.VMEM((NVAR, 2 * ROWS, LANE), f32),
            pltpu.VMEM((ITERS, NVAR, 2 * ROWS, LANE), f32),
            pltpu.VMEM((NVAR, 2 * ROWS, LANE), f32),
            pltpu.VMEM((tiles * ROWS, LANE), f32),
            pltpu.VMEM((tiles * ROWS, LANE), jnp.int32),
            pltpu.VMEM((NVAR * NVAR * tiles * ROWS, LANE), f32),
            pltpu.VMEM((NVAR * ROWS, cells), f32),
            pltpu.VMEM((3 * ROWS, slots), f32),
            pltpu.VMEM((2, 3 * ROWS, slots), f32),
            pltpu.VMEM((3, cells, slots), bf16),
            pltpu.VMEM((3, shell_total, TMAP * slots), bf16),
            pltpu.VMEM((3, NPB, TMAP * slots), f32),
            pltpu.VMEM((NB, ROWS, BLK * BLK), f32),
            pltpu.VMEM((ROWS, BLK * BLK), f32),
            pltpu.VMEM((LANE, BLK * BLK), bf16),
            pltpu.VMEM((block_rows, LANE), f32),
            pltpu.VMEM((block_rows, LANE), f32),
            pltpu.VMEM((ITERS, shell_total, LANE), f32),
            pltpu.VMEM((NB * ROWS, LANE), f32),
            pltpu.VMEM((ROWS, LANE), f32),
            pltpu.VMEM((BLK * ROWS, LANE), f32),
            pltpu.VMEM((piece, BLK, 2 * LANE), bf16),
            pltpu.VMEM((ITERS, shell_total, LANE), f32),
            pltpu.VMEM((ITERS, total, piece, LANE), f32),
            pltpu.VMEM((ITERS, piece, LANE), f32),
            pltpu.VMEM((fluid_n, piece, LANE), f32),
            dma((6, 4)),
            dma((6, 4)),
            dma((9, 2)),
            dma((9, 2)),
            dma((struct_n,)),
            dma((struct_n,)),
            dma((ITERS,)),
            dma((ITERS,)),
            dma,
            dma,
            dma((fluid_n,)),
            dma((fluid_n,)),
            dma((NB + 1,)),
            dma((13,)),
            pltpu.VMEM((NVAR, cells), f32),
            pltpu.VMEM((NVAR, cells), f32),
            pltpu.VMEM((NVAR, NVAR, cells), f32),
            pltpu.VMEM((NVAR, NVAR, FACES, cells), f32),
            pltpu.VMEM((FACES, cells), jnp.int32),
            pltpu.VMEM((1, slots), jnp.int32),
            pltpu.VMEM((TMAP, slots), jnp.int32),
            pltpu.VMEM((TMAP, slots), f32),
            pltpu.VMEM((NVAR, 3, slots), f32),
            pltpu.VMEM((NVAR, 3, slots), f32),
            pltpu.VMEM((block_rows * BLK // LANE, LANE), f32),
            pltpu.VMEM((block_rows * BLK // LANE, LANE), f32),
            pltpu.SMEM((NB, block_rows), jnp.int32),
        ],
        compiler_params=pltpu.CompilerParams(collective_id=0, has_side_effects=True),
    )(
        fluid_adjoint,
        fluid_rhs,
        diag_inverse,
        jnp.transpose(face_blocks, (1, 2, 0, 3)),
        face_index,
        surface_cell.reshape(1, slots),
        surface_count.reshape(1, 1),
        transfer_node,
        transfer_weight,
        jnp.transpose(load_sens, (1, 0, 2)),
        disp_sens,
        struct_adjoint.reshape(-1, LANE),
        struct_rhs.reshape(-1, LANE),
        shell_blocks,
        shell_inverse,
        shell_columns,
    )
    fluid_out, struct_out = pl.pallas_call(
        finish,
        out_shape=(
            jax.ShapeDtypeStruct((NVAR, cells), f32),
            jax.ShapeDtypeStruct((block_rows * BLK // LANE, LANE), f32),
        ),
        in_specs=[vmem, vmem],
        out_specs=(vmem, vmem),
    )(fluid_out, struct_out)
    return fluid_out, struct_out.reshape(-1)


def solution(mesh):
    placed = (
        P(None, ("fluid", "struct")),
        P(None, ("fluid", "struct")),
        P(None, None, ("fluid", "struct")),
        P(None, None, None, ("fluid", "struct")),
        P(None, ("fluid", "struct")),
        P(("fluid", "struct")),
        P(("fluid", "struct")),
        P(None, ("fluid", "struct")),
        P(None, ("fluid", "struct")),
        P(None, None, ("fluid", "struct")),
        P(None, None, ("fluid", "struct")),
        P("struct"),
        P("struct"),
        P(None, "struct", None),
        P("struct", None),
        P(None, "struct"),
    )
    return jax.shard_map(
        functools.partial(body, mesh.shape["fluid"], mesh.shape["struct"]),
        mesh=mesh,
        in_specs=placed,
        out_specs=(P(None, ("fluid", "struct")), P("struct")),
        check_vma=False,
    )
```

```python
import functools

import jax
import jax.numpy as jnp
from jax import lax
from jax.experimental import pallas as pl
from jax.experimental.pallas import tpu as pltpu
from jax.sharding import PartitionSpec as P

NVAR = 5
FACES = 6
TMAP = 3
DOF = 6
BLK = 96
NB = 4
SWEEPS = 6
ITERS = 2
NPB = BLK // DOF
LANE = 128
ROWS = 8
FOLD = 384
CHUNK = 768
NEAR = (2, 5)
FAR = 3
MESH = pl.DeviceIdType.MESH
NN = (((1,), (0,)), ((), ()))
NT = (((1,), (1,)), ((), ()))


def split(value):
    high = value.astype(jnp.bfloat16)
    return high, (value - high.astype(jnp.float32)).astype(jnp.bfloat16)


def dot(left, right, dims):
    return lax.dot_general(left, right, dims, preferred_element_type=jnp.float32)


def dot_left(value, table, dims):
    rows = value.shape[0]
    stacked = jnp.concatenate([p.astype(jnp.float32) for p in split(value)], axis=0)
    out = dot(stacked.astype(jnp.bfloat16), table, dims)
    return out[0:rows] + out[rows : 2 * rows]


def dot_right(table, value, dims):
    high, low = split(value)
    return dot(table, high, dims) + dot(table, low, dims)


def iota(shape, axis):
    return lax.broadcasted_iota(jnp.int32, shape, axis)


def pad_rows(value, rows=ROWS):
    return jnp.concatenate(
        [value, jnp.zeros((rows - value.shape[0], value.shape[1]), value.dtype)], axis=0
    )


def by_block(flat, out):
    groups = flat.shape[0] * LANE // FOLD
    wide = jnp.concatenate(
        [flat[pl.ds(a, groups, stride=FOLD // LANE)] for a in range(FOLD // LANE)], axis=1
    )
    for q in range(FOLD // BLK):
        part = wide[:, q * BLK : (q + 1) * BLK]
        full = jnp.concatenate([part, jnp.zeros((groups, LANE - BLK), jnp.float32)], axis=1)
        out[pl.ds(q, groups, stride=FOLD // BLK)] = full


def kernel(
    fluid_n,
    struct_n,
    piece,
    adj_far,
    rhs_far,
    diag_far,
    face_far,
    index_far,
    cell_far,
    count_ref,
    node_far,
    weight_far,
    load_far,
    disp_far,
    sadj_far,
    srhs_far,
    blocks_ref,
    inverse_ref,
    columns_far,
    fluid_ref,
    struct_ref,
    state,
    work,
    folded,
    code,
    pair_fold,
    pair_code,
    base_bias,
    bias,
    partial,
    mix,
    mix_int,
    fold_mix,
    diag_mix,
    pack,
    pack_near,
    cell_table,
    slot_map,
    block_table,
    node_mask,
    blocks,
    inverse,
    expand,
    start_struct,
    right_struct,
    struct_all,
    rows_x,
    known,
    flat,
    mats,
    forces_out,
    forces_land,
    result,
    final_land,
    state_send,
    state_recv,
    once_send,
    once_recv,
    start_send,
    start_recv,
    force_send,
    force_recv,
    gather_send,
    gather_recv,
    final_send,
    final_recv,
    local_sem,
    input_sem,
    adj_ref,
    rhs_ref,
    diag_ref,
    face_ref,
    index_ref,
    cell_ref,
    node_ref,
    weight_ref,
    load_ref,
    disp_ref,
    sadj_ref,
    srhs_ref,
    columns_ref,
):
    me_f = lax.axis_index("fluid")
    me_s = lax.axis_index("struct")
    me = me_f * struct_n + me_s
    total = fluid_n * struct_n
    cells = adj_ref.shape[1]
    tiles = cells // LANE
    half = tiles // 2
    slots = cell_ref.shape[1]
    shell_total = struct_all.shape[1]
    shard_rows = start_struct.shape[0]
    my_row = me_f * piece
    base = (my_row // ROWS) * ROWS
    own_row = me_s * shard_rows + my_row
    own_x = 3 * half
    own = tiles

    def dev(index):
        return (index // struct_n, index % struct_n)

    peers_f = [(me_f + r) % fluid_n for r in range(fluid_n)]
    peers_s = [(me_s + r) % struct_n for r in range(struct_n)]
    barrier = pltpu.get_barrier_semaphore()
    for rf in reversed(range(fluid_n)):
        for rs in reversed(range(struct_n)):
            if rf + rs:
                pl.semaphore_signal(
                    barrier, inc=1, device_id=(peers_f[rf], peers_s[rs]), device_id_type=MESH
                )

    inputs = []
    for n, (source, landing) in enumerate(
        (
            (sadj_far, sadj_ref),
            (adj_far, adj_ref),
            (srhs_far, srhs_ref),
            (diag_far, diag_ref),
            (face_far, face_ref),
            (index_far, index_ref),
            (cell_far, cell_ref),
            (node_far, node_ref),
            (weight_far, weight_ref),
            (load_far, load_ref),
            (rhs_far, rhs_ref),
            (disp_far, disp_ref),
            (columns_far, columns_ref),
        )
    ):
        inputs.append(pltpu.make_async_copy(source, landing, input_sem.at[n]))
        inputs[n].start()
    local = []
    for m in range(NB):
        local.append(
            pltpu.make_async_copy(
                blocks_ref.at[m, pl.ds(pl.multiple_of(base, ROWS), ROWS)],
                blocks.at[m],
                local_sem.at[m],
            )
        )
    local.append(
        pltpu.make_async_copy(
            inverse_ref.at[pl.ds(pl.multiple_of(base, ROWS), ROWS)], inverse, local_sem.at[NB]
        )
    )
    for copy in local:
        copy.start()

    shifts = (-1, 1, -2, 2)
    sends = (me > 0, me < total - 1, me > 1, me < total - 2)
    takes = (me < total - 1, me > 0, me < total - 2, me > 1)

    def swap_start(copies, send, recv):
        for d, (source, landing) in enumerate(copies):
            @pl.when(sends[d])
            def _():
                pltpu.make_async_remote_copy(
                    src_ref=source,
                    dst_ref=landing,
                    send_sem=send.at[d],
                    recv_sem=recv.at[d],
                    device_id=dev(me + shifts[d]),
                    device_id_type=MESH,
                ).start()

    def swap_wait(copies, send, recv):
        for d, (source, landing) in enumerate(copies):
            copy = pltpu.make_async_remote_copy(
                src_ref=source,
                dst_ref=landing,
                send_sem=send.at[d],
                recv_sem=recv.at[d],
                device_id=dev(me + shifts[d]),
                device_id_type=MESH,
            )

            @pl.when(takes[d])
            def _():
                copy.wait_recv()

            @pl.when(sends[d])
            def _():
                copy.wait_send()

    def rows(ref, first, count):
        return ref.at[:, first : first + count]

    def state_swap(e, wide):
        now = state.at[e]
        copies = [
            (rows(now, own_x, tiles), rows(now, own_x + tiles, tiles)),
            (rows(now, own_x, tiles), rows(now, own_x - tiles, tiles)),
        ]
        if wide:
            copies += [
                (rows(now, own_x, half), rows(now, own_x + 2 * tiles, half)),
                (rows(now, own_x + half, half), rows(now, 0, half)),
            ]
        return copies, state_send.at[e], state_recv.at[e]

    def row_swap(ref, n):
        copies = [
            (rows(ref, own, tiles), rows(ref, own + tiles, tiles)),
            (rows(ref, own, tiles), rows(ref, 0, tiles)),
        ]
        return copies, once_send.at[n], once_recv.at[n]

    def fold_swap(n, first_face, faces, far):
        some = folded.at[first_face * NVAR * NVAR : (first_face + faces) * NVAR * NVAR]
        low, high = rows(some, own, half), rows(some, own + half, half)
        if far:
            copies = [(high, rows(some, own + tiles + half, half)), (low, rows(some, 0, half))]
        else:
            copies = [(low, rows(some, own + tiles, half)), (high, rows(some, half, half))]
        return copies, once_send.at[n], once_recv.at[n]

    near_first = (0, 0, NEAR[0], False)
    near_next = (3, NEAR[0], NEAR[1] - NEAR[0], False)
    near_rest = (8, NEAR[1], FACES - NEAR[1], False)
    far_first = (6, 0, FAR, True)
    far_rest = (7, FAR, FACES - FAR, True)

    def pack_swap(n):
        copies = [(pack, pack_near.at[1]), (pack, pack_near.at[0])]
        return copies, once_send.at[n], once_recv.at[n]

    def span(a):
        return slice(a * LANE, (a + 1) * LANE)

    def to_rows(value, scratch, count):
        for a in range(tiles):
            scratch[a * ROWS : a * ROWS + count] = value[:, span(a)]
        return [scratch[pl.ds(v, tiles, stride=ROWS)] for v in range(count)]

    def clear(ref, first, count):
        ref[:, first : first + count] = jnp.zeros((ref.shape[0], count, LANE), ref.dtype)

    spare = state.shape[2]
    for e in range(state.shape[0]):
        clear(state.at[e], own_x + 2 * tiles + half, spare - own_x - 2 * tiles - half)

        @pl.when(me == 0)
        def _():
            clear(state.at[e], 0, own_x)

        @pl.when(me == 1)
        def _():
            clear(state.at[e], 0, half)

        @pl.when(me == total - 2)
        def _():
            clear(state.at[e], own_x + 2 * tiles, half)

        @pl.when(me == total - 1)
        def _():
            clear(state.at[e], own_x + tiles, tiles + half)

    @pl.when(me == 0)
    def _():
        for ref in (folded, code, base_bias, bias.at[0]):
            clear(ref, 0, tiles)
        pack_near[0] = jnp.zeros_like(pack)

    @pl.when(me == total - 1)
    def _():
        for ref in (folded, code, base_bias, bias.at[0]):
            clear(ref, own + tiles, tiles)
        pack_near[1] = jnp.zeros_like(pack)

    for copy in inputs[0:3]:
        copy.wait()
    for v, value in enumerate(to_rows(adj_ref[...], mix.at[0], NVAR)):
        state[0, v, own_x : own_x + tiles] = value
    by_block(sadj_ref, start_struct)
    by_block(srhs_ref, right_struct)
    forces_out[...] = jnp.zeros_like(forces_out)
    result[...] = jnp.zeros_like(result)

    pl.semaphore_wait(barrier, total - 1)

    def start_copy(r, landing):
        return pltpu.make_async_remote_copy(
            src_ref=start_struct,
            dst_ref=struct_all.at[0, pl.ds(pl.multiple_of(landing * shard_rows, shard_rows), shard_rows)],
            send_sem=start_send.at[r],
            recv_sem=start_recv.at[landing],
            device_id=(me_f, peers_s[r]),
            device_id_type=MESH,
        )

    for r in range(1, struct_n):
        start_copy(r, me_s).start()
    swap_start(*state_swap(0, False))

    for copy in inputs[3:]:
        copy.wait()

    def pair(k):
        return slice((k % 2) * tiles, (k % 2 + 1) * tiles)

    for a in range(tiles):
        for v in range(NVAR):
            scale = [
                jnp.broadcast_to(diag_ref[v, w : w + 1, span(a)], (FACES, LANE)) for w in range(NVAR)
            ]
            for u in range(NVAR):
                out = scale[0] * face_ref[u, 0, :, span(a)]
                for w in range(1, NVAR):
                    out = out + scale[w] * face_ref[u, w, :, span(a)]
                at = ((u * NVAR + v) * tiles + a) * ROWS
                fold_mix[at : at + FACES] = out
    for k in range(FACES):
        for u in range(NVAR):
            for v in range(NVAR):
                at = (u * NVAR + v) * tiles * ROWS + k
                value = fold_mix[pl.ds(at, tiles, stride=ROWS)]
                folded[(k * NVAR + u) * NVAR + v, own : own + tiles] = value
                pair_fold[((k // 2) * NVAR + u) * NVAR + v, pair(k)] = value
        if k + 1 == NEAR[0]:
            swap_start(*fold_swap(*near_first))
    for k, value in enumerate(to_rows(index_ref[...], mix_int, FACES)):
        value = value - LANE * iota((tiles, LANE), 0)
        code[k, own : own + tiles] = value
        pair_code[k // 2, pair(k)] = value
    swap_start(*row_swap(code, 1))

    def tables(b, node_of, weight_of, cell_of):
        cell_table[...] = jnp.where(iota((cells, slots), 0) == cell_of, 1.0, 0.0).astype(jnp.bfloat16)
        ids = (iota((ROWS, slots), 1) + 1).astype(jnp.float32)
        slot_map[b] = dot_left(ids, cell_table[...], NT).astype(jnp.int32)
        for t in range(TMAP):
            node = node_of(t)
            block_of = lax.shift_right_logical(node, NPB.bit_length() - 1)
            inside = node & (NPB - 1)
            block_table[b, :, t * slots : (t + 1) * slots] = jnp.where(
                iota((shell_total, slots), 0) == block_of, 1.0, 0.0
            ).astype(jnp.bfloat16)
            node_mask[b, :, t * slots : (t + 1) * slots] = jnp.where(
                iota((NPB, slots), 0) == inside, weight_of(t), 0.0
            )

    live = (iota((1, slots), 1) < count_ref[...]).astype(jnp.float32)
    tables(0, lambda t: node_ref[t : t + 1], lambda t: weight_ref[t : t + 1], cell_ref[...])

    for u in range(NVAR):
        for v in range(NVAR):
            diag_mix[u * ROWS + v : u * ROWS + v + 1] = diag_ref[v, u : u + 1]
    at_slots = dot_left(diag_mix[...], cell_table[...], NN)
    for j in range(3):
        out = at_slots[0:NVAR] * load_ref[0, j : j + 1]
        for u in range(1, NVAR):
            out = out + at_slots[u * ROWS : u * ROWS + NVAR] * load_ref[u, j : j + 1]
        pack[j * ROWS : j * ROWS + NVAR] = out * live
    pack[NVAR : NVAR + TMAP] = weight_ref[...]
    pack[ROWS + NVAR : ROWS + NVAR + TMAP] = node_ref[...].astype(jnp.float32)
    pack[2 * ROWS + NVAR : 3 * ROWS] = jnp.concatenate(
        [cell_ref[...].astype(jnp.float32)] * (ROWS - NVAR), axis=0
    )

    for v in range(NVAR):
        mixed = jnp.sum(diag_ref[v] * rhs_ref[...], axis=0, keepdims=True)
        for a in range(tiles):
            base_bias[v, own + a : own + a + 1] = mixed[:, span(a)]

    width = 3 * NPB
    out_row = iota((width, LANE), 0)
    perm = jnp.where(
        iota((width, LANE), 1)
        == (out_row & (NPB - 1)) * DOF + lax.shift_right_logical(out_row, NPB.bit_length() - 1),
        1.0,
        0.0,
    ).astype(jnp.bfloat16)
    perm_twice = jnp.concatenate([perm, perm], axis=0)
    behind = iota((FOLD, LANE), 0) - iota((FOLD, LANE), 1)
    near = (behind == 0) | (behind == BLK) | (behind == 2 * BLK) | (behind == 3 * BLK)
    fold = jnp.where(near & (iota((FOLD, LANE), 1) < BLK), 1.0, 0.0).astype(jnp.bfloat16)

    def sweep(source, first, start):
        acc = list(start)
        for k in range(FACES):
            place = code[k, first : first + ROWS]
            lane = place & (LANE - 1)
            tile = lax.shift_right_logical(place, LANE.bit_length() - 1)
            picks = [tile == o for o in range(tiles + 1)]
            for u in range(NVAR):
                beside = None
                for o in range(tiles + 1):
                    found = jnp.take_along_axis(
                        source[u, first + o : first + o + ROWS], lane, axis=1, mode="promise_in_bounds"
                    )
                    beside = found if beside is None else jnp.where(picks[o], found, beside)
                for v in range(NVAR):
                    at = (k * NVAR + u) * NVAR + v
                    acc[v] = acc[v] - folded[at, first : first + ROWS] * beside
        return acc

    def own_sweep(source):
        acc = [None] * NVAR
        beside_rows = {}
        for u in range(NVAR):
            for o in range(tiles + 1):
                first = own_x - half + o
                once = source[u, first : first + tiles]
                beside_rows[u, o] = jnp.concatenate([once, once], axis=0)
        for k in range(FACES // 2):
            place = pair_code[k]
            lane = place & (LANE - 1)
            tile = lax.shift_right_logical(place, LANE.bit_length() - 1)
            picks = [tile == o for o in range(tiles + 1)]
            for u in range(NVAR):
                beside = None
                for o in range(tiles + 1):
                    found = jnp.take_along_axis(
                        beside_rows[u, o], lane, axis=1, mode="promise_in_bounds"
                    )
                    beside = found if beside is None else jnp.where(picks[o], found, beside)
                for v in range(NVAR):
                    term = pair_fold[(k * NVAR + u) * NVAR + v] * beside
                    acc[v] = term if acc[v] is None else acc[v] + term
        return [a[0:tiles] + a[tiles : 2 * tiles] for a in acc]

    def own_step(i, e, source):
        for v, taken in enumerate(own_sweep(source)):
            state[e, v, own_x : own_x + tiles] = bias[i, v, own : own + tiles] - taken

    def bias_rows(i, first):
        return [bias[i, v, first : first + ROWS] for v in range(NVAR)]

    def into_work(first, values):
        for v in range(NVAR):
            work[v, first + half : first + half + ROWS] = values[v]

    def last_steps(i, e):
        into_work(half, sweep(work, half, bias_rows(i, half)))
        own_step(i, e, work)

    def two_steps(i, e):
        into_work(half, sweep(state.at[e], half, bias_rows(i, half)))
        own_step(i, e + 1, work)

    def three_steps(i, e):
        outer = [sweep(state.at[e], f, bias_rows(i, f)) for f in (0, ROWS)]
        into_work(0, outer[0])
        into_work(ROWS, outer[1])
        last_steps(i, e + 1)

    def gather_rows(sources, place):
        lane = place & (LANE - 1)
        tile = lax.shift_right_logical(place, LANE.bit_length() - 1)
        out = None
        for c, source in enumerate(sources):
            found = jnp.take_along_axis(source, lane, axis=1, mode="promise_in_bounds")
            out = found if out is None else jnp.where(tile == c, found, out)
        return out

    def couple(i, which):
        by_node = dot(perm, jnp.concatenate(split(struct_all[i]), axis=0), NT)
        parts = jnp.concatenate(
            [by_node[:, 0:shell_total], by_node[:, shell_total : 2 * shell_total]], axis=0
        ).astype(jnp.bfloat16)
        for b in which:
            picked = dot(parts, block_table[b], NN)
            picked = picked[0:width] + picked[width : 2 * width]
            moved = []
            for j in range(3):
                masked = picked[j * NPB : (j + 1) * NPB] * node_mask[b]
                shifted = masked[:, 0:slots]
                for t in range(1, TMAP):
                    shifted = shifted + masked[:, t * slots : (t + 1) * slots]
                moved.append(jnp.sum(shifted, axis=0, keepdims=True))
            displaced = jnp.concatenate(moved, axis=0)
            rates = pack if b == 0 else pack_near.at[b - 1]
            coupled = rates[0:ROWS] * displaced[0:1]
            for j in range(1, 3):
                coupled = coupled + rates[j * ROWS : (j + 1) * ROWS] * displaced[j : j + 1]
            spread = []
            for a in range(tiles):
                place = slot_map[b, :, span(a)]
                found = gather_rows([coupled[:, span(c)] for c in range(slots // LANE)], place - 1)
                spread.append(jnp.where(place > 0, found, 0.0))
            first = (own, 0, own + tiles)[b]
            for v, value in enumerate(to_rows(jnp.concatenate(spread, axis=1)[0:NVAR], mix.at[b], NVAR)):
                bias[i, v, first : first + tiles] = base_bias[v, first : first + tiles] + value

    def all_start(source, landing, send, recv):
        for rf in reversed(range(fluid_n)):
            for rs in reversed(range(struct_n)):
                if rf + rs == 0:
                    continue
                peer_f, peer_s = peers_f[rf], peers_s[rs]
                pltpu.make_async_remote_copy(
                    src_ref=source(peer_s * fluid_n + peer_f),
                    dst_ref=landing,
                    send_sem=send,
                    recv_sem=recv,
                    device_id=(peer_f, peer_s),
                    device_id_type=MESH,
                ).start()

    def all_wait(every, send, recv):
        done = pltpu.make_async_remote_copy(
            src_ref=every,
            dst_ref=every,
            send_sem=send,
            recv_sem=recv,
            device_id=(peers_f[1], me_s),
            device_id_type=MESH,
        )
        done.wait_recv()
        done.wait_send()

    def shell_terms(i):
        for m in range(NB):
            for r in range(ROWS):
                column = columns_ref[m, base + r]
                rows_x[m * ROWS + r : m * ROWS + r + 1] = struct_all[i, pl.ds(column, 1)]
        if i == 0:
            for copy in local:
                copy.wait()
        entries = rows_x[...]
        parts = jnp.concatenate([p.astype(jnp.float32) for p in split(entries)], axis=0).astype(
            jnp.bfloat16
        )
        count = NB * ROWS
        acc = jnp.zeros((ROWS, FOLD), jnp.float32)
        for c in range(0, BLK * BLK, CHUNK):
            wide = dot(parts, expand[:, c : c + CHUNK], NN)
            wide = wide[0:count] + wide[count:]
            for m in range(NB):
                product = wide[m * ROWS : (m + 1) * ROWS] * blocks[m, :, c : c + CHUNK]
                for g in range(0, CHUNK, FOLD):
                    acc = acc + product[:, g : g + FOLD]
        known[...] = right_struct[pl.ds(pl.multiple_of(base, ROWS), ROWS)] - dot_left(acc, fold, NN)

    def send_forces(i, e):
        for v in range(NVAR):
            mix[0, v * tiles : (v + 1) * tiles] = state[e, v, own_x : own_x + tiles]
        parts = [pad_rows(mix[0, pl.ds(a, NVAR, stride=tiles)]) for a in range(tiles)]
        last = jnp.concatenate([p[0:NVAR] for p in parts], axis=1)
        place = jnp.broadcast_to(cell_ref[...], (ROWS, slots))
        at_surface = jnp.concatenate(
            [gather_rows(parts, place[:, span(c)]) for c in range(slots // LANE)], axis=1
        )
        sens = jnp.zeros((3, slots), jnp.float32)
        for v in range(NVAR):
            sens = sens + disp_ref[v] * at_surface[v : v + 1]
        sens = sens * live
        scaled = []
        for j in range(3):
            row = sens[j : j + 1]
            scaled.append(node_mask[0] * jnp.concatenate([row] * TMAP, axis=1))
        values = jnp.concatenate(scaled, axis=0)
        both = jnp.concatenate([p.astype(jnp.float32) for p in split(values)], axis=0)
        forces_out[i, :, 0 : 2 * width] = dot(block_table[0], both.astype(jnp.bfloat16), NT)
        all_start(
            lambda p: forces_out.at[i, pl.ds(pl.multiple_of(p * piece, piece), piece)],
            forces_land.at[i, me],
            force_send.at[i],
            force_recv.at[i],
        )
        forces_land[i, me] = forces_out[i, pl.ds(pl.multiple_of(own_row, piece), piece)]
        return last

    def solve(i):
        all_wait(forces_land.at[i, 0 : total - 1], force_send.at[i], force_recv.at[i])
        pieces = [forces_land[i, q] for q in range(total)]
        while len(pieces) > 1:
            pieces = [sum(pieces[q : q + 2][1:], pieces[q]) for q in range(0, len(pieces), 2)]
        mine = jnp.concatenate(pieces * (ROWS // piece), axis=0)
        spread = dot_left(mine[:, 0 : 2 * width], perm_twice, NN)
        load = known[pl.ds(pl.multiple_of(my_row - base, piece), piece)] + spread[0:piece]
        high, low = [p.astype(jnp.float32) for p in split(load)]
        parts = jnp.concatenate(
            [
                jnp.concatenate([high, high], axis=1),
                jnp.concatenate([low, jnp.zeros_like(low)], axis=1),
            ],
            axis=0,
        ).astype(jnp.bfloat16)
        for r in range(piece):
            out = dot(parts, mats[r], NT)
            result[i, r : r + 1, 0:BLK] = out[r : r + 1] + out[piece + r : piece + r + 1]

    def matrices():
        for p in range(BLK):
            flat[p * ROWS : (p + 1) * ROWS] = jnp.concatenate(
                [inverse[:, p * BLK : (p + 1) * BLK], jnp.zeros((ROWS, LANE - BLK), jnp.float32)],
                axis=1,
            )
        for g in range(ROWS // piece):
            @pl.when(my_row - base == g * piece)
            def _():
                for r in range(piece):
                    high, low = split(flat[pl.ds(g * piece + r, BLK, stride=ROWS)])
                    mats[r, :, 0:LANE] = high
                    mats[r, :, LANE : 2 * LANE] = low

    swap_wait(*state_swap(0, False))
    early = own_sweep(state.at[0])
    struct_all[0, pl.ds(pl.multiple_of(me_s * shard_rows, shard_rows), shard_rows)] = start_struct[...]
    for r in range(1, struct_n):
        start_copy(r, peers_s[r]).wait()
    couple(0, (0,))
    for v in range(NVAR):
        state[1, v, own_x : own_x + tiles] = bias[0, v, own : own + tiles] - early[v]
    swap_start(*state_swap(1, False))
    swap_start(*row_swap(bias.at[0], 2))
    swap_start(*fold_swap(*near_next))
    for c in range(0, BLK * BLK, CHUNK):
        offset = iota((LANE, CHUNK), 1) + c - BLK * iota((LANE, CHUNK), 0)
        expand[:, c : c + CHUNK] = jnp.where((offset >= 0) & (offset < BLK), 1.0, 0.0).astype(
            jnp.bfloat16
        )
    shell_terms(0)
    swap_wait(*state_swap(1, False))
    own_step(0, 2, state.at[1])
    swap_start(*state_swap(2, False))
    swap_start(*fold_swap(*near_rest))
    swap_start(*pack_swap(4))
    swap_start(*row_swap(base_bias, 5))
    matrices()
    swap_wait(*fold_swap(*near_first))
    swap_wait(*fold_swap(*near_next))
    swap_wait(*fold_swap(*near_rest))
    swap_wait(*row_swap(code, 1))
    swap_wait(*row_swap(bias.at[0], 2))
    swap_wait(*state_swap(2, False))
    two_steps(0, 2)
    swap_start(*state_swap(3, False))
    swap_start(*fold_swap(*far_first))
    swap_wait(*state_swap(3, False))
    two_steps(0, 3)
    swap_start(*state_swap(4, True))
    send_forces(0, 4)
    swap_start(*fold_swap(*far_rest))

    swap_wait(*pack_swap(4))
    swap_wait(*row_swap(base_bias, 5))
    for b in (1, 2):
        near_pack = pack_near.at[b - 1]
        tables(
            b,
            lambda t: near_pack[ROWS + NVAR + t : ROWS + NVAR + t + 1].astype(jnp.int32),
            lambda t: near_pack[NVAR + t : NVAR + t + 1],
            near_pack[2 * ROWS + NVAR : 2 * ROWS + NVAR + 1].astype(jnp.int32),
        )
    solve(0)
    landing = struct_all.at[1, pl.ds(pl.multiple_of(own_row, piece), piece)]
    all_start(lambda p: result.at[0], landing, gather_send, gather_recv)
    struct_all[1, pl.ds(pl.multiple_of(own_row, piece), piece)] = result[0]
    swap_wait(*fold_swap(*far_first))
    swap_wait(*fold_swap(*far_rest))
    swap_wait(*state_swap(4, True))
    for f in (0, ROWS):
        outer = sweep(state.at[4], f, [jnp.zeros((ROWS, LANE), jnp.float32)] * NVAR)
        for v in range(NVAR):
            partial[v, f : f + ROWS] = outer[v]
    all_wait(struct_all.at[1, 0 : shell_total - piece], gather_send, gather_recv)

    couple(1, (0, 1, 2))
    for f in (0, ROWS):
        into_work(f, [partial[v, f : f + ROWS] + bias[1, v, f : f + ROWS] for v in range(NVAR)])
    last_steps(1, 5)
    swap_start(*state_swap(5, True))
    shell_terms(1)
    swap_wait(*state_swap(5, True))
    three_steps(1, 5)
    last = send_forces(1, 6)
    fluid_ref[...] = last
    solve(1)

    def final_copy(r, landing):
        return pltpu.make_async_remote_copy(
            src_ref=result.at[1],
            dst_ref=final_land.at[landing],
            send_sem=final_send.at[r],
            recv_sem=final_recv.at[landing],
            device_id=(peers_f[r], me_s),
            device_id_type=MESH,
        )

    for r in range(1, fluid_n):
        final_copy(r, me_f).start()
    final_land[me_f] = result[1]
    for r in range(1, fluid_n):
        final_copy(r, peers_f[r]).wait()
    for f in range(fluid_n):
        struct_ref[f * piece : (f + 1) * piece] = final_land[f]


def finish(fluid_in, struct_in, fluid_ref, struct_ref):
    fluid_ref[...] = fluid_in[...]
    per = FOLD // BLK
    groups = struct_in.shape[0] // per
    wide = jnp.concatenate(
        [struct_in[pl.ds(q, groups, stride=per)][:, 0:BLK] for q in range(per)], axis=1
    )
    for q in range(FOLD // LANE):
        struct_ref[pl.ds(q, groups, stride=FOLD // LANE)] = wide[:, q * LANE : (q + 1) * LANE]


def body(
    fluid_n,
    struct_n,
    fluid_adjoint,
    fluid_rhs,
    diag_inverse,
    face_blocks,
    face_index,
    surface_cell,
    surface_count,
    transfer_node,
    transfer_weight,
    load_sens,
    disp_sens,
    struct_adjoint,
    struct_rhs,
    shell_blocks,
    shell_inverse,
    shell_columns,
):
    cells = fluid_adjoint.shape[1]
    slots = surface_cell.shape[0]
    block_rows = struct_adjoint.shape[0] // BLK
    shell_total = block_rows * struct_n
    piece = block_rows // fluid_n
    total = fluid_n * struct_n
    tiles = cells // LANE
    vmem = pl.BlockSpec(memory_space=pltpu.VMEM)
    far = pl.BlockSpec(memory_space=pl.ANY)
    f32, bf16 = jnp.float32, jnp.bfloat16
    dma = pltpu.SemaphoreType.DMA

    fluid_out, struct_out = pl.pallas_call(
        functools.partial(kernel, fluid_n, struct_n, piece),
        out_shape=(
            jax.ShapeDtypeStruct((NVAR, cells), f32),
            jax.ShapeDtypeStruct((block_rows, LANE), f32),
        ),
        in_specs=[far] * 6 + [vmem] + [far] * 9,
        out_specs=(vmem, vmem),
        scratch_shapes=[
            pltpu.VMEM((7, NVAR, 3 * ROWS, LANE), f32),
            pltpu.VMEM((NVAR, 3 * ROWS, LANE), f32),
            pltpu.VMEM((FACES * NVAR * NVAR, 2 * ROWS, LANE), f32),
            pltpu.VMEM((FACES, 2 * ROWS, LANE), jnp.int32),
            pltpu.VMEM((FACES // 2 * NVAR * NVAR, ROWS, LANE), f32),
            pltpu.VMEM((FACES // 2, ROWS, LANE), jnp.int32),
            pltpu.VMEM((NVAR, 2 * ROWS, LANE), f32),
            pltpu.VMEM((ITERS, NVAR, 2 * ROWS, LANE), f32),
            pltpu.VMEM((NVAR, 2 * ROWS, LANE), f32),
            pltpu.VMEM((3, tiles * ROWS, LANE), f32),
            pltpu.VMEM((tiles * ROWS, LANE), jnp.int32),
            pltpu.VMEM((NVAR * NVAR * tiles * ROWS, LANE), f32),
            pltpu.VMEM((NVAR * ROWS, cells), f32),
            pltpu.VMEM((3 * ROWS, slots), f32),
            pltpu.VMEM((2, 3 * ROWS, slots), f32),
            pltpu.VMEM((cells, slots), bf16),
            pltpu.VMEM((3, ROWS, cells), jnp.int32),
            pltpu.VMEM((3, shell_total, TMAP * slots), bf16),
            pltpu.VMEM((3, NPB, TMAP * slots), f32),
            pltpu.VMEM((NB, ROWS, BLK * BLK), f32),
            pltpu.VMEM((ROWS, BLK * BLK), f32),
            pltpu.VMEM((LANE, BLK * BLK), bf16),
            pltpu.VMEM((block_rows, LANE), f32),
            pltpu.VMEM((block_rows, LANE), f32),
            pltpu.VMEM((ITERS, shell_total, LANE), f32),
            pltpu.VMEM((NB * ROWS, LANE), f32),
            pltpu.VMEM((ROWS, LANE), f32),
            pltpu.VMEM((BLK * ROWS, LANE), f32),
            pltpu.VMEM((piece, BLK, 2 * LANE), bf16),
            pltpu.VMEM((ITERS, shell_total, LANE), f32),
            pltpu.VMEM((ITERS, total, piece, LANE), f32),
            pltpu.VMEM((ITERS, piece, LANE), f32),
            pltpu.VMEM((fluid_n, piece, LANE), f32),
            dma((6, 4)),
            dma((6, 4)),
            dma((9, 2)),
            dma((9, 2)),
            dma((struct_n,)),
            dma((struct_n,)),
            dma((ITERS,)),
            dma((ITERS,)),
            dma,
            dma,
            dma((fluid_n,)),
            dma((fluid_n,)),
            dma((NB + 1,)),
            dma((13,)),
            pltpu.VMEM((NVAR, cells), f32),
            pltpu.VMEM((NVAR, cells), f32),
            pltpu.VMEM((NVAR, NVAR, cells), f32),
            pltpu.VMEM((NVAR, NVAR, FACES, cells), f32),
            pltpu.VMEM((FACES, cells), jnp.int32),
            pltpu.VMEM((1, slots), jnp.int32),
            pltpu.VMEM((TMAP, slots), jnp.int32),
            pltpu.VMEM((TMAP, slots), f32),
            pltpu.VMEM((NVAR, 3, slots), f32),
            pltpu.VMEM((NVAR, 3, slots), f32),
            pltpu.VMEM((block_rows * BLK // LANE, LANE), f32),
            pltpu.VMEM((block_rows * BLK // LANE, LANE), f32),
            pltpu.SMEM((NB, block_rows), jnp.int32),
        ],
        compiler_params=pltpu.CompilerParams(collective_id=0, has_side_effects=True),
    )(
        fluid_adjoint,
        fluid_rhs,
        diag_inverse,
        jnp.transpose(face_blocks, (1, 2, 0, 3)),
        face_index,
        surface_cell.reshape(1, slots),
        surface_count.reshape(1, 1),
        transfer_node,
        transfer_weight,
        jnp.transpose(load_sens, (1, 0, 2)),
        disp_sens,
        struct_adjoint.reshape(-1, LANE),
        struct_rhs.reshape(-1, LANE),
        shell_blocks,
        shell_inverse,
        shell_columns,
    )
    fluid_out, struct_out = pl.pallas_call(
        finish,
        out_shape=(
            jax.ShapeDtypeStruct((NVAR, cells), f32),
            jax.ShapeDtypeStruct((block_rows * BLK // LANE, LANE), f32),
        ),
        in_specs=[vmem, vmem],
        out_specs=(vmem, vmem),
    )(fluid_out, struct_out)
    return fluid_out, struct_out.reshape(-1)


def solution(mesh):
    placed = (
        P(None, ("fluid", "struct")),
        P(None, ("fluid", "struct")),
        P(None, None, ("fluid", "struct")),
        P(None, None, None, ("fluid", "struct")),
        P(None, ("fluid", "struct")),
        P(("fluid", "struct")),
        P(("fluid", "struct")),
        P(None, ("fluid", "struct")),
        P(None, ("fluid", "struct")),
        P(None, None, ("fluid", "struct")),
        P(None, None, ("fluid", "struct")),
        P("struct"),
        P("struct"),
        P(None, "struct", None),
        P("struct", None),
        P(None, "struct"),
    )
    return jax.shard_map(
        functools.partial(body, mesh.shape["fluid"], mesh.shape["struct"]),
        mesh=mesh,
        in_specs=placed,
        out_specs=(P(None, ("fluid", "struct")), P("struct")),
        check_vma=False,
    )
```

```python
import functools

import jax
import jax.numpy as jnp
from jax import lax
from jax.experimental import pallas as pl
from jax.experimental.pallas import tpu as pltpu
from jax.sharding import PartitionSpec as P

NVAR = 5
FACES = 6
TMAP = 3
DOF = 6
BLK = 96
NB = 4
SWEEPS = 6
ITERS = 2
NPB = BLK // DOF
LANE = 128
ROWS = 8
FOLD = 384
CHUNK = 768
NEAR = (2, 5)
FAR = 3
MESH = pl.DeviceIdType.MESH
NN = (((1,), (0,)), ((), ()))
NT = (((1,), (1,)), ((), ()))


def split(value):
    high = value.astype(jnp.bfloat16)
    return high, (value - high.astype(jnp.float32)).astype(jnp.bfloat16)


def dot(left, right, dims):
    return lax.dot_general(left, right, dims, preferred_element_type=jnp.float32)


def dot_left(value, table, dims):
    rows = value.shape[0]
    stacked = jnp.concatenate([p.astype(jnp.float32) for p in split(value)], axis=0)
    out = dot(stacked.astype(jnp.bfloat16), table, dims)
    return out[0:rows] + out[rows : 2 * rows]


def dot_right(table, value, dims):
    high, low = split(value)
    return dot(table, high, dims) + dot(table, low, dims)


def iota(shape, axis):
    return lax.broadcasted_iota(jnp.int32, shape, axis)


def pad_rows(value, rows=ROWS):
    return jnp.concatenate(
        [value, jnp.zeros((rows - value.shape[0], value.shape[1]), value.dtype)], axis=0
    )


def by_block(flat, out):
    groups = flat.shape[0] * LANE // FOLD
    wide = jnp.concatenate(
        [flat[pl.ds(a, groups, stride=FOLD // LANE)] for a in range(FOLD // LANE)], axis=1
    )
    for q in range(FOLD // BLK):
        part = wide[:, q * BLK : (q + 1) * BLK]
        full = jnp.concatenate([part, jnp.zeros((groups, LANE - BLK), jnp.float32)], axis=1)
        out[pl.ds(q, groups, stride=FOLD // BLK)] = full


def kernel(
    fluid_n,
    struct_n,
    piece,
    adj_far,
    rhs_far,
    diag_far,
    face_far,
    index_far,
    cell_far,
    count_ref,
    node_far,
    weight_far,
    load_far,
    disp_far,
    sadj_far,
    srhs_far,
    blocks_ref,
    inverse_ref,
    columns_far,
    fluid_ref,
    struct_ref,
    state,
    work,
    folded,
    code,
    pair_fold,
    pair_code,
    base_bias,
    bias,
    partial,
    mix,
    mix_int,
    fold_mix,
    diag_mix,
    pack,
    pack_near,
    cell_table,
    slot_map,
    block_table,
    node_mask,
    blocks,
    inverse,
    expand,
    start_struct,
    right_struct,
    struct_all,
    rows_x,
    known,
    flat,
    mats,
    forces_out,
    forces_land,
    result,
    final_land,
    state_send,
    state_recv,
    once_send,
    once_recv,
    start_send,
    start_recv,
    force_send,
    force_recv,
    gather_send,
    gather_recv,
    final_send,
    final_recv,
    round_sem,
    local_sem,
    input_sem,
    adj_ref,
    rhs_ref,
    diag_ref,
    face_ref,
    index_ref,
    cell_ref,
    node_ref,
    weight_ref,
    load_ref,
    disp_ref,
    sadj_ref,
    srhs_ref,
    columns_ref,
):
    me_f = lax.axis_index("fluid")
    me_s = lax.axis_index("struct")
    me = me_f * struct_n + me_s
    total = fluid_n * struct_n
    cells = adj_ref.shape[1]
    tiles = cells // LANE
    half = tiles // 2
    slots = cell_ref.shape[1]
    shell_total = struct_all.shape[1]
    shard_rows = start_struct.shape[0]
    my_row = me_f * piece
    base = (my_row // ROWS) * ROWS
    own_row = me_s * shard_rows + my_row
    own_x = 3 * half
    own = tiles

    def dev(index):
        return (index // struct_n, index % struct_n)

    peers_f = [(me_f + r) % fluid_n for r in range(fluid_n)]
    peers_s = [(me_s + r) % struct_n for r in range(struct_n)]
    barrier = pltpu.get_barrier_semaphore()
    bits = [1 << d for d in range(fluid_n.bit_length() - 1)]
    partners = [(me_f + j - 2 * j * ((me_f // j) % 2), me_s) for j in bits]

    def greet(semaphore, device):
        pl.semaphore_signal(semaphore, inc=1, device_id=device, device_id_type=MESH)

    last_s = struct_n - 1

    @pl.when(me_s == last_s)
    def _():
        greet(barrier, (peers_f[1], 0))

    @pl.when(me_s == 0)
    def _():
        greet(barrier, (peers_f[fluid_n - 1], last_s))

    for r in range(1, struct_n):
        greet(barrier, (me_f, peers_s[r]))
    for partner in partners:
        greet(barrier, partner)
    ends = jnp.where(me_s == 0, 1, 0) + jnp.where(me_s == last_s, 1, 0)

    def round_start(n):
        for partner in partners:
            greet(round_sem.at[n], partner)

    def round_wait(n):
        pl.semaphore_wait(round_sem.at[n], len(partners))

    inputs = []
    for n, (source, landing) in enumerate(
        (
            (sadj_far, sadj_ref),
            (adj_far, adj_ref),
            (srhs_far, srhs_ref),
            (diag_far, diag_ref),
            (face_far, face_ref),
            (index_far, index_ref),
            (cell_far, cell_ref),
            (node_far, node_ref),
            (weight_far, weight_ref),
            (load_far, load_ref),
            (rhs_far, rhs_ref),
            (disp_far, disp_ref),
            (columns_far, columns_ref),
        )
    ):
        inputs.append(pltpu.make_async_copy(source, landing, input_sem.at[n]))
        inputs[n].start()
    local = []
    for m in range(NB):
        local.append(
            pltpu.make_async_copy(
                blocks_ref.at[m, pl.ds(pl.multiple_of(base, ROWS), ROWS)],
                blocks.at[m],
                local_sem.at[m],
            )
        )
    local.append(
        pltpu.make_async_copy(
            inverse_ref.at[pl.ds(pl.multiple_of(base, ROWS), ROWS)], inverse, local_sem.at[NB]
        )
    )
    for copy in local:
        copy.start()

    shifts = (-1, 1, -2, 2)
    sends = (me > 0, me < total - 1, me > 1, me < total - 2)
    takes = (me < total - 1, me > 0, me < total - 2, me > 1)

    def swap_start(copies, send, recv):
        for d, (source, landing) in enumerate(copies):
            @pl.when(sends[d])
            def _():
                pltpu.make_async_remote_copy(
                    src_ref=source,
                    dst_ref=landing,
                    send_sem=send.at[d],
                    recv_sem=recv.at[d],
                    device_id=dev(me + shifts[d]),
                    device_id_type=MESH,
                ).start()

    def swap_wait(copies, send, recv):
        for d, (source, landing) in enumerate(copies):
            copy = pltpu.make_async_remote_copy(
                src_ref=source,
                dst_ref=landing,
                send_sem=send.at[d],
                recv_sem=recv.at[d],
                device_id=dev(me + shifts[d]),
                device_id_type=MESH,
            )

            @pl.when(takes[d])
            def _():
                copy.wait_recv()

            @pl.when(sends[d])
            def _():
                copy.wait_send()

    def rows(ref, first, count):
        return ref.at[:, first : first + count]

    def state_swap(e, wide):
        now = state.at[e]
        copies = [
            (rows(now, own_x, tiles), rows(now, own_x + tiles, tiles)),
            (rows(now, own_x, tiles), rows(now, own_x - tiles, tiles)),
        ]
        if wide:
            copies += [
                (rows(now, own_x, half), rows(now, own_x + 2 * tiles, half)),
                (rows(now, own_x + half, half), rows(now, 0, half)),
            ]
        return copies, state_send.at[e], state_recv.at[e]

    def row_swap(ref, n):
        copies = [
            (rows(ref, own, tiles), rows(ref, own + tiles, tiles)),
            (rows(ref, own, tiles), rows(ref, 0, tiles)),
        ]
        return copies, once_send.at[n], once_recv.at[n]

    def fold_swap(n, first_face, faces, far):
        some = folded.at[first_face * NVAR * NVAR : (first_face + faces) * NVAR * NVAR]
        low, high = rows(some, own, half), rows(some, own + half, half)
        if far:
            copies = [(high, rows(some, own + tiles + half, half)), (low, rows(some, 0, half))]
        else:
            copies = [(low, rows(some, own + tiles, half)), (high, rows(some, half, half))]
        return copies, once_send.at[n], once_recv.at[n]

    near_first = (0, 0, NEAR[0], False)
    near_next = (3, NEAR[0], NEAR[1] - NEAR[0], False)
    near_rest = (8, NEAR[1], FACES - NEAR[1], False)
    far_first = (6, 0, FAR, True)
    far_rest = (7, FAR, FACES - FAR, True)

    def pack_swap(n):
        copies = [(pack, pack_near.at[1]), (pack, pack_near.at[0])]
        return copies, once_send.at[n], once_recv.at[n]

    def span(a):
        return slice(a * LANE, (a + 1) * LANE)

    def to_rows(value, scratch, count):
        for a in range(tiles):
            scratch[a * ROWS : a * ROWS + count] = value[:, span(a)]
        return [scratch[pl.ds(v, tiles, stride=ROWS)] for v in range(count)]

    def clear(ref, first, count):
        ref[:, first : first + count] = jnp.zeros((ref.shape[0], count, LANE), ref.dtype)

    for copy in inputs[0:3]:
        copy.wait()
    for v, value in enumerate(to_rows(adj_ref[...], mix.at[0], NVAR)):
        state[0, v, own_x : own_x + tiles] = value
    by_block(sadj_ref, start_struct)

    pl.semaphore_wait(barrier, struct_n - 1 + len(partners) + ends)
    round_start(0)

    def start_copy(r, landing):
        return pltpu.make_async_remote_copy(
            src_ref=start_struct,
            dst_ref=struct_all.at[0, pl.ds(pl.multiple_of(landing * shard_rows, shard_rows), shard_rows)],
            send_sem=start_send.at[r],
            recv_sem=start_recv.at[landing],
            device_id=(me_f, peers_s[r]),
            device_id_type=MESH,
        )

    for r in range(1, struct_n):
        start_copy(r, me_s).start()
    swap_start(*state_swap(0, False))
    spare = state.shape[2]
    for e in range(state.shape[0]):
        clear(state.at[e], own_x + 2 * tiles + half, spare - own_x - 2 * tiles - half)

        @pl.when(me == 0)
        def _():
            clear(state.at[e], 0, own_x)

        @pl.when(me == 1)
        def _():
            clear(state.at[e], 0, half)

        @pl.when(me == total - 2)
        def _():
            clear(state.at[e], own_x + 2 * tiles, half)

        @pl.when(me == total - 1)
        def _():
            clear(state.at[e], own_x + tiles, tiles + half)

    @pl.when(me == 0)
    def _():
        for ref in (folded, code, base_bias, bias.at[0]):
            clear(ref, 0, tiles)
        pack_near[0] = jnp.zeros_like(pack)

    @pl.when(me == total - 1)
    def _():
        for ref in (folded, code, base_bias, bias.at[0]):
            clear(ref, own + tiles, tiles)
        pack_near[1] = jnp.zeros_like(pack)

    by_block(srhs_ref, right_struct)
    forces_out[...] = jnp.zeros_like(forces_out)
    result[...] = jnp.zeros_like(result)

    for copy in inputs[3:]:
        copy.wait()

    def pair(k):
        return slice((k % 2) * tiles, (k % 2 + 1) * tiles)

    for a in range(tiles):
        for v in range(NVAR):
            scale = [
                jnp.broadcast_to(diag_ref[v, w : w + 1, span(a)], (FACES, LANE)) for w in range(NVAR)
            ]
            for u in range(NVAR):
                out = scale[0] * face_ref[u, 0, :, span(a)]
                for w in range(1, NVAR):
                    out = out + scale[w] * face_ref[u, w, :, span(a)]
                at = ((u * NVAR + v) * tiles + a) * ROWS
                fold_mix[at : at + FACES] = out
    for k in range(FACES):
        for u in range(NVAR):
            for v in range(NVAR):
                at = (u * NVAR + v) * tiles * ROWS + k
                value = fold_mix[pl.ds(at, tiles, stride=ROWS)]
                folded[(k * NVAR + u) * NVAR + v, own : own + tiles] = value
                pair_fold[((k // 2) * NVAR + u) * NVAR + v, pair(k)] = value
        if k + 1 == NEAR[0]:
            swap_start(*fold_swap(*near_first))
    for k, value in enumerate(to_rows(index_ref[...], mix_int, FACES)):
        value = value - LANE * iota((tiles, LANE), 0)
        code[k, own : own + tiles] = value
        pair_code[k // 2, pair(k)] = value
    swap_start(*row_swap(code, 1))

    def tables(b, node_of, weight_of, cell_of):
        cell_table[...] = jnp.where(iota((cells, slots), 0) == cell_of, 1.0, 0.0).astype(jnp.bfloat16)
        ids = (iota((ROWS, slots), 1) + 1).astype(jnp.float32)
        slot_map[b] = dot_left(ids, cell_table[...], NT).astype(jnp.int32)
        for t in range(TMAP):
            node = node_of(t)
            block_of = lax.shift_right_logical(node, NPB.bit_length() - 1)
            inside = node & (NPB - 1)
            block_table[b, :, t * slots : (t + 1) * slots] = jnp.where(
                iota((shell_total, slots), 0) == block_of, 1.0, 0.0
            ).astype(jnp.bfloat16)
            node_mask[b, :, t * slots : (t + 1) * slots] = jnp.where(
                iota((NPB, slots), 0) == inside, weight_of(t), 0.0
            )

    live = (iota((1, slots), 1) < count_ref[...]).astype(jnp.float32)
    tables(0, lambda t: node_ref[t : t + 1], lambda t: weight_ref[t : t + 1], cell_ref[...])

    for u in range(NVAR):
        for v in range(NVAR):
            diag_mix[u * ROWS + v : u * ROWS + v + 1] = diag_ref[v, u : u + 1]
    at_slots = dot_left(diag_mix[...], cell_table[...], NN)
    for j in range(3):
        out = at_slots[0:NVAR] * load_ref[0, j : j + 1]
        for u in range(1, NVAR):
            out = out + at_slots[u * ROWS : u * ROWS + NVAR] * load_ref[u, j : j + 1]
        pack[j * ROWS : j * ROWS + NVAR] = out * live
    pack[NVAR : NVAR + TMAP] = weight_ref[...]
    pack[ROWS + NVAR : ROWS + NVAR + TMAP] = node_ref[...].astype(jnp.float32)
    pack[2 * ROWS + NVAR : 3 * ROWS] = jnp.concatenate(
        [cell_ref[...].astype(jnp.float32)] * (ROWS - NVAR), axis=0
    )

    for v in range(NVAR):
        mixed = jnp.sum(diag_ref[v] * rhs_ref[...], axis=0, keepdims=True)
        for a in range(tiles):
            base_bias[v, own + a : own + a + 1] = mixed[:, span(a)]

    width = 3 * NPB
    out_row = iota((width, LANE), 0)
    perm = jnp.where(
        iota((width, LANE), 1)
        == (out_row & (NPB - 1)) * DOF + lax.shift_right_logical(out_row, NPB.bit_length() - 1),
        1.0,
        0.0,
    ).astype(jnp.bfloat16)
    perm_twice = jnp.concatenate([perm, perm], axis=0)
    behind = iota((FOLD, LANE), 0) - iota((FOLD, LANE), 1)
    near = (behind == 0) | (behind == BLK) | (behind == 2 * BLK) | (behind == 3 * BLK)
    fold = jnp.where(near & (iota((FOLD, LANE), 1) < BLK), 1.0, 0.0).astype(jnp.bfloat16)

    def sweep(source, first, start):
        acc = list(start)
        for k in range(FACES):
            place = code[k, first : first + ROWS]
            lane = place & (LANE - 1)
            tile = lax.shift_right_logical(place, LANE.bit_length() - 1)
            picks = [tile == o for o in range(tiles + 1)]
            for u in range(NVAR):
                beside = None
                for o in range(tiles + 1):
                    found = jnp.take_along_axis(
                        source[u, first + o : first + o + ROWS], lane, axis=1, mode="promise_in_bounds"
                    )
                    beside = found if beside is None else jnp.where(picks[o], found, beside)
                for v in range(NVAR):
                    at = (k * NVAR + u) * NVAR + v
                    acc[v] = acc[v] - folded[at, first : first + ROWS] * beside
        return acc

    def own_sweep(source):
        acc = [None] * NVAR
        beside_rows = {}
        for u in range(NVAR):
            for o in range(tiles + 1):
                first = own_x - half + o
                once = source[u, first : first + tiles]
                beside_rows[u, o] = jnp.concatenate([once, once], axis=0)
        for k in range(FACES // 2):
            place = pair_code[k]
            lane = place & (LANE - 1)
            tile = lax.shift_right_logical(place, LANE.bit_length() - 1)
            picks = [tile == o for o in range(tiles + 1)]
            for u in range(NVAR):
                beside = None
                for o in range(tiles + 1):
                    found = jnp.take_along_axis(
                        beside_rows[u, o], lane, axis=1, mode="promise_in_bounds"
                    )
                    beside = found if beside is None else jnp.where(picks[o], found, beside)
                for v in range(NVAR):
                    term = pair_fold[(k * NVAR + u) * NVAR + v] * beside
                    acc[v] = term if acc[v] is None else acc[v] + term
        return [a[0:tiles] + a[tiles : 2 * tiles] for a in acc]

    def own_step(i, e, source):
        for v, taken in enumerate(own_sweep(source)):
            state[e, v, own_x : own_x + tiles] = bias[i, v, own : own + tiles] - taken

    def bias_rows(i, first):
        return [bias[i, v, first : first + ROWS] for v in range(NVAR)]

    def into_work(first, values):
        for v in range(NVAR):
            work[v, first + half : first + half + ROWS] = values[v]

    def last_steps(i, e):
        into_work(half, sweep(work, half, bias_rows(i, half)))
        own_step(i, e, work)

    def two_steps(i, e):
        into_work(half, sweep(state.at[e], half, bias_rows(i, half)))
        own_step(i, e + 1, work)

    def three_steps(i, e):
        outer = [sweep(state.at[e], f, bias_rows(i, f)) for f in (0, ROWS)]
        into_work(0, outer[0])
        into_work(ROWS, outer[1])
        last_steps(i, e + 1)

    def gather_rows(sources, place):
        lane = place & (LANE - 1)
        tile = lax.shift_right_logical(place, LANE.bit_length() - 1)
        out = None
        for c, source in enumerate(sources):
            found = jnp.take_along_axis(source, lane, axis=1, mode="promise_in_bounds")
            out = found if out is None else jnp.where(tile == c, found, out)
        return out

    def couple(i, which):
        by_node = dot(perm, jnp.concatenate(split(struct_all[i]), axis=0), NT)
        parts = jnp.concatenate(
            [by_node[:, 0:shell_total], by_node[:, shell_total : 2 * shell_total]], axis=0
        ).astype(jnp.bfloat16)
        for b in which:
            picked = dot(parts, block_table[b], NN)
            picked = picked[0:width] + picked[width : 2 * width]
            moved = []
            for j in range(3):
                masked = picked[j * NPB : (j + 1) * NPB] * node_mask[b]
                shifted = masked[:, 0:slots]
                for t in range(1, TMAP):
                    shifted = shifted + masked[:, t * slots : (t + 1) * slots]
                moved.append(jnp.sum(shifted, axis=0, keepdims=True))
            displaced = jnp.concatenate(moved, axis=0)
            rates = pack if b == 0 else pack_near.at[b - 1]
            coupled = rates[0:ROWS] * displaced[0:1]
            for j in range(1, 3):
                coupled = coupled + rates[j * ROWS : (j + 1) * ROWS] * displaced[j : j + 1]
            spread = []
            for a in range(tiles):
                place = slot_map[b, :, span(a)]
                found = gather_rows([coupled[:, span(c)] for c in range(slots // LANE)], place - 1)
                spread.append(jnp.where(place > 0, found, 0.0))
            first = (own, 0, own + tiles)[b]
            for v, value in enumerate(to_rows(jnp.concatenate(spread, axis=1)[0:NVAR], mix.at[b], NVAR)):
                bias[i, v, first : first + tiles] = base_bias[v, first : first + tiles] + value

    def all_start(source, landing, send, recv):
        for rf in reversed(range(fluid_n)):
            for rs in reversed(range(struct_n)):
                if rf + rs == 0:
                    continue
                peer_f, peer_s = peers_f[rf], peers_s[rs]
                pltpu.make_async_remote_copy(
                    src_ref=source(peer_s * fluid_n + peer_f),
                    dst_ref=landing,
                    send_sem=send,
                    recv_sem=recv,
                    device_id=(peer_f, peer_s),
                    device_id_type=MESH,
                ).start()

    def all_wait(every, send, recv):
        done = pltpu.make_async_remote_copy(
            src_ref=every,
            dst_ref=every,
            send_sem=send,
            recv_sem=recv,
            device_id=(peers_f[1], me_s),
            device_id_type=MESH,
        )
        done.wait_recv()
        done.wait_send()

    def shell_terms(i):
        for m in range(NB):
            for r in range(ROWS):
                column = columns_ref[m, base + r]
                rows_x[m * ROWS + r : m * ROWS + r + 1] = struct_all[i, pl.ds(column, 1)]
        if i == 0:
            for copy in local:
                copy.wait()
        entries = rows_x[...]
        parts = jnp.concatenate([p.astype(jnp.float32) for p in split(entries)], axis=0).astype(
            jnp.bfloat16
        )
        count = NB * ROWS
        acc = jnp.zeros((ROWS, FOLD), jnp.float32)
        for c in range(0, BLK * BLK, CHUNK):
            wide = dot(parts, expand[:, c : c + CHUNK], NN)
            wide = wide[0:count] + wide[count:]
            for m in range(NB):
                product = wide[m * ROWS : (m + 1) * ROWS] * blocks[m, :, c : c + CHUNK]
                for g in range(0, CHUNK, FOLD):
                    acc = acc + product[:, g : g + FOLD]
        known[...] = right_struct[pl.ds(pl.multiple_of(base, ROWS), ROWS)] - dot_left(acc, fold, NN)

    def send_forces(i, e):
        for v in range(NVAR):
            mix[0, v * tiles : (v + 1) * tiles] = state[e, v, own_x : own_x + tiles]
        parts = [pad_rows(mix[0, pl.ds(a, NVAR, stride=tiles)]) for a in range(tiles)]
        last = jnp.concatenate([p[0:NVAR] for p in parts], axis=1)
        place = jnp.broadcast_to(cell_ref[...], (ROWS, slots))
        at_surface = jnp.concatenate(
            [gather_rows(parts, place[:, span(c)]) for c in range(slots // LANE)], axis=1
        )
        sens = jnp.zeros((3, slots), jnp.float32)
        for v in range(NVAR):
            sens = sens + disp_ref[v] * at_surface[v : v + 1]
        sens = sens * live
        scaled = []
        for j in range(3):
            row = sens[j : j + 1]
            scaled.append(node_mask[0] * jnp.concatenate([row] * TMAP, axis=1))
        values = jnp.concatenate(scaled, axis=0)
        both = jnp.concatenate([p.astype(jnp.float32) for p in split(values)], axis=0)
        forces_out[i, :, 0 : 2 * width] = dot(block_table[0], both.astype(jnp.bfloat16), NT)
        all_start(
            lambda p: forces_out.at[i, pl.ds(pl.multiple_of(p * piece, piece), piece)],
            forces_land.at[i, me],
            force_send.at[i],
            force_recv.at[i],
        )
        forces_land[i, me] = forces_out[i, pl.ds(pl.multiple_of(own_row, piece), piece)]
        return last

    def solve(i):
        all_wait(forces_land.at[i, 0 : total - 1], force_send.at[i], force_recv.at[i])
        pieces = [forces_land[i, q] for q in range(total)]
        while len(pieces) > 1:
            pieces = [sum(pieces[q : q + 2][1:], pieces[q]) for q in range(0, len(pieces), 2)]
        mine = jnp.concatenate(pieces * (ROWS // piece), axis=0)
        spread = dot_left(mine[:, 0 : 2 * width], perm_twice, NN)
        load = known[pl.ds(pl.multiple_of(my_row - base, piece), piece)] + spread[0:piece]
        high, low = [p.astype(jnp.float32) for p in split(load)]
        parts = jnp.concatenate(
            [
                jnp.concatenate([high, high], axis=1),
                jnp.concatenate([low, jnp.zeros_like(low)], axis=1),
            ],
            axis=0,
        ).astype(jnp.bfloat16)
        for r in range(piece):
            out = dot(parts, mats[r], NT)
            result[i, r : r + 1, 0:BLK] = out[r : r + 1] + out[piece + r : piece + r + 1]

    def matrices():
        for p in range(BLK):
            flat[p * ROWS : (p + 1) * ROWS] = jnp.concatenate(
                [inverse[:, p * BLK : (p + 1) * BLK], jnp.zeros((ROWS, LANE - BLK), jnp.float32)],
                axis=1,
            )
        for g in range(ROWS // piece):
            @pl.when(my_row - base == g * piece)
            def _():
                for r in range(piece):
                    high, low = split(flat[pl.ds(g * piece + r, BLK, stride=ROWS)])
                    mats[r, :, 0:LANE] = high
                    mats[r, :, LANE : 2 * LANE] = low

    swap_wait(*state_swap(0, False))
    early = own_sweep(state.at[0])
    struct_all[0, pl.ds(pl.multiple_of(me_s * shard_rows, shard_rows), shard_rows)] = start_struct[...]
    for r in range(1, struct_n):
        start_copy(r, peers_s[r]).wait()
    couple(0, (0,))
    for v in range(NVAR):
        state[1, v, own_x : own_x + tiles] = bias[0, v, own : own + tiles] - early[v]
    swap_start(*state_swap(1, False))
    swap_start(*row_swap(bias.at[0], 2))
    swap_start(*fold_swap(*near_next))
    for c in range(0, BLK * BLK, CHUNK):
        offset = iota((LANE, CHUNK), 1) + c - BLK * iota((LANE, CHUNK), 0)
        expand[:, c : c + CHUNK] = jnp.where((offset >= 0) & (offset < BLK), 1.0, 0.0).astype(
            jnp.bfloat16
        )
    shell_terms(0)
    swap_wait(*state_swap(1, False))
    round_wait(0)
    round_start(1)
    own_step(0, 2, state.at[1])
    swap_start(*state_swap(2, False))
    swap_start(*fold_swap(*near_rest))
    swap_start(*pack_swap(4))
    swap_start(*row_swap(base_bias, 5))
    matrices()
    swap_wait(*fold_swap(*near_first))
    swap_wait(*fold_swap(*near_next))
    swap_wait(*fold_swap(*near_rest))
    swap_wait(*row_swap(code, 1))
    swap_wait(*row_swap(bias.at[0], 2))
    swap_wait(*state_swap(2, False))
    round_wait(1)
    round_start(2)
    two_steps(0, 2)
    swap_start(*state_swap(3, False))
    swap_start(*fold_swap(*far_first))
    swap_wait(*state_swap(3, False))
    round_wait(2)
    for n in range(3, len(bits)):
        round_start(n)
        round_wait(n)
    two_steps(0, 3)
    swap_start(*state_swap(4, True))
    send_forces(0, 4)
    swap_start(*fold_swap(*far_rest))

    swap_wait(*pack_swap(4))
    swap_wait(*row_swap(base_bias, 5))
    for b in (1, 2):
        near_pack = pack_near.at[b - 1]
        tables(
            b,
            lambda t: near_pack[ROWS + NVAR + t : ROWS + NVAR + t + 1].astype(jnp.int32),
            lambda t: near_pack[NVAR + t : NVAR + t + 1],
            near_pack[2 * ROWS + NVAR : 2 * ROWS + NVAR + 1].astype(jnp.int32),
        )
    solve(0)
    landing = struct_all.at[1, pl.ds(pl.multiple_of(own_row, piece), piece)]
    all_start(lambda p: result.at[0], landing, gather_send, gather_recv)
    struct_all[1, pl.ds(pl.multiple_of(own_row, piece), piece)] = result[0]
    swap_wait(*fold_swap(*far_first))
    swap_wait(*fold_swap(*far_rest))
    swap_wait(*state_swap(4, True))
    for f in (0, ROWS):
        outer = sweep(state.at[4], f, [jnp.zeros((ROWS, LANE), jnp.float32)] * NVAR)
        for v in range(NVAR):
            partial[v, f : f + ROWS] = outer[v]
    all_wait(struct_all.at[1, 0 : shell_total - piece], gather_send, gather_recv)

    couple(1, (0, 1, 2))
    for f in (0, ROWS):
        into_work(f, [partial[v, f : f + ROWS] + bias[1, v, f : f + ROWS] for v in range(NVAR)])
    last_steps(1, 5)
    swap_start(*state_swap(5, True))
    shell_terms(1)
    swap_wait(*state_swap(5, True))
    three_steps(1, 5)
    last = send_forces(1, 6)
    fluid_ref[...] = last
    solve(1)

    def final_copy(r, landing):
        return pltpu.make_async_remote_copy(
            src_ref=result.at[1],
            dst_ref=final_land.at[landing],
            send_sem=final_send.at[r],
            recv_sem=final_recv.at[landing],
            device_id=(peers_f[r], me_s),
            device_id_type=MESH,
        )

    for r in range(1, fluid_n):
        final_copy(r, me_f).start()
    final_land[me_f] = result[1]
    for r in range(1, fluid_n):
        final_copy(r, peers_f[r]).wait()
    for f in range(fluid_n):
        struct_ref[f * piece : (f + 1) * piece] = final_land[f]


def finish(fluid_in, struct_in, fluid_ref, struct_ref):
    fluid_ref[...] = fluid_in[...]
    per = FOLD // BLK
    groups = struct_in.shape[0] // per
    wide = jnp.concatenate(
        [struct_in[pl.ds(q, groups, stride=per)][:, 0:BLK] for q in range(per)], axis=1
    )
    for q in range(FOLD // LANE):
        struct_ref[pl.ds(q, groups, stride=FOLD // LANE)] = wide[:, q * LANE : (q + 1) * LANE]


def body(
    fluid_n,
    struct_n,
    fluid_adjoint,
    fluid_rhs,
    diag_inverse,
    face_blocks,
    face_index,
    surface_cell,
    surface_count,
    transfer_node,
    transfer_weight,
    load_sens,
    disp_sens,
    struct_adjoint,
    struct_rhs,
    shell_blocks,
    shell_inverse,
    shell_columns,
):
    cells = fluid_adjoint.shape[1]
    slots = surface_cell.shape[0]
    block_rows = struct_adjoint.shape[0] // BLK
    shell_total = block_rows * struct_n
    piece = block_rows // fluid_n
    total = fluid_n * struct_n
    tiles = cells // LANE
    vmem = pl.BlockSpec(memory_space=pltpu.VMEM)
    far = pl.BlockSpec(memory_space=pl.ANY)
    f32, bf16 = jnp.float32, jnp.bfloat16
    dma = pltpu.SemaphoreType.DMA

    fluid_out, struct_out = pl.pallas_call(
        functools.partial(kernel, fluid_n, struct_n, piece),
        out_shape=(
            jax.ShapeDtypeStruct((NVAR, cells), f32),
            jax.ShapeDtypeStruct((block_rows, LANE), f32),
        ),
        in_specs=[far] * 6 + [vmem] + [far] * 9,
        out_specs=(vmem, vmem),
        scratch_shapes=[
            pltpu.VMEM((7, NVAR, 3 * ROWS, LANE), f32),
            pltpu.VMEM((NVAR, 3 * ROWS, LANE), f32),
            pltpu.VMEM((FACES * NVAR * NVAR, 2 * ROWS, LANE), f32),
            pltpu.VMEM((FACES, 2 * ROWS, LANE), jnp.int32),
            pltpu.VMEM((FACES // 2 * NVAR * NVAR, ROWS, LANE), f32),
            pltpu.VMEM((FACES // 2, ROWS, LANE), jnp.int32),
            pltpu.VMEM((NVAR, 2 * ROWS, LANE), f32),
            pltpu.VMEM((ITERS, NVAR, 2 * ROWS, LANE), f32),
            pltpu.VMEM((NVAR, 2 * ROWS, LANE), f32),
            pltpu.VMEM((3, tiles * ROWS, LANE), f32),
            pltpu.VMEM((tiles * ROWS, LANE), jnp.int32),
            pltpu.VMEM((NVAR * NVAR * tiles * ROWS, LANE), f32),
            pltpu.VMEM((NVAR * ROWS, cells), f32),
            pltpu.VMEM((3 * ROWS, slots), f32),
            pltpu.VMEM((2, 3 * ROWS, slots), f32),
            pltpu.VMEM((cells, slots), bf16),
            pltpu.VMEM((3, ROWS, cells), jnp.int32),
            pltpu.VMEM((3, shell_total, TMAP * slots), bf16),
            pltpu.VMEM((3, NPB, TMAP * slots), f32),
            pltpu.VMEM((NB, ROWS, BLK * BLK), f32),
            pltpu.VMEM((ROWS, BLK * BLK), f32),
            pltpu.VMEM((LANE, BLK * BLK), bf16),
            pltpu.VMEM((block_rows, LANE), f32),
            pltpu.VMEM((block_rows, LANE), f32),
            pltpu.VMEM((ITERS, shell_total, LANE), f32),
            pltpu.VMEM((NB * ROWS, LANE), f32),
            pltpu.VMEM((ROWS, LANE), f32),
            pltpu.VMEM((BLK * ROWS, LANE), f32),
            pltpu.VMEM((piece, BLK, 2 * LANE), bf16),
            pltpu.VMEM((ITERS, shell_total, LANE), f32),
            pltpu.VMEM((ITERS, total, piece, LANE), f32),
            pltpu.VMEM((ITERS, piece, LANE), f32),
            pltpu.VMEM((fluid_n, piece, LANE), f32),
            dma((6, 4)),
            dma((6, 4)),
            dma((9, 2)),
            dma((9, 2)),
            dma((struct_n,)),
            dma((struct_n,)),
            dma((ITERS,)),
            dma((ITERS,)),
            dma,
            dma,
            dma((fluid_n,)),
            dma((fluid_n,)),
            pltpu.SemaphoreType.REGULAR((max(3, fluid_n.bit_length() - 1),)),
            dma((NB + 1,)),
            dma((13,)),
            pltpu.VMEM((NVAR, cells), f32),
            pltpu.VMEM((NVAR, cells), f32),
            pltpu.VMEM((NVAR, NVAR, cells), f32),
            pltpu.VMEM((NVAR, NVAR, FACES, cells), f32),
            pltpu.VMEM((FACES, cells), jnp.int32),
            pltpu.VMEM((1, slots), jnp.int32),
            pltpu.VMEM((TMAP, slots), jnp.int32),
            pltpu.VMEM((TMAP, slots), f32),
            pltpu.VMEM((NVAR, 3, slots), f32),
            pltpu.VMEM((NVAR, 3, slots), f32),
            pltpu.VMEM((block_rows * BLK // LANE, LANE), f32),
            pltpu.VMEM((block_rows * BLK // LANE, LANE), f32),
            pltpu.SMEM((NB, block_rows), jnp.int32),
        ],
        compiler_params=pltpu.CompilerParams(collective_id=0, has_side_effects=True),
    )(
        fluid_adjoint,
        fluid_rhs,
        diag_inverse,
        jnp.transpose(face_blocks, (1, 2, 0, 3)),
        face_index,
        surface_cell.reshape(1, slots),
        surface_count.reshape(1, 1),
        transfer_node,
        transfer_weight,
        jnp.transpose(load_sens, (1, 0, 2)),
        disp_sens,
        struct_adjoint.reshape(-1, LANE),
        struct_rhs.reshape(-1, LANE),
        shell_blocks,
        shell_inverse,
        shell_columns,
    )
    fluid_out, struct_out = pl.pallas_call(
        finish,
        out_shape=(
            jax.ShapeDtypeStruct((NVAR, cells), f32),
            jax.ShapeDtypeStruct((block_rows * BLK // LANE, LANE), f32),
        ),
        in_specs=[vmem, vmem],
        out_specs=(vmem, vmem),
    )(fluid_out, struct_out)
    return fluid_out, struct_out.reshape(-1)


def solution(mesh):
    placed = (
        P(None, ("fluid", "struct")),
        P(None, ("fluid", "struct")),
        P(None, None, ("fluid", "struct")),
        P(None, None, None, ("fluid", "struct")),
        P(None, ("fluid", "struct")),
        P(("fluid", "struct")),
        P(("fluid", "struct")),
        P(None, ("fluid", "struct")),
        P(None, ("fluid", "struct")),
        P(None, None, ("fluid", "struct")),
        P(None, None, ("fluid", "struct")),
        P("struct"),
        P("struct"),
        P(None, "struct", None),
        P("struct", None),
        P(None, "struct"),
    )
    return jax.shard_map(
        functools.partial(body, mesh.shape["fluid"], mesh.shape["struct"]),
        mesh=mesh,
        in_specs=placed,
        out_specs=(P(None, ("fluid", "struct")), P("struct")),
        check_vma=False,
    )
```

```python
import functools

import jax
import jax.numpy as jnp
from jax import lax
from jax.experimental import pallas as pl
from jax.experimental.pallas import tpu as pltpu
from jax.sharding import PartitionSpec as P

NVAR = 5
FACES = 6
TMAP = 3
DOF = 6
BLK = 96
NB = 4
SWEEPS = 6
ITERS = 2
NPB = BLK // DOF
LANE = 128
ROWS = 8
FOLD = 384
CHUNK = 768
NEAR = (2, 5)
FAR = 3
MESH = pl.DeviceIdType.MESH
NN = (((1,), (0,)), ((), ()))
NT = (((1,), (1,)), ((), ()))


def split(value):
    high = value.astype(jnp.bfloat16)
    return high, (value - high.astype(jnp.float32)).astype(jnp.bfloat16)


def dot(left, right, dims):
    return lax.dot_general(left, right, dims, preferred_element_type=jnp.float32)


def dot_left(value, table, dims):
    rows = value.shape[0]
    stacked = jnp.concatenate([p.astype(jnp.float32) for p in split(value)], axis=0)
    out = dot(stacked.astype(jnp.bfloat16), table, dims)
    return out[0:rows] + out[rows : 2 * rows]


def dot_right(table, value, dims):
    high, low = split(value)
    return dot(table, high, dims) + dot(table, low, dims)


def iota(shape, axis):
    return lax.broadcasted_iota(jnp.int32, shape, axis)


def pad_rows(value, rows=ROWS):
    return jnp.concatenate(
        [value, jnp.zeros((rows - value.shape[0], value.shape[1]), value.dtype)], axis=0
    )


def by_block(flat, out):
    groups = flat.shape[0] * LANE // FOLD
    wide = jnp.concatenate(
        [flat[pl.ds(a, groups, stride=FOLD // LANE)] for a in range(FOLD // LANE)], axis=1
    )
    for q in range(FOLD // BLK):
        part = wide[:, q * BLK : (q + 1) * BLK]
        full = jnp.concatenate([part, jnp.zeros((groups, LANE - BLK), jnp.float32)], axis=1)
        out[pl.ds(q, groups, stride=FOLD // BLK)] = full


def kernel(
    fluid_n,
    struct_n,
    piece,
    adj_far,
    rhs_far,
    diag_far,
    face_far,
    index_far,
    cell_far,
    count_ref,
    node_far,
    weight_far,
    load_far,
    disp_far,
    sadj_far,
    srhs_far,
    blocks_ref,
    inverse_ref,
    columns_far,
    fluid_ref,
    struct_ref,
    state,
    work,
    folded,
    code,
    pair_fold,
    pair_code,
    base_bias,
    bias,
    partial,
    mix,
    mix_int,
    fold_mix,
    diag_mix,
    pack,
    pack_near,
    cell_table,
    slot_map,
    block_table,
    node_mask,
    blocks,
    inverse,
    expand,
    start_struct,
    right_struct,
    struct_all,
    rows_x,
    known,
    flat,
    mats,
    plain,
    ready,
    forces_out,
    forces_land,
    result,
    final_land,
    state_send,
    state_recv,
    once_send,
    once_recv,
    start_send,
    start_recv,
    force_send,
    force_recv,
    gather_send,
    gather_recv,
    final_send,
    final_recv,
    round_sem,
    local_sem,
    input_sem,
    adj_ref,
    rhs_ref,
    diag_ref,
    face_ref,
    index_ref,
    cell_ref,
    node_ref,
    weight_ref,
    load_ref,
    disp_ref,
    sadj_ref,
    srhs_ref,
    columns_ref,
):
    me_f = lax.axis_index("fluid")
    me_s = lax.axis_index("struct")
    me = me_f * struct_n + me_s
    total = fluid_n * struct_n
    cells = adj_ref.shape[1]
    tiles = cells // LANE
    half = tiles // 2
    slots = cell_ref.shape[1]
    shell_total = struct_all.shape[1]
    shard_rows = start_struct.shape[0]
    my_row = me_f * piece
    base = (my_row // ROWS) * ROWS
    own_row = me_s * shard_rows + my_row
    own_x = 3 * half
    own = tiles

    def dev(index):
        return (index // struct_n, index % struct_n)

    peers_f = [(me_f + r) % fluid_n for r in range(fluid_n)]
    peers_s = [(me_s + r) % struct_n for r in range(struct_n)]
    barrier = pltpu.get_barrier_semaphore()
    bits = [1 << d for d in range(fluid_n.bit_length() - 1)]
    partners = [(me_f + j - 2 * j * ((me_f // j) % 2), me_s) for j in bits]

    def greet(semaphore, device):
        pl.semaphore_signal(semaphore, inc=1, device_id=device, device_id_type=MESH)

    last_s = struct_n - 1

    @pl.when(me_s == last_s)
    def _():
        greet(barrier, (peers_f[1], 0))

    @pl.when(me_s == 0)
    def _():
        greet(barrier, (peers_f[fluid_n - 1], last_s))

    for r in range(1, struct_n):
        greet(barrier, (me_f, peers_s[r]))
    for partner in partners:
        greet(barrier, partner)
    ends = jnp.where(me_s == 0, 1, 0) + jnp.where(me_s == last_s, 1, 0)

    def round_start(n):
        for partner in partners:
            greet(round_sem.at[n], partner)

    def round_wait(n):
        pl.semaphore_wait(round_sem.at[n], len(partners))

    inputs = []
    for n, (source, landing) in enumerate(
        (
            (sadj_far, sadj_ref),
            (adj_far, adj_ref),
            (srhs_far, srhs_ref),
            (diag_far, diag_ref),
            (face_far, face_ref),
            (index_far, index_ref),
            (cell_far, cell_ref),
            (node_far, node_ref),
            (weight_far, weight_ref),
            (load_far, load_ref),
            (rhs_far, rhs_ref),
            (disp_far, disp_ref),
            (columns_far, columns_ref),
        )
    ):
        inputs.append(pltpu.make_async_copy(source, landing, input_sem.at[n]))
        inputs[n].start()
    local = []
    for m in range(NB):
        local.append(
            pltpu.make_async_copy(
                blocks_ref.at[m, pl.ds(pl.multiple_of(base, ROWS), ROWS)],
                blocks.at[m],
                local_sem.at[m],
            )
        )
    local.append(
        pltpu.make_async_copy(
            inverse_ref.at[pl.ds(pl.multiple_of(base, ROWS), ROWS)], inverse, local_sem.at[NB]
        )
    )
    for copy in local:
        copy.start()

    shifts = (-1, 1, -2, 2)
    sends = (me > 0, me < total - 1, me > 1, me < total - 2)
    takes = (me < total - 1, me > 0, me < total - 2, me > 1)

    def swap_start(copies, send, recv):
        for d, (source, landing) in enumerate(copies):
            @pl.when(sends[d])
            def _():
                pltpu.make_async_remote_copy(
                    src_ref=source,
                    dst_ref=landing,
                    send_sem=send.at[d],
                    recv_sem=recv.at[d],
                    device_id=dev(me + shifts[d]),
                    device_id_type=MESH,
                ).start()

    def swap_wait(copies, send, recv):
        for d, (source, landing) in enumerate(copies):
            copy = pltpu.make_async_remote_copy(
                src_ref=source,
                dst_ref=landing,
                send_sem=send.at[d],
                recv_sem=recv.at[d],
                device_id=dev(me + shifts[d]),
                device_id_type=MESH,
            )

            @pl.when(takes[d])
            def _():
                copy.wait_recv()

            @pl.when(sends[d])
            def _():
                copy.wait_send()

    def rows(ref, first, count):
        return ref.at[:, first : first + count]

    def state_swap(e, wide):
        now = state.at[e]
        copies = [
            (rows(now, own_x, tiles), rows(now, own_x + tiles, tiles)),
            (rows(now, own_x, tiles), rows(now, own_x - tiles, tiles)),
        ]
        if wide:
            copies += [
                (rows(now, own_x, half), rows(now, own_x + 2 * tiles, half)),
                (rows(now, own_x + half, half), rows(now, 0, half)),
            ]
        return copies, state_send.at[e], state_recv.at[e]

    def row_swap(ref, n):
        copies = [
            (rows(ref, own, tiles), rows(ref, own + tiles, tiles)),
            (rows(ref, own, tiles), rows(ref, 0, tiles)),
        ]
        return copies, once_send.at[n], once_recv.at[n]

    def fold_swap(n, first_face, faces, far):
        some = folded.at[first_face * NVAR * NVAR : (first_face + faces) * NVAR * NVAR]
        low, high = rows(some, own, half), rows(some, own + half, half)
        if far:
            copies = [(high, rows(some, own + tiles + half, half)), (low, rows(some, 0, half))]
        else:
            copies = [(low, rows(some, own + tiles, half)), (high, rows(some, half, half))]
        return copies, once_send.at[n], once_recv.at[n]

    near_first = (0, 0, NEAR[0], False)
    near_next = (3, NEAR[0], NEAR[1] - NEAR[0], False)
    near_rest = (8, NEAR[1], FACES - NEAR[1], False)
    far_first = (6, 0, FAR, True)
    far_rest = (7, FAR, FACES - FAR, True)

    def pack_swap(n):
        copies = [(pack, pack_near.at[1]), (pack, pack_near.at[0])]
        return copies, once_send.at[n], once_recv.at[n]

    def span(a):
        return slice(a * LANE, (a + 1) * LANE)

    def to_rows(value, scratch, count):
        for a in range(tiles):
            scratch[a * ROWS : a * ROWS + count] = value[:, span(a)]
        return [scratch[pl.ds(v, tiles, stride=ROWS)] for v in range(count)]

    def clear(ref, first, count):
        ref[:, first : first + count] = jnp.zeros((ref.shape[0], count, LANE), ref.dtype)

    for copy in inputs[0:3]:
        copy.wait()
    for v, value in enumerate(to_rows(adj_ref[...], mix.at[0], NVAR)):
        state[0, v, own_x : own_x + tiles] = value
    by_block(sadj_ref, start_struct)

    pl.semaphore_wait(barrier, struct_n - 1 + len(partners) + ends)
    round_start(0)

    def start_copy(r, landing):
        return pltpu.make_async_remote_copy(
            src_ref=start_struct,
            dst_ref=struct_all.at[0, pl.ds(pl.multiple_of(landing * shard_rows, shard_rows), shard_rows)],
            send_sem=start_send.at[r],
            recv_sem=start_recv.at[landing],
            device_id=(me_f, peers_s[r]),
            device_id_type=MESH,
        )

    for r in range(1, struct_n):
        start_copy(r, me_s).start()
    swap_start(*state_swap(0, False))
    for copy in inputs[3:]:
        copy.wait()

    def pair(k):
        return slice((k % 2) * tiles, (k % 2 + 1) * tiles)

    for a in range(tiles):
        for v in range(NVAR):
            scale = [
                jnp.broadcast_to(diag_ref[v, w : w + 1, span(a)], (FACES, LANE)) for w in range(NVAR)
            ]
            for u in range(NVAR):
                out = scale[0] * face_ref[u, 0, :, span(a)]
                for w in range(1, NVAR):
                    out = out + scale[w] * face_ref[u, w, :, span(a)]
                at = ((u * NVAR + v) * tiles + a) * ROWS
                fold_mix[at : at + FACES] = out
    for k in range(FACES):
        for u in range(NVAR):
            for v in range(NVAR):
                at = (u * NVAR + v) * tiles * ROWS + k
                value = fold_mix[pl.ds(at, tiles, stride=ROWS)]
                folded[(k * NVAR + u) * NVAR + v, own : own + tiles] = value
                pair_fold[((k // 2) * NVAR + u) * NVAR + v, pair(k)] = value
        if k + 1 == NEAR[0]:
            swap_start(*fold_swap(*near_first))
    for k, value in enumerate(to_rows(index_ref[...], mix_int, FACES)):
        value = value - LANE * iota((tiles, LANE), 0)
        code[k, own : own + tiles] = value
        pair_code[k // 2, pair(k)] = value
    swap_start(*row_swap(code, 1))

    def tables(b, node_of, weight_of, cell_of):
        cell_table[...] = jnp.where(iota((cells, slots), 0) == cell_of, 1.0, 0.0).astype(jnp.bfloat16)
        ids = (iota((ROWS, slots), 1) + 1).astype(jnp.float32)
        slot_map[b] = dot_left(ids, cell_table[...], NT).astype(jnp.int32)
        for t in range(TMAP):
            node = node_of(t)
            block_of = lax.shift_right_logical(node, NPB.bit_length() - 1)
            inside = node & (NPB - 1)
            block_table[b, :, t * slots : (t + 1) * slots] = jnp.where(
                iota((shell_total, slots), 0) == block_of, 1.0, 0.0
            ).astype(jnp.bfloat16)
            node_mask[b, :, t * slots : (t + 1) * slots] = jnp.where(
                iota((NPB, slots), 0) == inside, weight_of(t), 0.0
            )

    spare = state.shape[2]
    for e in range(state.shape[0]):
        clear(state.at[e], own_x + 2 * tiles + half, spare - own_x - 2 * tiles - half)

        @pl.when(me == 0)
        def _():
            clear(state.at[e], 0, own_x)

        @pl.when(me == 1)
        def _():
            clear(state.at[e], 0, half)

        @pl.when(me == total - 2)
        def _():
            clear(state.at[e], own_x + 2 * tiles, half)

        @pl.when(me == total - 1)
        def _():
            clear(state.at[e], own_x + tiles, tiles + half)

    @pl.when(me == 0)
    def _():
        for ref in (folded, code, base_bias, bias.at[0]):
            clear(ref, 0, tiles)
        pack_near[0] = jnp.zeros_like(pack)

    @pl.when(me == total - 1)
    def _():
        for ref in (folded, code, base_bias, bias.at[0]):
            clear(ref, own + tiles, tiles)
        pack_near[1] = jnp.zeros_like(pack)

    by_block(srhs_ref, right_struct)
    forces_out[...] = jnp.zeros_like(forces_out)
    result[...] = jnp.zeros_like(result)

    live = (iota((1, slots), 1) < count_ref[...]).astype(jnp.float32)
    tables(0, lambda t: node_ref[t : t + 1], lambda t: weight_ref[t : t + 1], cell_ref[...])

    for u in range(NVAR):
        for v in range(NVAR):
            diag_mix[u * ROWS + v : u * ROWS + v + 1] = diag_ref[v, u : u + 1]
    at_slots = dot_left(diag_mix[...], cell_table[...], NN)
    for j in range(3):
        out = at_slots[0:NVAR] * load_ref[0, j : j + 1]
        for u in range(1, NVAR):
            out = out + at_slots[u * ROWS : u * ROWS + NVAR] * load_ref[u, j : j + 1]
        pack[j * ROWS : j * ROWS + NVAR] = out * live
    pack[NVAR : NVAR + TMAP] = weight_ref[...]
    pack[ROWS + NVAR : ROWS + NVAR + TMAP] = node_ref[...].astype(jnp.float32)
    pack[2 * ROWS + NVAR : 3 * ROWS] = jnp.concatenate(
        [cell_ref[...].astype(jnp.float32)] * (ROWS - NVAR), axis=0
    )

    for v in range(NVAR):
        mixed = jnp.sum(diag_ref[v] * rhs_ref[...], axis=0, keepdims=True)
        for a in range(tiles):
            base_bias[v, own + a : own + a + 1] = mixed[:, span(a)]

    width = 3 * NPB
    out_row = iota((width, LANE), 0)
    perm = jnp.where(
        iota((width, LANE), 1)
        == (out_row & (NPB - 1)) * DOF + lax.shift_right_logical(out_row, NPB.bit_length() - 1),
        1.0,
        0.0,
    ).astype(jnp.bfloat16)
    perm_twice = jnp.concatenate([perm, perm], axis=0)
    behind = iota((FOLD, LANE), 0) - iota((FOLD, LANE), 1)
    near = (behind == 0) | (behind == BLK) | (behind == 2 * BLK) | (behind == 3 * BLK)
    fold = jnp.where(near & (iota((FOLD, LANE), 1) < BLK), 1.0, 0.0).astype(jnp.bfloat16)

    def sweep(source, first, start):
        acc = list(start)
        for k in range(FACES):
            place = code[k, first : first + ROWS]
            lane = place & (LANE - 1)
            tile = lax.shift_right_logical(place, LANE.bit_length() - 1)
            picks = [tile == o for o in range(tiles + 1)]
            for u in range(NVAR):
                beside = None
                for o in range(tiles + 1):
                    found = jnp.take_along_axis(
                        source[u, first + o : first + o + ROWS], lane, axis=1, mode="promise_in_bounds"
                    )
                    beside = found if beside is None else jnp.where(picks[o], found, beside)
                for v in range(NVAR):
                    at = (k * NVAR + u) * NVAR + v
                    acc[v] = acc[v] - folded[at, first : first + ROWS] * beside
        return acc

    def own_sweep(source):
        acc = [None] * NVAR
        beside_rows = {}
        for u in range(NVAR):
            for o in range(tiles + 1):
                first = own_x - half + o
                once = source[u, first : first + tiles]
                beside_rows[u, o] = jnp.concatenate([once, once], axis=0)
        for k in range(FACES // 2):
            place = pair_code[k]
            lane = place & (LANE - 1)
            tile = lax.shift_right_logical(place, LANE.bit_length() - 1)
            picks = [tile == o for o in range(tiles + 1)]
            for u in range(NVAR):
                beside = None
                for o in range(tiles + 1):
                    found = jnp.take_along_axis(
                        beside_rows[u, o], lane, axis=1, mode="promise_in_bounds"
                    )
                    beside = found if beside is None else jnp.where(picks[o], found, beside)
                for v in range(NVAR):
                    term = pair_fold[(k * NVAR + u) * NVAR + v] * beside
                    acc[v] = term if acc[v] is None else acc[v] + term
        return [a[0:tiles] + a[tiles : 2 * tiles] for a in acc]

    def own_step(i, e, source):
        for v, taken in enumerate(own_sweep(source)):
            state[e, v, own_x : own_x + tiles] = bias[i, v, own : own + tiles] - taken

    def bias_rows(i, first):
        return [bias[i, v, first : first + ROWS] for v in range(NVAR)]

    def into_work(first, values):
        for v in range(NVAR):
            work[v, first + half : first + half + ROWS] = values[v]

    def last_steps(i, e):
        into_work(half, sweep(work, half, bias_rows(i, half)))
        own_step(i, e, work)

    def two_steps(i, e):
        into_work(half, sweep(state.at[e], half, bias_rows(i, half)))
        own_step(i, e + 1, work)

    def three_steps(i, e):
        outer = [sweep(state.at[e], f, bias_rows(i, f)) for f in (0, ROWS)]
        into_work(0, outer[0])
        into_work(ROWS, outer[1])
        last_steps(i, e + 1)

    def gather_rows(sources, place):
        lane = place & (LANE - 1)
        tile = lax.shift_right_logical(place, LANE.bit_length() - 1)
        out = None
        for c, source in enumerate(sources):
            found = jnp.take_along_axis(source, lane, axis=1, mode="promise_in_bounds")
            out = found if out is None else jnp.where(tile == c, found, out)
        return out

    def couple(i, which):
        by_node = dot(perm, jnp.concatenate(split(struct_all[i]), axis=0), NT)
        parts = jnp.concatenate(
            [by_node[:, 0:shell_total], by_node[:, shell_total : 2 * shell_total]], axis=0
        ).astype(jnp.bfloat16)
        for b in which:
            picked = dot(parts, block_table[b], NN)
            picked = picked[0:width] + picked[width : 2 * width]
            moved = []
            for j in range(3):
                masked = picked[j * NPB : (j + 1) * NPB] * node_mask[b]
                shifted = masked[:, 0:slots]
                for t in range(1, TMAP):
                    shifted = shifted + masked[:, t * slots : (t + 1) * slots]
                moved.append(jnp.sum(shifted, axis=0, keepdims=True))
            displaced = jnp.concatenate(moved, axis=0)
            rates = pack if b == 0 else pack_near.at[b - 1]
            coupled = rates[0:ROWS] * displaced[0:1]
            for j in range(1, 3):
                coupled = coupled + rates[j * ROWS : (j + 1) * ROWS] * displaced[j : j + 1]
            spread = []
            for a in range(tiles):
                place = slot_map[b, :, span(a)]
                found = gather_rows([coupled[:, span(c)] for c in range(slots // LANE)], place - 1)
                spread.append(jnp.where(place > 0, found, 0.0))
            first = (own, 0, own + tiles)[b]
            for v, value in enumerate(to_rows(jnp.concatenate(spread, axis=1)[0:NVAR], mix.at[b], NVAR)):
                bias[i, v, first : first + tiles] = base_bias[v, first : first + tiles] + value

    def all_start(source, landing, send, recv):
        for rf in reversed(range(fluid_n)):
            for rs in reversed(range(struct_n)):
                if rf + rs == 0:
                    continue
                peer_f, peer_s = peers_f[rf], peers_s[rs]
                pltpu.make_async_remote_copy(
                    src_ref=source(peer_s * fluid_n + peer_f),
                    dst_ref=landing,
                    send_sem=send,
                    recv_sem=recv,
                    device_id=(peer_f, peer_s),
                    device_id_type=MESH,
                ).start()

    def all_wait(every, send, recv):
        done = pltpu.make_async_remote_copy(
            src_ref=every,
            dst_ref=every,
            send_sem=send,
            recv_sem=recv,
            device_id=(peers_f[1], me_s),
            device_id_type=MESH,
        )
        done.wait_recv()
        done.wait_send()

    def shell_terms(i):
        for m in range(NB):
            for r in range(ROWS):
                column = columns_ref[m, base + r]
                rows_x[m * ROWS + r : m * ROWS + r + 1] = struct_all[i, pl.ds(column, 1)]
        if i == 0:
            for copy in local:
                copy.wait()
        entries = rows_x[...]
        parts = jnp.concatenate([p.astype(jnp.float32) for p in split(entries)], axis=0).astype(
            jnp.bfloat16
        )
        count = NB * ROWS
        acc = jnp.zeros((ROWS, FOLD), jnp.float32)
        for c in range(0, BLK * BLK, CHUNK):
            wide = dot(parts, expand[:, c : c + CHUNK], NN)
            wide = wide[0:count] + wide[count:]
            for m in range(NB):
                product = wide[m * ROWS : (m + 1) * ROWS] * blocks[m, :, c : c + CHUNK]
                for g in range(0, CHUNK, FOLD):
                    acc = acc + product[:, g : g + FOLD]
        known[...] = right_struct[pl.ds(pl.multiple_of(base, ROWS), ROWS)] - dot_left(acc, fold, NN)

    def send_forces(i, e):
        for v in range(NVAR):
            mix[0, v * tiles : (v + 1) * tiles] = state[e, v, own_x : own_x + tiles]
        parts = [pad_rows(mix[0, pl.ds(a, NVAR, stride=tiles)]) for a in range(tiles)]
        last = jnp.concatenate([p[0:NVAR] for p in parts], axis=1)
        place = jnp.broadcast_to(cell_ref[...], (ROWS, slots))
        at_surface = jnp.concatenate(
            [gather_rows(parts, place[:, span(c)]) for c in range(slots // LANE)], axis=1
        )
        sens = jnp.zeros((3, slots), jnp.float32)
        for v in range(NVAR):
            sens = sens + disp_ref[v] * at_surface[v : v + 1]
        sens = sens * live
        scaled = []
        for j in range(3):
            row = sens[j : j + 1]
            scaled.append(node_mask[0] * jnp.concatenate([row] * TMAP, axis=1))
        values = jnp.concatenate(scaled, axis=0)
        both = jnp.concatenate([p.astype(jnp.float32) for p in split(values)], axis=0)
        forces_out[i, :, 0 : 2 * width] = dot(block_table[0], both.astype(jnp.bfloat16), NT)
        all_start(
            lambda p: forces_out.at[i, pl.ds(pl.multiple_of(p * piece, piece), piece)],
            forces_land.at[i, me],
            force_send.at[i],
            force_recv.at[i],
        )
        forces_land[i, me] = forces_out[i, pl.ds(pl.multiple_of(own_row, piece), piece)]
        return last

    def solve(i):
        all_wait(forces_land.at[i, 0 : total - 1], force_send.at[i], force_recv.at[i])
        pieces = [forces_land[i, q] for q in range(total)]
        while len(pieces) > 1:
            pieces = [sum(pieces[q : q + 2][1:], pieces[q]) for q in range(0, len(pieces), 2)]
        for r, out in enumerate(products(pieces[0], mats)):
            result[i, r : r + 1, 0:BLK] = ready[r : r + 1, 0:BLK] + out

    def products(value, table):
        high, low = [p.astype(jnp.float32) for p in split(value)]
        parts = jnp.concatenate(
            [
                jnp.concatenate([high, high], axis=1),
                jnp.concatenate([low, jnp.zeros_like(low)], axis=1),
            ],
            axis=0,
        ).astype(jnp.bfloat16)
        outs = [dot(parts, table[r], NT) for r in range(piece)]
        return [out[r : r + 1] + out[piece + r : piece + r + 1] for r, out in enumerate(outs)]

    def solve_known():
        value = known[pl.ds(pl.multiple_of(my_row - base, piece), piece)]
        for r, out in enumerate(products(value, plain)):
            ready[r : r + 1, 0:BLK] = out

    def matrices():
        for p in range(BLK):
            flat[p * ROWS : (p + 1) * ROWS] = jnp.concatenate(
                [inverse[:, p * BLK : (p + 1) * BLK], jnp.zeros((ROWS, LANE - BLK), jnp.float32)],
                axis=1,
            )
        for g in range(ROWS // piece):
            @pl.when(my_row - base == g * piece)
            def _():
                for r in range(piece):
                    high, low = split(flat[pl.ds(g * piece + r, BLK, stride=ROWS)])
                    for n, part in enumerate((high, low)):
                        plain[r, :, n * LANE : (n + 1) * LANE] = part
                        mixed = dot(part, perm_twice, NT)
                        mats[r, :, n * LANE : (n + 1) * LANE] = jnp.concatenate(
                            [mixed, jnp.zeros((BLK, LANE - 2 * width), jnp.float32)], axis=1
                        ).astype(jnp.bfloat16)

    swap_wait(*state_swap(0, False))
    early = own_sweep(state.at[0])
    struct_all[0, pl.ds(pl.multiple_of(me_s * shard_rows, shard_rows), shard_rows)] = start_struct[...]
    for r in range(1, struct_n):
        start_copy(r, peers_s[r]).wait()
    couple(0, (0,))
    for v in range(NVAR):
        state[1, v, own_x : own_x + tiles] = bias[0, v, own : own + tiles] - early[v]
    swap_start(*state_swap(1, False))
    swap_start(*row_swap(bias.at[0], 2))
    swap_start(*fold_swap(*near_next))
    for c in range(0, BLK * BLK, CHUNK):
        offset = iota((LANE, CHUNK), 1) + c - BLK * iota((LANE, CHUNK), 0)
        expand[:, c : c + CHUNK] = jnp.where((offset >= 0) & (offset < BLK), 1.0, 0.0).astype(
            jnp.bfloat16
        )
    shell_terms(0)
    swap_wait(*state_swap(1, False))
    round_wait(0)
    round_start(1)
    own_step(0, 2, state.at[1])
    swap_start(*state_swap(2, False))
    swap_start(*fold_swap(*near_rest))
    swap_start(*pack_swap(4))
    swap_start(*row_swap(base_bias, 5))
    matrices()
    solve_known()
    swap_wait(*fold_swap(*near_first))
    swap_wait(*fold_swap(*near_next))
    swap_wait(*fold_swap(*near_rest))
    swap_wait(*row_swap(code, 1))
    swap_wait(*row_swap(bias.at[0], 2))
    swap_wait(*state_swap(2, False))
    round_wait(1)
    round_start(2)
    two_steps(0, 2)
    swap_start(*state_swap(3, False))
    swap_start(*fold_swap(*far_first))
    swap_wait(*state_swap(3, False))
    round_wait(2)
    for n in range(3, len(bits)):
        round_start(n)
        round_wait(n)
    two_steps(0, 3)
    swap_start(*state_swap(4, True))
    send_forces(0, 4)
    swap_start(*fold_swap(*far_rest))

    swap_wait(*pack_swap(4))
    swap_wait(*row_swap(base_bias, 5))
    for b in (1, 2):
        near_pack = pack_near.at[b - 1]
        tables(
            b,
            lambda t: near_pack[ROWS + NVAR + t : ROWS + NVAR + t + 1].astype(jnp.int32),
            lambda t: near_pack[NVAR + t : NVAR + t + 1],
            near_pack[2 * ROWS + NVAR : 2 * ROWS + NVAR + 1].astype(jnp.int32),
        )
    solve(0)
    landing = struct_all.at[1, pl.ds(pl.multiple_of(own_row, piece), piece)]
    all_start(lambda p: result.at[0], landing, gather_send, gather_recv)
    struct_all[1, pl.ds(pl.multiple_of(own_row, piece), piece)] = result[0]
    swap_wait(*fold_swap(*far_first))
    swap_wait(*fold_swap(*far_rest))
    swap_wait(*state_swap(4, True))
    for f in (0, ROWS):
        outer = sweep(state.at[4], f, [jnp.zeros((ROWS, LANE), jnp.float32)] * NVAR)
        for v in range(NVAR):
            partial[v, f : f + ROWS] = outer[v]
    all_wait(struct_all.at[1, 0 : shell_total - piece], gather_send, gather_recv)

    couple(1, (0, 1, 2))
    for f in (0, ROWS):
        into_work(f, [partial[v, f : f + ROWS] + bias[1, v, f : f + ROWS] for v in range(NVAR)])
    last_steps(1, 5)
    swap_start(*state_swap(5, True))
    shell_terms(1)
    solve_known()
    swap_wait(*state_swap(5, True))
    three_steps(1, 5)
    last = send_forces(1, 6)
    fluid_ref[...] = last
    solve(1)

    def final_copy(r, landing):
        return pltpu.make_async_remote_copy(
            src_ref=result.at[1],
            dst_ref=final_land.at[landing],
            send_sem=final_send.at[r],
            recv_sem=final_recv.at[landing],
            device_id=(peers_f[r], me_s),
            device_id_type=MESH,
        )

    for r in range(1, fluid_n):
        final_copy(r, me_f).start()
    final_land[me_f] = result[1]
    for r in range(1, fluid_n):
        final_copy(r, peers_f[r]).wait()
    for f in range(fluid_n):
        struct_ref[f * piece : (f + 1) * piece] = final_land[f]


def finish(fluid_in, struct_in, fluid_ref, struct_ref):
    fluid_ref[...] = fluid_in[...]
    per = FOLD // BLK
    groups = struct_in.shape[0] // per
    wide = jnp.concatenate(
        [struct_in[pl.ds(q, groups, stride=per)][:, 0:BLK] for q in range(per)], axis=1
    )
    for q in range(FOLD // LANE):
        struct_ref[pl.ds(q, groups, stride=FOLD // LANE)] = wide[:, q * LANE : (q + 1) * LANE]


def body(
    fluid_n,
    struct_n,
    fluid_adjoint,
    fluid_rhs,
    diag_inverse,
    face_blocks,
    face_index,
    surface_cell,
    surface_count,
    transfer_node,
    transfer_weight,
    load_sens,
    disp_sens,
    struct_adjoint,
    struct_rhs,
    shell_blocks,
    shell_inverse,
    shell_columns,
):
    cells = fluid_adjoint.shape[1]
    slots = surface_cell.shape[0]
    block_rows = struct_adjoint.shape[0] // BLK
    shell_total = block_rows * struct_n
    piece = block_rows // fluid_n
    total = fluid_n * struct_n
    tiles = cells // LANE
    vmem = pl.BlockSpec(memory_space=pltpu.VMEM)
    far = pl.BlockSpec(memory_space=pl.ANY)
    f32, bf16 = jnp.float32, jnp.bfloat16
    dma = pltpu.SemaphoreType.DMA

    fluid_out, struct_out = pl.pallas_call(
        functools.partial(kernel, fluid_n, struct_n, piece),
        out_shape=(
            jax.ShapeDtypeStruct((NVAR, cells), f32),
            jax.ShapeDtypeStruct((block_rows, LANE), f32),
        ),
        in_specs=[far] * 6 + [vmem] + [far] * 9,
        out_specs=(vmem, vmem),
        scratch_shapes=[
            pltpu.VMEM((7, NVAR, 3 * ROWS, LANE), f32),
            pltpu.VMEM((NVAR, 3 * ROWS, LANE), f32),
            pltpu.VMEM((FACES * NVAR * NVAR, 2 * ROWS, LANE), f32),
            pltpu.VMEM((FACES, 2 * ROWS, LANE), jnp.int32),
            pltpu.VMEM((FACES // 2 * NVAR * NVAR, ROWS, LANE), f32),
            pltpu.VMEM((FACES // 2, ROWS, LANE), jnp.int32),
            pltpu.VMEM((NVAR, 2 * ROWS, LANE), f32),
            pltpu.VMEM((ITERS, NVAR, 2 * ROWS, LANE), f32),
            pltpu.VMEM((NVAR, 2 * ROWS, LANE), f32),
            pltpu.VMEM((3, tiles * ROWS, LANE), f32),
            pltpu.VMEM((tiles * ROWS, LANE), jnp.int32),
            pltpu.VMEM((NVAR * NVAR * tiles * ROWS, LANE), f32),
            pltpu.VMEM((NVAR * ROWS, cells), f32),
            pltpu.VMEM((3 * ROWS, slots), f32),
            pltpu.VMEM((2, 3 * ROWS, slots), f32),
            pltpu.VMEM((cells, slots), bf16),
            pltpu.VMEM((3, ROWS, cells), jnp.int32),
            pltpu.VMEM((3, shell_total, TMAP * slots), bf16),
            pltpu.VMEM((3, NPB, TMAP * slots), f32),
            pltpu.VMEM((NB, ROWS, BLK * BLK), f32),
            pltpu.VMEM((ROWS, BLK * BLK), f32),
            pltpu.VMEM((LANE, BLK * BLK), bf16),
            pltpu.VMEM((block_rows, LANE), f32),
            pltpu.VMEM((block_rows, LANE), f32),
            pltpu.VMEM((ITERS, shell_total, LANE), f32),
            pltpu.VMEM((NB * ROWS, LANE), f32),
            pltpu.VMEM((ROWS, LANE), f32),
            pltpu.VMEM((BLK * ROWS, LANE), f32),
            pltpu.VMEM((piece, BLK, 2 * LANE), bf16),
            pltpu.VMEM((piece, BLK, 2 * LANE), bf16),
            pltpu.VMEM((piece, LANE), f32),
            pltpu.VMEM((ITERS, shell_total, LANE), f32),
            pltpu.VMEM((ITERS, total, piece, LANE), f32),
            pltpu.VMEM((ITERS, piece, LANE), f32),
            pltpu.VMEM((fluid_n, piece, LANE), f32),
            dma((6, 4)),
            dma((6, 4)),
            dma((9, 2)),
            dma((9, 2)),
            dma((struct_n,)),
            dma((struct_n,)),
            dma((ITERS,)),
            dma((ITERS,)),
            dma,
            dma,
            dma((fluid_n,)),
            dma((fluid_n,)),
            pltpu.SemaphoreType.REGULAR((max(3, fluid_n.bit_length() - 1),)),
            dma((NB + 1,)),
            dma((13,)),
            pltpu.VMEM((NVAR, cells), f32),
            pltpu.VMEM((NVAR, cells), f32),
            pltpu.VMEM((NVAR, NVAR, cells), f32),
            pltpu.VMEM((NVAR, NVAR, FACES, cells), f32),
            pltpu.VMEM((FACES, cells), jnp.int32),
            pltpu.VMEM((1, slots), jnp.int32),
            pltpu.VMEM((TMAP, slots), jnp.int32),
            pltpu.VMEM((TMAP, slots), f32),
            pltpu.VMEM((NVAR, 3, slots), f32),
            pltpu.VMEM((NVAR, 3, slots), f32),
            pltpu.VMEM((block_rows * BLK // LANE, LANE), f32),
            pltpu.VMEM((block_rows * BLK // LANE, LANE), f32),
            pltpu.SMEM((NB, block_rows), jnp.int32),
        ],
        compiler_params=pltpu.CompilerParams(collective_id=0, has_side_effects=True),
    )(
        fluid_adjoint,
        fluid_rhs,
        diag_inverse,
        jnp.transpose(face_blocks, (1, 2, 0, 3)),
        face_index,
        surface_cell.reshape(1, slots),
        surface_count.reshape(1, 1),
        transfer_node,
        transfer_weight,
        jnp.transpose(load_sens, (1, 0, 2)),
        disp_sens,
        struct_adjoint.reshape(-1, LANE),
        struct_rhs.reshape(-1, LANE),
        shell_blocks,
        shell_inverse,
        shell_columns,
    )
    fluid_out, struct_out = pl.pallas_call(
        finish,
        out_shape=(
            jax.ShapeDtypeStruct((NVAR, cells), f32),
            jax.ShapeDtypeStruct((block_rows * BLK // LANE, LANE), f32),
        ),
        in_specs=[vmem, vmem],
        out_specs=(vmem, vmem),
    )(fluid_out, struct_out)
    return fluid_out, struct_out.reshape(-1)


def solution(mesh):
    placed = (
        P(None, ("fluid", "struct")),
        P(None, ("fluid", "struct")),
        P(None, None, ("fluid", "struct")),
        P(None, None, None, ("fluid", "struct")),
        P(None, ("fluid", "struct")),
        P(("fluid", "struct")),
        P(("fluid", "struct")),
        P(None, ("fluid", "struct")),
        P(None, ("fluid", "struct")),
        P(None, None, ("fluid", "struct")),
        P(None, None, ("fluid", "struct")),
        P("struct"),
        P("struct"),
        P(None, "struct", None),
        P("struct", None),
        P(None, "struct"),
    )
    return jax.shard_map(
        functools.partial(body, mesh.shape["fluid"], mesh.shape["struct"]),
        mesh=mesh,
        in_specs=placed,
        out_specs=(P(None, ("fluid", "struct")), P("struct")),
        check_vma=False,
    )
```
